32 devices in a mesh: rows: 16 (over z, y, x), strips: 2 (over core).
Axes of the slice: x: 2, y: 2, z: 4, core: 2. Of those that a mesh axis runs over, the one named last changes fastest.
Arguments:
- left_pixels: int32 [64, 1024], P('rows', 'strips'), may hold values from 2240 to 2368
- right_pixels: int32 [64, 1024], P('rows', 'strips'), may hold values from 2238 to 2370
- valid_mask: int32 [64, 1024], P('rows', 'strips'), may hold values 0 or 1
- first_weight: bfloat16 [64, 1, 3, 3], replicated, may hold values from -6 to 6
- conv_weights: bfloat16 [3, 64, 64, 3, 3], replicated, may hold values from -0.875 to 0.875
Outputs:
- aggregated: float32 [64, 1024, 128], P('rows', 'strips')
The draws below stay inside these ranges and needn't reach their ends.
All inputs are finite; a program needn't handle non-finite values. No bound on the sum of `valid_mask` on one device may be relied on, other than what follows from the above.
Results may differ from the reference program's by a relative error of at most 0.012.
The reference program's roundings to bfloat16 on the way count: a program that leaves them out, or rounds other values in their place, can miss the bound.
Values may be sent and summed in bfloat16 or wider, within the bound.
No kernel may reach another device: no remote copies, remote signals or barrier semaphores. Data moves between devices by JAX's collectives and lax.ppermute only.
A program may use at most 128 MiB of HBM per device.

```python
import math
import jax
import jax.numpy as jnp
from jax import lax

CH = 64
DISP = 128
LAYERS = 4
ROWS = 64
COLS = 1024


def stereo_pair(key):
    width_total = COLS + DISP
    row_blocks = (ROWS + 63) // 64
    col_blocks = (width_total + 63) // 64
    level_index = jax.random.randint(jax.random.fold_in(key, 101), (row_blocks, col_blocks), 0, 3)
    first_block = (jnp.arange(row_blocks)[:, None] == 0) & (jnp.arange(col_blocks)[None, :] == 0)
    level_index = jnp.where(first_block, 2, level_index)
    multiplier = jnp.where(level_index == 2, 16, jnp.where(level_index == 1, 4, 1)).astype(jnp.int32)
    row_block = jnp.arange(ROWS) // 64
    col_block = jnp.arange(width_total) // 64
    amplitude = multiplier[row_block][:, col_block]
    noise_field = jax.random.randint(jax.random.fold_in(key, 102), (ROWS, width_total), -4, 5)
    texture = 2304 + noise_field * amplitude
    displacement = jax.random.randint(jax.random.fold_in(key, 103), (row_blocks, (COLS + 63) // 64), 0, DISP)
    per_pixel = displacement[row_block][:, jnp.arange(COLS) // 64]
    sampled_cols = (jnp.arange(COLS)[None, :] + per_pixel).astype(jnp.int32)
    right_noise = jax.random.randint(jax.random.fold_in(key, 104), (ROWS, COLS), -2, 3)
    right_image = jnp.take_along_axis(texture, sampled_cols, axis=1) + right_noise
    return (texture[:, :COLS].astype(jnp.int32), right_image.astype(jnp.int32))


def draw_left_pixels(key, part):
    return stereo_pair(key)[0]


def draw_right_pixels(key, part):
    return stereo_pair(key)[1]


def with_ends(values, rng, least, largest):
    shape = values.shape
    index_at = [jax.random.randint(jax.random.fold_in(rng, axis), (), 0, shape[axis]) for axis in range(len(shape))]
    values = values.at[tuple(index_at)].set(least)
    longest = shape.index(max(shape))
    index_at[longest] = (index_at[longest] + 1) % shape[longest]
    return values.at[tuple(index_at)].set(largest)


def gaussian(own_key, shape, width, bound, held_as=jnp.bfloat16):
    entries = width * jax.random.normal(own_key, shape, jnp.float32)
    return jnp.clip(entries, min=-bound, max=bound).astype(held_as)


def setup_inputs(seed: int = 0) -> dict:
    seeds = jax.random.split(jax.random.key(seed), 6)
    return {
        "left_pixels": draw_left_pixels(jax.random.fold_in(seeds[5], 71), 0),
        "right_pixels": draw_right_pixels(jax.random.fold_in(seeds[5], 71), 0),
        "valid_mask": with_ends((jax.random.randint(seeds[2], (ROWS, COLS), 0, 4) < 3).astype(jnp.int32), jax.random.fold_in(seeds[2], 1), 0, 1),
        "first_weight": gaussian(seeds[3], (CH, 1, 3, 3), ((2.0 / 9) ** 0.5), 6.0),
        "conv_weights": gaussian(seeds[4], (LAYERS - 1, CH, CH, 3, 3), ((2.0 / (9 * CH)) ** 0.5), 0.875),
    }


P_SMALL = 0.5
P_LARGE = 2.0

def sgm_step(previous, cost_row):
    lowest = lax.optimization_barrier(jnp.min(previous, axis=-1, keepdims=True))
    higher_side = jnp.concatenate([previous[..., 1:], previous[..., -1:]], axis=-1)
    lower_side = jnp.concatenate([previous[..., :1], previous[..., :-1]], axis=-1)
    chosen = jnp.minimum(jnp.minimum(previous, jnp.minimum(higher_side, lower_side) + P_SMALL), lowest + P_LARGE)
    updated = cost_row + chosen - lowest
    return (updated, updated)

def aggregate_path(cost_first):
    initial = jnp.zeros(cost_first.shape[1:], jnp.float32)
    return lax.scan(sgm_step, initial, cost_first)[1]

def conv_stack(image_pixels, first_weight, conv_weights):
    layer_in = (image_pixels.astype(jnp.float32) / 1024.0 - 2.0).astype(jnp.bfloat16)[None, None]
    weights = [first_weight] + [conv_weights[layer] for layer in range(LAYERS - 1)]
    for layer in range(LAYERS):
        layer_out = lax.conv_general_dilated(layer_in.astype(jnp.float32), weights[layer].astype(jnp.float32), (1, 1), 'SAME', dimension_numbers=('NCHW', 'OIHW', 'NCHW'), precision=lax.Precision.HIGHEST)
        if layer + 1 < LAYERS:
            layer_out = jnp.maximum(layer_out, 0.0)
        layer_in = layer_out.astype(jnp.bfloat16)
    return layer_in[0]

def reference(left_pixels, right_pixels, valid_mask, first_weight, conv_weights):
    left_features = conv_stack(left_pixels, first_weight, conv_weights)
    right_features = conv_stack(right_pixels, first_weight, conv_weights)
    left_rows = jnp.swapaxes(left_features, 0, 1)
    right_rows = jnp.swapaxes(right_features, 0, 1)
    band_index = (jnp.arange(COLS)[:, None] - jnp.arange(DISP)[None, :] + DISP).astype(jnp.int32)
    inv_root = 1.0 / math.sqrt(CH)

    def row_cost(row_pair):
        left_row, right_row = row_pair
        right_padded = jnp.pad(right_row.astype(jnp.float32), ((0, 0), (DISP, 0)))
        product = jnp.dot(left_row.astype(jnp.float32).T, right_padded, preferred_element_type=jnp.float32, precision=lax.Precision.HIGHEST)
        return -inv_root * jnp.take_along_axis(product, band_index, axis=1)
    cost_volume = lax.map(row_cost, (left_rows, right_rows))
    cost_volume = valid_mask.astype(jnp.float32)[:, :, None] * cost_volume
    across = jnp.swapaxes(cost_volume, 0, 1)
    horizontal = aggregate_path(across) + aggregate_path(across[::-1])[::-1]
    summed = jnp.swapaxes(horizontal, 0, 1)
    summed = summed + aggregate_path(cost_volume)
    summed = summed + aggregate_path(cost_volume[::-1])[::-1]
    return summed
```

```python
import functools
import math

import jax
import jax.numpy as jnp
from jax import lax
from jax.experimental import pallas as pl
from jax.experimental.pallas import tpu as pltpu
from jax.sharding import PartitionSpec as P

DISP = 128
P_SMALL = 0.5
P_LARGE = 2.0
BIG = 3.0e38
CH = 64
EDGE = 8
LANES = 128


def chunking(need):
    best = None
    for size in (128, 144, 160, 176):
        total = -(-need // size) * size
        if best is None or total < best[1]:
            best = (size, total)
    return best


def plan(width):
    steps = [chunking(width)]
    for _ in range(2):
        steps.append(chunking(steps[-1][1] + 2 * EDGE))
    need = steps[-1][1] + 2 * EDGE
    steps.append((128, -(-need // 128) * 128))
    return steps[::-1]


def feature_stack(pix_ref, w1_ref, wt_ref, bufs, sizes, col_of, row_low, row_high, flipped, last_mask_ref):
    def in_image(base, count, lanes, halo, lane0):
        position = lax.broadcasted_iota(jnp.int32, (count, lanes), 0) + base
        row = (lax.broadcasted_iota(jnp.int32, (count, lanes), 1) + lane0) // CH - halo
        low, high = col_of(position)
        return low & high & (row >= row_low) & (row < row_high)

    chunk, total = sizes[0]
    lanes = bufs[0].shape[1]

    def first(index, carry):
        start = pl.multiple_of(index * chunk, chunk)
        value = jnp.dot(pix_ref[pl.ds(start, chunk), :], w1_ref[...], preferred_element_type=jnp.float32)
        inside = in_image(start - 3 * EDGE, chunk, lanes, 3, 0)
        value = jnp.where(inside, jnp.maximum(value, 0.0), 0.0)
        bufs[0][pl.ds(start, chunk), :] = value.astype(jnp.bfloat16)
        return carry

    lax.fori_loop(0, total // chunk, first, 0)

    for layer in range(1, 4):
        source, target = bufs[layer - 1], bufs[layer]
        out_rows = target.shape[1] // CH
        chunk, total = sizes[layer]
        reach = chunk + 2 * EDGE
        for group in range(0, out_rows, 4):
            count = min(4, out_rows - group)
            wide, deep = count * CH, (count + 2) * CH

            def convolve(index, carry, layer=layer, group=group, wide=wide, deep=deep, chunk=chunk, reach=reach, source=source, target=target):
                start = pl.multiple_of(index * chunk, 16)
                block = source[pl.ds(start, reach), group * CH : group * CH + deep]
                parts = [
                    jnp.dot(block, wt_ref[layer - 1, dx, :deep, :wide], preferred_element_type=jnp.float32)
                    for dx in range(3)
                ]
                before, after = (parts[2], parts[0]) if flipped else (parts[0], parts[2])
                value = pltpu.roll(before, 1, 0) + parts[1] + pltpu.roll(after, reach - 1, 0)
                value = value[EDGE : EDGE + chunk]
                halo = 3 - layer
                if layer < 3:
                    value = jnp.maximum(value, 0.0)
                inside = in_image(start - halo * EDGE, chunk, wide, halo, group * CH)
                value = jnp.where(inside, value, 0.0).astype(jnp.bfloat16)
                target[pl.ds(start, chunk), group * CH : group * CH + wide] = value
                return carry

            lax.fori_loop(0, total // chunk, convolve, 0)


def cost_kernel(dims, where_ref, left_ref, right_ref, mask_ref, w1_ref, wt_ref, cost_ref, *bufs):
    rows, cols, total_rows, total_cols = dims
    first_row, first_col = where_ref[0], where_ref[1]
    row_low, row_high = -first_row, total_rows - first_row
    left_bufs, right_bufs = bufs[:4], bufs[4:]

    def left_col(position):
        col = position + first_col
        return col >= 0, col < total_cols

    def right_col(position):
        col = first_col + cols - 1 - position
        return col >= 0, col < total_cols

    feature_stack(left_ref, w1_ref, wt_ref, left_bufs, plan(cols), left_col, row_low, row_high, False, mask_ref)
    feature_stack(right_ref, w1_ref, wt_ref, right_bufs, plan(cols + DISP), right_col, row_low, row_high, True, None)
    left, right = left_bufs[3], right_bufs[3]
    for row in range(rows):
        pair = row // 2 * LANES
        lane = lax.broadcasted_iota(jnp.int32, (LANES, LANES), 1)
        own = (lane // CH) == row % 2

        def block(index, carry, pair=pair, own=own, row=row):
            start = pl.multiple_of(index * LANES, LANES)
            window = pl.multiple_of(cols - LANES - start, LANES)
            scale = mask_ref[pl.ds(start, LANES), pair : pair + LANES]
            a = jnp.where(own, left[pl.ds(start, LANES), pair : pair + LANES] * scale, jnp.zeros((), jnp.bfloat16))
            b = right[pl.ds(window, 2 * LANES), pair : pair + LANES]
            product = lax.dot_general(a, b, (((1,), (1,)), ((), ())), preferred_element_type=jnp.float32)
            skewed = pltpu.roll(product, LANES + 1, 1, stride=1, stride_axis=0)
            cost_ref[row, pl.ds(start, LANES), :] = skewed[:, :LANES]
            return carry

        lax.fori_loop(0, cols // LANES, block, 0)


def cost_volume(left_stack, right_stack, mask, w1, wt, place, rows, cols, total_rows, total_cols):
    bufs = []
    for width in (cols, cols + DISP):
        sizes = plan(width)
        for layer in range(4):
            out_rows = rows + 2 * (3 - layer)
            length = sizes[layer][1]
            bufs.append(pltpu.VMEM((length, out_rows * CH), jnp.bfloat16))
    vmem = pl.BlockSpec(memory_space=pltpu.VMEM)
    return pl.pallas_call(
        functools.partial(cost_kernel, (rows, cols, total_rows, total_cols)),
        out_shape=jax.ShapeDtypeStruct((rows, cols, DISP), jnp.float32),
        in_specs=[pl.BlockSpec(memory_space=pltpu.SMEM)] + [vmem] * 5,
        out_specs=vmem,
        scratch_shapes=bufs,
        compiler_params=pltpu.CompilerParams(vmem_limit_bytes=40 << 20),
        cost_estimate=pl.CostEstimate(flops=8_000_000_000, bytes_accessed=6_000_000, transcendentals=0),
    )(place, left_stack, right_stack, mask, w1, wt)


def row_scan_kernel(dims, has_sum, place_ref, cost_ref, state_ref, *rest):
    rows, cols, flip = dims
    if has_sum:
        lead_ref, out_ref, end_ref, tile_ref, spread_ref, path_ref, low_ref = rest
    else:
        out_ref, end_ref, tile_ref, spread_ref, path_ref, low_ref = rest
    width = LANES // rows
    count = cols // width
    forward = place_ref[2] == (1 if flip else 0)
    lane = lax.broadcasted_iota(jnp.int32, (8, LANES), 1)
    sublane = lax.broadcasted_iota(jnp.int32, (8, LANES), 0)
    lane_base = lane // width * width
    lane_col = lane % width

    def lowest(state):
        level = list(state)
        while len(level) > 1:
            level = [jnp.minimum(level[i], level[i + 1]) for i in range(0, len(level), 2)]
        low = level[0]
        for shift in (4, 2, 1):
            low = jnp.minimum(low, pltpu.roll(low, shift, 0))
        return low

    def one_chunk(index, state):
        chunk = jnp.where(forward, index, count - 1 - index)
        start = pl.multiple_of(chunk * width, width)
        for row in range(rows):
            tile_ref[row * width : (row + 1) * width, :] = cost_ref[row, pl.ds(start, width), :]
        tile_ref[...] = tile_ref[...].T
        planes = [tile_ref[pl.ds(v, 8, stride=16), :] for v in range(16)]

        def spread(step, carry):
            col = jnp.where(forward, step, width - 1 - step)
            index = lane_base + col
            for v in range(16):
                spread_ref[step, v] = jnp.take_along_axis(planes[v], index, axis=1)
            return carry

        lax.fori_loop(0, width, spread, 0, unroll=4)

        def advance(step, state):
            col = jnp.where(forward, step, width - 1 - step)
            mask = lane_col == col
            low = lowest(state)
            bound = low + P_LARGE
            above = jnp.where(sublane == 7, BIG, pltpu.roll(state[0], 7, 0))
            below = jnp.where(sublane == 0, BIG, pltpu.roll(state[15], 1, 0))
            padded = [below] + list(state) + [above]
            fresh = []
            for v in range(16):
                near = jnp.minimum(padded[v], padded[v + 2]) + P_SMALL
                best = jnp.minimum(jnp.minimum(state[v], near), bound)
                value = spread_ref[step, v] + best
                pltpu.store(path_ref.at[v], value, mask=mask)
                fresh.append(value)
            pltpu.store(low_ref, low, mask=mask)
            return tuple(fresh)

        def group(step4, state):
            for k in range(4):
                state = advance(step4 * 4 + k, state)
            return state

        state = lax.fori_loop(0, width // 4, group, state)
        low = low_ref[...]
        for v in range(16):
            tile_ref[pl.ds(v, 8, stride=16), :] = path_ref[v] - low
        done = tile_ref[...].T
        for row in range(rows):
            piece = done[row * width : (row + 1) * width]
            if has_sum:
                piece = piece + lead_ref[row, pl.ds(start, width), :]
            out_ref[row, pl.ds(start, width), :] = piece
        low = lowest(state)
        return tuple(value - low for value in state)

    state = tuple(state_ref[v] for v in range(16))
    state = lax.fori_loop(0, count, one_chunk, state)
    for v in range(16):
        end_ref[v] = state[v]


def row_scan(place, cost, state, lead, flip):
    rows, cols, _ = cost.shape
    width = LANES // rows
    vmem = pl.BlockSpec(memory_space=pltpu.VMEM)
    args = [place, cost, state] + ([] if lead is None else [lead])
    return pl.pallas_call(
        functools.partial(row_scan_kernel, (rows, cols, flip), lead is not None),
        out_shape=(
            jax.ShapeDtypeStruct(cost.shape, jnp.float32),
            jax.ShapeDtypeStruct((16, 8, LANES), jnp.float32),
        ),
        in_specs=[pl.BlockSpec(memory_space=pltpu.SMEM)] + [vmem] * (len(args) - 1),
        out_specs=(vmem, vmem),
        scratch_shapes=[
            pltpu.VMEM((LANES, LANES), jnp.float32),
            pltpu.VMEM((width, 16, 8, LANES), jnp.float32),
            pltpu.VMEM((16, 8, LANES), jnp.float32),
            pltpu.VMEM((8, LANES), jnp.float32),
        ],
        compiler_params=pltpu.CompilerParams(vmem_limit_bytes=24 << 20),
        cost_estimate=pl.CostEstimate(flops=2_000_000_000, bytes_accessed=30_000_000, transcendentals=0),
    )(*args)


def column_kernel(cost_ref, out_ref):
    length, width, _ = cost_ref.shape
    lane = lax.broadcasted_iota(jnp.int32, (width, DISP), 1)

    def step(state, cost):
        low = jnp.min(state, axis=1, keepdims=True)
        above = jnp.where(lane == DISP - 1, BIG, pltpu.roll(state, DISP - 1, 1))
        below = jnp.where(lane == 0, BIG, pltpu.roll(state, 1, 1))
        near = jnp.minimum(above, below) + P_SMALL
        return cost + jnp.minimum(jnp.minimum(state, near), low + P_LARGE) - low

    def first(index, states):
        down = step(states[0], cost_ref[index])
        up = step(states[1], cost_ref[length - 1 - index])
        out_ref[index] = down
        out_ref[length - 1 - index] = up
        return down, up

    def second(index, states):
        down = step(states[0], cost_ref[index])
        up = step(states[1], cost_ref[length - 1 - index])
        out_ref[index] += down
        out_ref[length - 1 - index] += up
        return down, up

    zero = jnp.zeros((width, DISP), jnp.float32)
    states = lax.fori_loop(0, length // 2, first, (zero, zero))
    lax.fori_loop(length // 2, length, second, states)


def column_scan(columns):
    vmem = pl.BlockSpec(memory_space=pltpu.VMEM)
    return pl.pallas_call(
        column_kernel,
        out_shape=jax.ShapeDtypeStruct(columns.shape, jnp.float32),
        in_specs=[vmem],
        out_specs=vmem,
        compiler_params=pltpu.CompilerParams(vmem_limit_bytes=24 << 20),
        cost_estimate=pl.CostEstimate(flops=200_000_000, bytes_accessed=2_000_000, transcendentals=0),
    )(columns)


def normalize(image_pixels):
    return (image_pixels.astype(jnp.float32) / 1024.0 - 2.0).astype(jnp.bfloat16)


def layer_weights(conv_weights, rows_in, rows_out):
    base = jnp.transpose(conv_weights, (0, 4, 3, 2, 1))
    taps = base.shape[2]
    columns = [
        jnp.pad(base, ((0, 0), (0, 0), (row, rows_in - taps - row), (0, 0), (0, 0)))
        for row in range(rows_out)
    ]
    joined = jnp.concatenate(columns, axis=-1)
    return joined.reshape(base.shape[0], base.shape[1], rows_in * base.shape[3], rows_out * base.shape[4])


def neighbours(pair, row_axis, strip_axis):
    groups, strips = lax.axis_size(row_axis), lax.axis_size(strip_axis)
    axes = (row_axis, strip_axis)
    strip = lax.axis_index(strip_axis)

    def moved(up, across):
        route = []
        for r in range(groups):
            for s in range(strips):
                source = (r + up, s ^ across)
                if 0 <= source[0] < groups:
                    route.append((source[0] * strips + source[1], r * strips + s))
        return lax.ppermute(pair, axes, route)

    bands = []
    for up in (-1, 0, 1):
        own = pair if up == 0 else moved(up, 0)
        other = moved(up, 1)
        joined = jnp.where(strip == 0, jnp.concatenate([own, other], 2), jnp.concatenate([other, own], 2))
        bands.append(joined)
    return jnp.concatenate(bands, axis=1)


def stacked(image, start, length, flipped):
    parts = []
    for dx in range(3):
        part = lax.dynamic_slice_in_dim(image, start + dx - 1, length, 1)
        parts.append(part[:, ::-1] if flipped else part)
    joined = jnp.concatenate(parts, axis=0)
    joined = jnp.pad(joined, ((0, LANES - joined.shape[0]), (0, 0)))
    return joined.T


def per_device(left_pixels, right_pixels, valid_mask, first_weight, conv_weights):
    rows, cols = left_pixels.shape
    groups, strips = lax.axis_size("rows"), lax.axis_size("strips")
    group, strip = lax.axis_index("rows"), lax.axis_index("strips")
    total_rows, total_cols = rows * groups, cols * strips

    wt = layer_weights(conv_weights, 6, 4)
    w1 = layer_weights(first_weight[None], rows + 8, rows + 6)[0].reshape(3 * (rows + 8), (rows + 6) * CH)
    w1 = jnp.pad(w1, ((0, LANES - w1.shape[0]), (0, 0)))

    pair = jnp.stack([normalize(left_pixels), normalize(right_pixels)])
    band = neighbours(pair, "rows", "strips")[:, rows - 4 : 2 * rows + 4]
    left_length, right_length = plan(cols)[0][1], plan(cols + DISP)[0][1]
    margin = right_length + 8
    band = jnp.pad(band, ((0, 0), (0, 0), (margin, margin)))
    first_col = strip * cols
    left_stack = stacked(band[0], margin + first_col - 3 * EDGE, left_length, False)
    right_start = first_col + cols - 1 + 3 * EDGE - (right_length - 1)
    right_stack = stacked(band[1], margin + right_start, right_length, True)
    scale = -1.0 / math.sqrt(CH)
    mask = jnp.repeat((valid_mask.astype(jnp.float32) * scale).astype(jnp.bfloat16).T, CH, axis=1)
    place = jnp.stack([group * rows, first_col, strip]).astype(jnp.int32)

    cost = cost_volume(left_stack, right_stack, mask, w1, wt, place, rows, cols, total_rows, total_cols)

    per_group = cols // groups
    grouped = jnp.swapaxes(cost.reshape(rows, groups, per_group, DISP), 0, 1)
    columns = lax.all_to_all(grouped, "rows", split_axis=0, concat_axis=0, tiled=True)
    columns = columns.reshape(total_rows, per_group, DISP)

    zero = jnp.zeros((16, 8, LANES), jnp.float32)
    leading, end = row_scan(place, cost, zero, None, False)
    received = lax.ppermute(end, "strips", [(i, i ^ 1) for i in range(strips)])
    column_sum = column_scan(columns)
    vertical = lax.all_to_all(
        column_sum.reshape(groups, rows, per_group, DISP), "rows", split_axis=0, concat_axis=0, tiled=True
    )
    horizontal, _ = row_scan(place, cost, received, leading, True)
    vertical = jnp.swapaxes(vertical, 0, 1).reshape(rows, cols, DISP)
    return horizontal + vertical


def solution(mesh):
    in_specs = (P("rows", "strips"), P("rows", "strips"), P("rows", "strips"), P(), P())
    out_specs = P("rows", "strips", None)
    return jax.shard_map(
        per_device, mesh=mesh, in_specs=in_specs, out_specs=out_specs, check_vma=False
    )
```

```python
import functools
import math

import jax
import jax.numpy as jnp
from jax import lax
from jax.experimental import pallas as pl
from jax.experimental.pallas import tpu as pltpu
from jax.sharding import PartitionSpec as P

DISP = 128
P_SMALL = 0.5
P_LARGE = 2.0
BIG = 3.0e38
CH = 64
EDGE = 8
LANES = 128
BATCH = 4


def chunking(need):
    best = None
    for size in (128, 144, 160, 176):
        total = -(-need // size) * size
        if best is None or total < best[1]:
            best = (size, total)
    return best


def plan(width):
    steps = [chunking(width)]
    for _ in range(2):
        steps.append(chunking(steps[-1][1] + 2 * EDGE))
    need = steps[-1][1] + 2 * EDGE
    steps.append((128, -(-need // 128) * 128))
    return steps[::-1]


def feature_stack(pix_ref, w1_ref, wt_ref, bufs, sizes, col_of, row_low, row_high, flipped, last_mask_ref):
    def in_image(base, count, lanes, halo, lane0):
        position = lax.broadcasted_iota(jnp.int32, (count, lanes), 0) + base
        row = (lax.broadcasted_iota(jnp.int32, (count, lanes), 1) + lane0) // CH - halo
        low, high = col_of(position)
        return low & high & (row >= row_low) & (row < row_high)

    chunk, total = sizes[0]
    lanes = bufs[0].shape[1]

    def first(index, carry):
        start = pl.multiple_of(index * chunk, chunk)
        value = jnp.dot(pix_ref[pl.ds(start, chunk), :], w1_ref[...], preferred_element_type=jnp.float32)
        inside = in_image(start - 3 * EDGE, chunk, lanes, 3, 0)
        value = jnp.where(inside, jnp.maximum(value, 0.0), 0.0)
        bufs[0][pl.ds(start, chunk), :] = value.astype(jnp.bfloat16)
        return carry

    lax.fori_loop(0, total // chunk, first, 0)

    for layer in range(1, 4):
        source, target = bufs[layer - 1], bufs[layer]
        out_rows = target.shape[1] // CH
        chunk, total = sizes[layer]
        reach = chunk + 2 * EDGE
        for group in range(0, out_rows, 4):
            count = min(4, out_rows - group)
            wide, deep = count * CH, (count + 2) * CH

            def convolve(index, carry, layer=layer, group=group, wide=wide, deep=deep, chunk=chunk, reach=reach, source=source, target=target):
                start = pl.multiple_of(index * chunk, 16)
                block = source[pl.ds(start, reach), group * CH : group * CH + deep]
                parts = [
                    jnp.dot(block, wt_ref[layer - 1, dx, :deep, :wide], preferred_element_type=jnp.float32)
                    for dx in range(3)
                ]
                before, after = (parts[2], parts[0]) if flipped else (parts[0], parts[2])
                value = pltpu.roll(before, 1, 0) + parts[1] + pltpu.roll(after, reach - 1, 0)
                value = value[EDGE : EDGE + chunk]
                halo = 3 - layer
                if layer < 3:
                    value = jnp.maximum(value, 0.0)
                inside = in_image(start - halo * EDGE, chunk, wide, halo, group * CH)
                value = jnp.where(inside, value, 0.0).astype(jnp.bfloat16)
                target[pl.ds(start, chunk), group * CH : group * CH + wide] = value
                return carry

            lax.fori_loop(0, total // chunk, convolve, 0)


def cost_kernel(dims, where_ref, left_ref, right_ref, mask_ref, w1_ref, wt_ref, cost_ref, *bufs):
    rows, cols, total_rows, total_cols = dims
    first_row, first_col = where_ref[0], where_ref[1]
    row_low, row_high = -first_row, total_rows - first_row
    left_bufs, right_bufs = bufs[:4], bufs[4:]

    def left_col(position):
        col = position + first_col
        return col >= 0, col < total_cols

    def right_col(position):
        col = first_col + cols - 1 - position
        return col >= 0, col < total_cols

    feature_stack(left_ref, w1_ref, wt_ref, left_bufs, plan(cols), left_col, row_low, row_high, False, mask_ref)
    feature_stack(right_ref, w1_ref, wt_ref, right_bufs, plan(cols + DISP), right_col, row_low, row_high, True, None)
    left, right = left_bufs[3], right_bufs[3]
    for row in range(rows):
        pair = row // 2 * LANES
        lane = lax.broadcasted_iota(jnp.int32, (LANES, LANES), 1)
        own = (lane // CH) == row % 2

        def block(index, carry, pair=pair, own=own, row=row):
            start = pl.multiple_of(index * LANES, LANES)
            window = pl.multiple_of(cols - LANES - start, LANES)
            scale = mask_ref[pl.ds(start, LANES), pair : pair + LANES]
            a = jnp.where(own, left[pl.ds(start, LANES), pair : pair + LANES] * scale, jnp.zeros((), jnp.bfloat16))
            b = right[pl.ds(window, 2 * LANES), pair : pair + LANES]
            product = lax.dot_general(a, b, (((1,), (1,)), ((), ())), preferred_element_type=jnp.float32)
            skewed = pltpu.roll(product, LANES + 1, 1, stride=1, stride_axis=0)
            cost_ref[row, pl.ds(start, LANES), :] = skewed[:, :LANES]
            return carry

        lax.fori_loop(0, cols // LANES, block, 0)


def cost_volume(left_stack, right_stack, mask, w1, wt, place, rows, cols, total_rows, total_cols):
    bufs = []
    for width in (cols, cols + DISP):
        sizes = plan(width)
        for layer in range(4):
            out_rows = rows + 2 * (3 - layer)
            length = sizes[layer][1]
            bufs.append(pltpu.VMEM((length, out_rows * CH), jnp.bfloat16))
    vmem = pl.BlockSpec(memory_space=pltpu.VMEM)
    return pl.pallas_call(
        functools.partial(cost_kernel, (rows, cols, total_rows, total_cols)),
        out_shape=jax.ShapeDtypeStruct((rows, cols, DISP), jnp.float32),
        in_specs=[pl.BlockSpec(memory_space=pltpu.SMEM)] + [vmem] * 5,
        out_specs=vmem,
        scratch_shapes=bufs,
        compiler_params=pltpu.CompilerParams(vmem_limit_bytes=40 << 20),
        cost_estimate=pl.CostEstimate(flops=8_000_000_000, bytes_accessed=6_000_000, transcendentals=0),
    )(place, left_stack, right_stack, mask, w1, wt)


def row_scan_kernel(dims, has_sum, place_ref, cost_ref, state_ref, *rest):
    rows, cols, flip, batch = dims
    if has_sum:
        lead_ref, rest = rest[0], rest[1:]
    out_ref, end_ref, tile_ref, turn_ref, pick_ref, split_ref, even_ref, odd_ref, path_ref, low_ref = rest
    width = LANES // rows
    count = cols // width
    forward = place_ref[2] == (1 if flip else 0)
    lane = lax.broadcasted_iota(jnp.int32, (8, LANES), 1)
    sublane = lax.broadcasted_iota(jnp.int32, (8, LANES), 0)
    lane_col = lane % width

    def build_pick(pair, carry):
        k = lax.broadcasted_iota(jnp.int32, (2 * LANES, 2 * LANES), 0) % LANES
        n = lax.broadcasted_iota(jnp.int32, (2 * LANES, 2 * LANES), 1)
        wanted = n % LANES // width * width + 2 * pair + n // LANES
        pick_ref[pair] = jnp.where(k == wanted, 1.0, 0.0).astype(jnp.bfloat16)
        return carry

    lax.fori_loop(0, width // 2, build_pick, 0)

    def lowest(state):
        level = list(state)
        while len(level) > 1:
            level = [jnp.minimum(level[i], level[i + 1]) for i in range(0, len(level), 2)]
        low = level[0]
        for shift in (4, 2, 1):
            low = jnp.minimum(low, pltpu.roll(low, shift, 0))
        return low

    def chunk_start(index):
        chunk = jnp.where(forward, index, count - 1 - index)
        return pl.multiple_of(chunk * width, width)

    def split(base, slot):
        start = chunk_start(base + slot)
        for row in range(rows):
            tile_ref[slot, row * width : (row + 1) * width, :] = cost_ref[row, pl.ds(start, width), :]
        tile_ref[slot] = tile_ref[slot].T
        for v in range(0, 16, 2):
            plane = jnp.concatenate(
                [tile_ref[slot, pl.ds(v, 8, stride=16), :], tile_ref[slot, pl.ds(v + 1, 8, stride=16), :]], axis=0
            )
            high = plane.astype(jnp.bfloat16)
            split_ref[slot * LANES + v * 8 : slot * LANES + v * 8 + 16, :LANES] = high
            split_ref[slot * LANES + v * 8 : slot * LANES + v * 8 + 16, LANES:] = (plane - high.astype(jnp.float32)).astype(jnp.bfloat16)

    def spread(target, pair):
        weight = pick_ref[pair]
        both = jnp.dot(split_ref[...], weight, preferred_element_type=jnp.float32)
        for slot in range(batch):
            target[slot, 2 * pair] = both[slot * LANES : slot * LANES + LANES, :LANES]
            target[slot, 2 * pair + 1] = both[slot * LANES : slot * LANES + LANES, LANES:]

    def one_batch(number, state, current, coming):
        base = number * batch
        later = jnp.minimum(base + batch, count - batch)
        for slot in range(batch):
            split(later, slot)

        def one_chunk(slot, state):
            def advance(step, state):
                col = jnp.where(forward, step, width - 1 - step)
                mask = lane_col == col
                low = lowest(state)
                bound = low + P_LARGE
                above = jnp.where(sublane == 7, BIG, pltpu.roll(state[0], 7, 0))
                below = jnp.where(sublane == 0, BIG, pltpu.roll(state[15], 1, 0))
                padded = [below] + list(state) + [above]
                fresh = []
                for v in range(16):
                    near = jnp.minimum(padded[v], padded[v + 2]) + P_SMALL
                    best = jnp.minimum(jnp.minimum(state[v], near), bound)
                    value = current[slot, col, v * 8 : v * 8 + 8, :] + best
                    pltpu.store(path_ref.at[v], value, mask=mask)
                    fresh.append(value)
                pltpu.store(low_ref, low, mask=mask)
                return tuple(fresh)

            per_pair = 2 * batch

            def group(index, state):
                spread(coming, slot * (width // per_pair) + index)
                for k in range(per_pair):
                    state = advance(index * per_pair + k, state)
                return state

            state = lax.fori_loop(0, width // per_pair, group, state)
            start = chunk_start(base + slot)
            low = low_ref[...]
            for v in range(16):
                turn_ref[pl.ds(v, 8, stride=16), :] = path_ref[v] - low
            done = turn_ref[...].T
            for row in range(rows):
                piece = done[row * width : (row + 1) * width]
                if has_sum:
                    piece = piece + lead_ref[row, pl.ds(start, width), :]
                out_ref[row, pl.ds(start, width), :] = piece
            low = lowest(state)
            return tuple(value - low for value in state)

        return lax.fori_loop(0, batch, one_chunk, state)

    for slot in range(batch):
        split(0, slot)

    def first(pair, carry):
        spread(even_ref, pair)
        return carry

    lax.fori_loop(0, width // 2, first, 0)

    def two_batches(index, state):
        state = one_batch(2 * index, state, even_ref, odd_ref)
        return one_batch(2 * index + 1, state, odd_ref, even_ref)

    state = tuple(state_ref[v] for v in range(16))
    state = lax.fori_loop(0, count // batch // 2, two_batches, state)
    for v in range(16):
        end_ref[v] = state[v]


def row_scan(place, cost, state, lead, flip):
    rows, cols, _ = cost.shape
    width = LANES // rows
    batch = math.gcd(cols // width // 2, BATCH)
    vmem = pl.BlockSpec(memory_space=pltpu.VMEM)
    args = [place, cost, state] + ([] if lead is None else [lead])
    return pl.pallas_call(
        functools.partial(row_scan_kernel, (rows, cols, flip, batch), lead is not None),
        out_shape=(
            jax.ShapeDtypeStruct(cost.shape, jnp.float32),
            jax.ShapeDtypeStruct((16, 8, LANES), jnp.float32),
        ),
        in_specs=[pl.BlockSpec(memory_space=pltpu.SMEM)] + [vmem] * (len(args) - 1),
        out_specs=(vmem, vmem),
        scratch_shapes=[
            pltpu.VMEM((batch, LANES, LANES), jnp.float32),
            pltpu.VMEM((LANES, LANES), jnp.float32),
            pltpu.VMEM((width // 2, 2 * LANES, 2 * LANES), jnp.bfloat16),
            pltpu.VMEM((batch * LANES, 2 * LANES), jnp.bfloat16),
            pltpu.VMEM((batch, width, LANES, LANES), jnp.float32),
            pltpu.VMEM((batch, width, LANES, LANES), jnp.float32),
            pltpu.VMEM((16, 8, LANES), jnp.float32),
            pltpu.VMEM((8, LANES), jnp.float32),
        ],
        compiler_params=pltpu.CompilerParams(vmem_limit_bytes=40 << 20),
        cost_estimate=pl.CostEstimate(flops=2_000_000_000, bytes_accessed=30_000_000, transcendentals=0),
    )(*args)


def column_kernel(cost_ref, out_ref):
    length, width, _ = cost_ref.shape
    lane = lax.broadcasted_iota(jnp.int32, (width, DISP), 1)

    def step(state, cost):
        low = jnp.min(state, axis=1, keepdims=True)
        above = jnp.where(lane == DISP - 1, BIG, pltpu.roll(state, DISP - 1, 1))
        below = jnp.where(lane == 0, BIG, pltpu.roll(state, 1, 1))
        near = jnp.minimum(above, below) + P_SMALL
        return cost + jnp.minimum(jnp.minimum(state, near), low + P_LARGE) - low

    def first(index, states):
        down = step(states[0], cost_ref[index])
        up = step(states[1], cost_ref[length - 1 - index])
        out_ref[index] = down
        out_ref[length - 1 - index] = up
        return down, up

    def second(index, states):
        down = step(states[0], cost_ref[index])
        up = step(states[1], cost_ref[length - 1 - index])
        out_ref[index] += down
        out_ref[length - 1 - index] += up
        return down, up

    zero = jnp.zeros((width, DISP), jnp.float32)
    states = lax.fori_loop(0, length // 2, first, (zero, zero))
    lax.fori_loop(length // 2, length, second, states)


def column_scan(columns):
    vmem = pl.BlockSpec(memory_space=pltpu.VMEM)
    return pl.pallas_call(
        column_kernel,
        out_shape=jax.ShapeDtypeStruct(columns.shape, jnp.float32),
        in_specs=[vmem],
        out_specs=vmem,
        compiler_params=pltpu.CompilerParams(vmem_limit_bytes=24 << 20),
        cost_estimate=pl.CostEstimate(flops=200_000_000, bytes_accessed=2_000_000, transcendentals=0),
    )(columns)


def normalize(image_pixels):
    return (image_pixels.astype(jnp.float32) / 1024.0 - 2.0).astype(jnp.bfloat16)


def layer_weights(conv_weights, rows_in, rows_out):
    base = jnp.transpose(conv_weights, (0, 4, 3, 2, 1))
    taps = base.shape[2]
    columns = [
        jnp.pad(base, ((0, 0), (0, 0), (row, rows_in - taps - row), (0, 0), (0, 0)))
        for row in range(rows_out)
    ]
    joined = jnp.concatenate(columns, axis=-1)
    return joined.reshape(base.shape[0], base.shape[1], rows_in * base.shape[3], rows_out * base.shape[4])


def neighbours(pair, row_axis, strip_axis):
    groups, strips = lax.axis_size(row_axis), lax.axis_size(strip_axis)
    axes = (row_axis, strip_axis)
    strip = lax.axis_index(strip_axis)

    def moved(up, across):
        route = []
        for r in range(groups):
            for s in range(strips):
                source = (r + up, s ^ across)
                if 0 <= source[0] < groups:
                    route.append((source[0] * strips + source[1], r * strips + s))
        return lax.ppermute(pair, axes, route)

    bands = []
    for up in (-1, 0, 1):
        own = pair if up == 0 else moved(up, 0)
        other = moved(up, 1)
        joined = jnp.where(strip == 0, jnp.concatenate([own, other], 2), jnp.concatenate([other, own], 2))
        bands.append(joined)
    return jnp.concatenate(bands, axis=1)


def stacked(image, start, length, flipped):
    parts = []
    for dx in range(3):
        part = lax.dynamic_slice_in_dim(image, start + dx - 1, length, 1)
        parts.append(part[:, ::-1] if flipped else part)
    joined = jnp.concatenate(parts, axis=0)
    joined = jnp.pad(joined, ((0, LANES - joined.shape[0]), (0, 0)))
    return joined.T


def per_device(left_pixels, right_pixels, valid_mask, first_weight, conv_weights):
    rows, cols = left_pixels.shape
    groups, strips = lax.axis_size("rows"), lax.axis_size("strips")
    group, strip = lax.axis_index("rows"), lax.axis_index("strips")
    total_rows, total_cols = rows * groups, cols * strips

    wt = layer_weights(conv_weights, 6, 4)
    w1 = layer_weights(first_weight[None], rows + 8, rows + 6)[0].reshape(3 * (rows + 8), (rows + 6) * CH)
    w1 = jnp.pad(w1, ((0, LANES - w1.shape[0]), (0, 0)))

    pair = jnp.stack([normalize(left_pixels), normalize(right_pixels)])
    band = neighbours(pair, "rows", "strips")[:, rows - 4 : 2 * rows + 4]
    left_length, right_length = plan(cols)[0][1], plan(cols + DISP)[0][1]
    margin = right_length + 8
    band = jnp.pad(band, ((0, 0), (0, 0), (margin, margin)))
    first_col = strip * cols
    left_stack = stacked(band[0], margin + first_col - 3 * EDGE, left_length, False)
    right_start = first_col + cols - 1 + 3 * EDGE - (right_length - 1)
    right_stack = stacked(band[1], margin + right_start, right_length, True)
    scale = -1.0 / math.sqrt(CH)
    mask = jnp.repeat((valid_mask.astype(jnp.float32) * scale).astype(jnp.bfloat16).T, CH, axis=1)
    place = jnp.stack([group * rows, first_col, strip]).astype(jnp.int32)

    cost = cost_volume(left_stack, right_stack, mask, w1, wt, place, rows, cols, total_rows, total_cols)

    per_group = cols // groups
    grouped = jnp.swapaxes(cost.reshape(rows, groups, per_group, DISP), 0, 1)
    columns = lax.all_to_all(grouped, "rows", split_axis=0, concat_axis=0, tiled=True)
    columns = columns.reshape(total_rows, per_group, DISP)

    zero = jnp.zeros((16, 8, LANES), jnp.float32)
    leading, end = row_scan(place, cost, zero, None, False)
    columns, end = lax.optimization_barrier((columns, end))
    column_sum = column_scan(columns)
    received = lax.ppermute(end, "strips", [(i, i ^ 1) for i in range(strips)])
    vertical = lax.all_to_all(
        column_sum.reshape(groups, rows, per_group, DISP), "rows", split_axis=0, concat_axis=0, tiled=True
    )
    horizontal, _ = row_scan(place, cost, received, leading, True)
    vertical = jnp.swapaxes(vertical, 0, 1).reshape(rows, cols, DISP)
    return horizontal + vertical


def solution(mesh):
    in_specs = (P("rows", "strips"), P("rows", "strips"), P("rows", "strips"), P(), P())
    out_specs = P("rows", "strips", None)
    return jax.shard_map(
        per_device, mesh=mesh, in_specs=in_specs, out_specs=out_specs, check_vma=False
    )
```

```python
import functools
import math

import jax
import jax.numpy as jnp
from jax import lax
from jax.experimental import pallas as pl
from jax.experimental.pallas import tpu as pltpu
from jax.sharding import PartitionSpec as P

DISP = 128
P_SMALL = 0.5
P_LARGE = 2.0
BIG = 3.0e38
CH = 64
EDGE = 8
LANES = 128
BATCH = 4
PARTS = 1
BLOCKS = 4


def plan(width):
    unit = 16 * PARTS
    totals = [-(-width // unit) * unit]
    for _ in range(3):
        totals.append(-(-(totals[-1] + 2 * EDGE) // unit) * unit)
    return totals[::-1]


def feature_stacks(stacks, w1_ref, wt_ref, row_low, row_high):
    def inside(test, base, count, lanes, halo, lane0):
        position = lax.broadcasted_iota(jnp.int32, (count, lanes), 0) + base
        row = (lax.broadcasted_iota(jnp.int32, (count, lanes), 1) + lane0) // CH - halo
        return test(position) & (row >= row_low) & (row < row_high)

    def first(index, carry):
        for pix_ref, bufs, test, flipped in stacks:
            chunk = bufs[0].shape[0] // PARTS
            start = pl.multiple_of(index * chunk, 16)
            value = jnp.dot(pix_ref[pl.ds(start, chunk), :], w1_ref[...], preferred_element_type=jnp.float32)
            keep = inside(test, start - 3 * EDGE, chunk, bufs[0].shape[1], 3, 0)
            bufs[0][pl.ds(start, chunk), :] = jnp.where(keep, jnp.maximum(value, 0.0), 0.0).astype(jnp.bfloat16)
        return carry

    lax.fori_loop(0, PARTS, first, 0)

    for layer in range(1, 4):

        def convolve(index, carry, layer=layer):
            halo = 3 - layer
            for pix_ref, bufs, test, flipped in stacks:
                source, target = bufs[layer - 1], bufs[layer]
                out_rows = target.shape[1] // CH
                chunk = target.shape[0] // PARTS
                reach = chunk + 2 * EDGE
                start = pl.multiple_of(index * chunk, 16)
                for group in range(0, out_rows, 4):
                    count = min(4, out_rows - group)
                    wide, deep = count * CH, (count + 2) * CH
                    block = source[pl.ds(start, reach), group * CH : group * CH + deep]
                    parts = [
                        jnp.dot(block, wt_ref[layer - 1, dx, :deep, :wide], preferred_element_type=jnp.float32)
                        for dx in range(3)
                    ]
                    before, after = (parts[2], parts[0]) if flipped else (parts[0], parts[2])
                    value = pltpu.roll(before, 1, 0) + parts[1] + pltpu.roll(after, reach - 1, 0)
                    value = value[EDGE : EDGE + chunk]
                    if layer < 3:
                        value = jnp.maximum(value, 0.0)
                    keep = inside(test, start - halo * EDGE, chunk, wide, halo, group * CH)
                    value = jnp.where(keep, value, 0.0).astype(jnp.bfloat16)
                    target[pl.ds(start, chunk), group * CH : group * CH + wide] = value
            return carry

        lax.fori_loop(0, PARTS, convolve, 0)


def cost_kernel(dims, where_ref, left_ref, right_ref, mask_ref, w1_ref, wt_ref, cost_ref, *bufs):
    rows, cols, total_rows, total_cols = dims
    first_row, first_col = where_ref[0], where_ref[1]
    row_low, row_high = -first_row, total_rows - first_row
    left_bufs, right_bufs = bufs[:4], bufs[4:]

    def left_col(position):
        col = position + first_col
        return (col >= 0) & (col < total_cols)

    def right_col(position):
        col = first_col + cols - 1 - position
        return (col >= 0) & (col < total_cols)

    feature_stacks(
        [(left_ref, left_bufs, left_col, False), (right_ref, right_bufs, right_col, True)],
        w1_ref, wt_ref, row_low, row_high,
    )
    left, right = left_bufs[3], right_bufs[3]
    for row in range(rows):
        pair = row // 2 * LANES
        lane = lax.broadcasted_iota(jnp.int32, (LANES, LANES), 1)
        own = (lane // CH) == row % 2

        def block(index, carry, pair=pair, own=own, row=row):
            start = pl.multiple_of(index * LANES, LANES)
            window = pl.multiple_of(cols - LANES - start, LANES)
            scale = mask_ref[pl.ds(start, LANES), pair : pair + LANES]
            a = jnp.where(own, left[pl.ds(start, LANES), pair : pair + LANES] * scale, jnp.zeros((), jnp.bfloat16))
            b = right[pl.ds(window, 2 * LANES), pair : pair + LANES]
            product = lax.dot_general(a, b, (((1,), (1,)), ((), ())), preferred_element_type=jnp.float32)
            skewed = pltpu.roll(product, LANES + 1, 1, stride=1, stride_axis=0)
            cost_ref[row, pl.ds(start, LANES), :] = skewed[:, :LANES]
            return carry

        lax.fori_loop(0, cols // LANES, block, 0, unroll=BLOCKS)


def cost_volume(left_stack, right_stack, mask, w1, wt, place, rows, cols, total_rows, total_cols):
    bufs = []
    for width in (cols, cols + DISP):
        sizes = plan(width)
        for layer in range(4):
            out_rows = rows + 2 * (3 - layer)
            length = sizes[layer]
            bufs.append(pltpu.VMEM((length, out_rows * CH), jnp.bfloat16))
    vmem = pl.BlockSpec(memory_space=pltpu.VMEM)
    return pl.pallas_call(
        functools.partial(cost_kernel, (rows, cols, total_rows, total_cols)),
        out_shape=jax.ShapeDtypeStruct((rows, cols, DISP), jnp.float32),
        in_specs=[pl.BlockSpec(memory_space=pltpu.SMEM)] + [vmem] * 5,
        out_specs=vmem,
        scratch_shapes=bufs,
        compiler_params=pltpu.CompilerParams(vmem_limit_bytes=40 << 20),
        cost_estimate=pl.CostEstimate(flops=8_000_000_000, bytes_accessed=6_000_000, transcendentals=0),
    )(place, left_stack, right_stack, mask, w1, wt)


def row_scan_kernel(dims, has_sum, place_ref, cost_ref, state_ref, *rest):
    rows, cols, flip, batch = dims
    if has_sum:
        lead_ref, rest = rest[0], rest[1:]
    out_ref, end_ref, tile_ref, turn_ref, pick_ref, split_a, split_b, even_ref, odd_ref, path_ref, low_ref = rest
    width = LANES // rows
    count = cols // width
    forward = place_ref[2] == (1 if flip else 0)
    lane = lax.broadcasted_iota(jnp.int32, (8, LANES), 1)
    sublane = lax.broadcasted_iota(jnp.int32, (8, LANES), 0)
    lane_col = lane % width

    def build_pick(pair, carry):
        k = lax.broadcasted_iota(jnp.int32, (2 * LANES, 2 * LANES), 0) % LANES
        n = lax.broadcasted_iota(jnp.int32, (2 * LANES, 2 * LANES), 1)
        wanted = n % LANES // width * width + 2 * pair + n // LANES
        pick_ref[pair] = jnp.where(k == wanted, 1.0, 0.0).astype(jnp.bfloat16)
        return carry

    lax.fori_loop(0, width // 2, build_pick, 0)

    def lowest(state):
        level = list(state)
        while len(level) > 1:
            level = [jnp.minimum(level[i], level[i + 1]) for i in range(0, len(level), 2)]
        low = level[0]
        for shift in (4, 2, 1):
            low = jnp.minimum(low, pltpu.roll(low, shift, 0))
        return low

    def chunk_start(index):
        chunk = jnp.where(forward, index, count - 1 - index)
        return pl.multiple_of(chunk * width, width)

    def split(index, target):
        start = chunk_start(jnp.minimum(index, count - 1))
        tile = jnp.concatenate([cost_ref[row, pl.ds(start, width), :] for row in range(rows)], axis=0)
        tile_ref[...] = tile.T
        for v in range(0, 16, 2):
            plane = jnp.concatenate(
                [tile_ref[pl.ds(v, 8, stride=16), :], tile_ref[pl.ds(v + 1, 8, stride=16), :]], axis=0
            )
            high = plane.astype(jnp.bfloat16)
            low = (plane - high.astype(jnp.float32)).astype(jnp.bfloat16)
            target[v * 8 : v * 8 + 16, :LANES] = high
            target[v * 8 : v * 8 + 16, LANES:] = low

    def spread(source, target, pair):
        both = jnp.dot(source[...], pick_ref[pair], preferred_element_type=jnp.float32)
        for slot in range(batch):
            target[slot, 2 * pair] = both[slot * LANES : slot * LANES + LANES, :LANES]
            target[slot, 2 * pair + 1] = both[slot * LANES : slot * LANES + LANES, LANES:]

    def emit(index):
        start = chunk_start(jnp.maximum(index, 0))
        low = low_ref[...]
        for v in range(16):
            turn_ref[pl.ds(v, 8, stride=16), :] = path_ref[v] - low
        done = turn_ref[...].T
        for row in range(rows):
            piece = done[row * width : (row + 1) * width]
            if has_sum:
                piece = piece + lead_ref[row, pl.ds(start, width), :]
            out_ref[row, pl.ds(start, width), :] = piece

    def advance(state, low, slot, step, current):
        col = jnp.where(forward, step, width - 1 - step)
        mask = lane_col == col
        bound = low + P_LARGE
        above = jnp.where(sublane == 7, BIG, pltpu.roll(state[0], 7, 0))
        below = jnp.where(sublane == 0, BIG, pltpu.roll(state[15], 1, 0))
        padded = [below] + list(state) + [above]
        fresh = []
        for v in range(16):
            near = jnp.minimum(padded[v], padded[v + 2]) + P_SMALL
            best = jnp.minimum(jnp.minimum(state[v], near), bound)
            value = current[slot, col, v * 8 : v * 8 + 8, :] + best
            pltpu.store(path_ref.at[v], value, mask=mask)
            fresh.append(value)
        pltpu.store(low_ref, low, mask=mask)
        return fresh

    def one_batch(number, state, current, coming, ready, filling):
        base = number * batch
        pairs = width // 2 // batch

        def one_chunk(slot, state):
            emit(base + slot - 1)
            split(base + 2 * batch + slot, filling.at[pl.ds(pl.multiple_of(slot * LANES, LANES), LANES)])
            low = lowest(state)
            state = [value - low for value in state]
            low = jnp.zeros_like(low)
            for step in range(width):
                if step % (2 * batch) == 0:
                    spread(ready, coming, slot * pairs + step // (2 * batch))
                if step:
                    low = lowest(state)
                state = advance(state, low, slot, step, current)
            return tuple(state)

        return lax.fori_loop(0, batch, one_chunk, state)

    for slot in range(batch):
        split(slot, split_a.at[pl.ds(slot * LANES, LANES)])
        split(batch + slot, split_b.at[pl.ds(slot * LANES, LANES)])

    def first(group, carry):
        for k in range(4):
            spread(split_a, even_ref, group * 4 + k)
        return carry

    lax.fori_loop(0, width // 8, first, 0)

    def two_batches(index, state):
        state = one_batch(2 * index, state, even_ref, odd_ref, split_b, split_a)
        return one_batch(2 * index + 1, state, odd_ref, even_ref, split_a, split_b)

    state = tuple(state_ref[v] for v in range(16))
    state = lax.fori_loop(0, count // batch // 2, two_batches, state)
    emit(count - 1)
    for v in range(16):
        end_ref[v] = state[v]


def row_scan(place, cost, state, lead, flip):
    rows, cols, _ = cost.shape
    width = LANES // rows
    batch = math.gcd(cols // width // 2, BATCH)
    vmem = pl.BlockSpec(memory_space=pltpu.VMEM)
    args = [place, cost, state] + ([] if lead is None else [lead])
    return pl.pallas_call(
        functools.partial(row_scan_kernel, (rows, cols, flip, batch), lead is not None),
        out_shape=(
            jax.ShapeDtypeStruct(cost.shape, jnp.float32),
            jax.ShapeDtypeStruct((16, 8, LANES), jnp.float32),
        ),
        in_specs=[pl.BlockSpec(memory_space=pltpu.SMEM)] + [vmem] * (len(args) - 1),
        out_specs=(vmem, vmem),
        scratch_shapes=[
            pltpu.VMEM((LANES, LANES), jnp.float32),
            pltpu.VMEM((LANES, LANES), jnp.float32),
            pltpu.VMEM((width // 2, 2 * LANES, 2 * LANES), jnp.bfloat16),
            pltpu.VMEM((batch * LANES, 2 * LANES), jnp.bfloat16),
            pltpu.VMEM((batch * LANES, 2 * LANES), jnp.bfloat16),
            pltpu.VMEM((batch, width, LANES, LANES), jnp.float32),
            pltpu.VMEM((batch, width, LANES, LANES), jnp.float32),
            pltpu.VMEM((16, 8, LANES), jnp.float32),
            pltpu.VMEM((8, LANES), jnp.float32),
        ],
        compiler_params=pltpu.CompilerParams(vmem_limit_bytes=40 << 20),
        cost_estimate=pl.CostEstimate(flops=2_000_000_000, bytes_accessed=30_000_000, transcendentals=0),
    )(*args)


def column_kernel(cost_ref, out_ref):
    length, width, _ = cost_ref.shape
    lane = lax.broadcasted_iota(jnp.int32, (width, DISP), 1)

    def step(state, cost):
        low = jnp.min(state, axis=1, keepdims=True)
        above = jnp.where(lane == DISP - 1, BIG, pltpu.roll(state, DISP - 1, 1))
        below = jnp.where(lane == 0, BIG, pltpu.roll(state, 1, 1))
        near = jnp.minimum(above, below) + P_SMALL
        return cost + jnp.minimum(jnp.minimum(state, near), low + P_LARGE) - low

    def first(index, states):
        down = step(states[0], cost_ref[index])
        up = step(states[1], cost_ref[length - 1 - index])
        out_ref[index] = down
        out_ref[length - 1 - index] = up
        return down, up

    def second(index, states):
        down = step(states[0], cost_ref[index])
        up = step(states[1], cost_ref[length - 1 - index])
        out_ref[index] += down
        out_ref[length - 1 - index] += up
        return down, up

    zero = jnp.zeros((width, DISP), jnp.float32)
    states = lax.fori_loop(0, length // 2, first, (zero, zero))
    lax.fori_loop(length // 2, length, second, states)


def column_scan(columns):
    vmem = pl.BlockSpec(memory_space=pltpu.VMEM)
    return pl.pallas_call(
        column_kernel,
        out_shape=jax.ShapeDtypeStruct(columns.shape, jnp.float32),
        in_specs=[vmem],
        out_specs=vmem,
        compiler_params=pltpu.CompilerParams(vmem_limit_bytes=24 << 20),
        cost_estimate=pl.CostEstimate(flops=200_000_000, bytes_accessed=2_000_000, transcendentals=0),
    )(columns)


def normalize(image_pixels):
    return (image_pixels.astype(jnp.float32) / 1024.0 - 2.0).astype(jnp.bfloat16)


def layer_weights(conv_weights, rows_in, rows_out):
    base = jnp.transpose(conv_weights, (0, 4, 3, 2, 1))
    taps = base.shape[2]
    columns = [
        jnp.pad(base, ((0, 0), (0, 0), (row, rows_in - taps - row), (0, 0), (0, 0)))
        for row in range(rows_out)
    ]
    joined = jnp.concatenate(columns, axis=-1)
    return joined.reshape(base.shape[0], base.shape[1], rows_in * base.shape[3], rows_out * base.shape[4])


def neighbours(pair, row_axis, strip_axis):
    groups, strips = lax.axis_size(row_axis), lax.axis_size(strip_axis)
    axes = (row_axis, strip_axis)
    strip = lax.axis_index(strip_axis)

    def moved(up, across):
        route = []
        for r in range(groups):
            for s in range(strips):
                source = (r + up, s ^ across)
                if 0 <= source[0] < groups:
                    route.append((source[0] * strips + source[1], r * strips + s))
        return lax.ppermute(pair, axes, route)

    bands = []
    for up in (-1, 0, 1):
        own = pair if up == 0 else moved(up, 0)
        other = moved(up, 1)
        joined = jnp.where(strip == 0, jnp.concatenate([own, other], 2), jnp.concatenate([other, own], 2))
        bands.append(joined)
    return jnp.concatenate(bands, axis=1)


def stacked(image, start, length, flipped):
    parts = []
    for dx in range(3):
        part = lax.dynamic_slice_in_dim(image, start + dx - 1, length, 1)
        parts.append(part[:, ::-1] if flipped else part)
    joined = jnp.concatenate(parts, axis=0)
    joined = jnp.pad(joined, ((0, LANES - joined.shape[0]), (0, 0)))
    return joined.T


def per_device(left_pixels, right_pixels, valid_mask, first_weight, conv_weights):
    rows, cols = left_pixels.shape
    groups, strips = lax.axis_size("rows"), lax.axis_size("strips")
    group, strip = lax.axis_index("rows"), lax.axis_index("strips")
    total_rows, total_cols = rows * groups, cols * strips

    wt = layer_weights(conv_weights, 6, 4)
    w1 = layer_weights(first_weight[None], rows + 8, rows + 6)[0].reshape(3 * (rows + 8), (rows + 6) * CH)
    w1 = jnp.pad(w1, ((0, LANES - w1.shape[0]), (0, 0)))

    pair = jnp.stack([normalize(left_pixels), normalize(right_pixels)])
    band = neighbours(pair, "rows", "strips")[:, rows - 4 : 2 * rows + 4]
    left_length, right_length = plan(cols)[0], plan(cols + DISP)[0]
    margin = right_length + 8
    band = jnp.pad(band, ((0, 0), (0, 0), (margin, margin)))
    first_col = strip * cols
    left_stack = stacked(band[0], margin + first_col - 3 * EDGE, left_length, False)
    right_start = first_col + cols - 1 + 3 * EDGE - (right_length - 1)
    right_stack = stacked(band[1], margin + right_start, right_length, True)
    scale = -1.0 / math.sqrt(CH)
    mask = jnp.repeat((valid_mask.astype(jnp.float32) * scale).astype(jnp.bfloat16).T, CH, axis=1)
    place = jnp.stack([group * rows, first_col, strip]).astype(jnp.int32)

    cost = cost_volume(left_stack, right_stack, mask, w1, wt, place, rows, cols, total_rows, total_cols)

    per_group = cols // groups
    grouped = jnp.swapaxes(cost.reshape(rows, groups, per_group, DISP), 0, 1)
    columns = lax.all_to_all(grouped, "rows", split_axis=0, concat_axis=0, tiled=True)
    columns = columns.reshape(total_rows, per_group, DISP)

    zero = jnp.zeros((16, 8, LANES), jnp.float32)
    leading, end = row_scan(place, cost, zero, None, False)
    columns, end = lax.optimization_barrier((columns, end))
    column_sum = column_scan(columns)
    received = lax.ppermute(end, "strips", [(i, i ^ 1) for i in range(strips)])
    vertical = lax.all_to_all(
        column_sum.reshape(groups, rows, per_group, DISP), "rows", split_axis=0, concat_axis=0, tiled=True
    )
    horizontal, _ = row_scan(place, cost, received, leading, True)
    vertical = jnp.swapaxes(vertical, 0, 1).reshape(rows, cols, DISP)
    return horizontal + vertical


def solution(mesh):
    in_specs = (P("rows", "strips"), P("rows", "strips"), P("rows", "strips"), P(), P())
    out_specs = P("rows", "strips", None)
    return jax.shard_map(
        per_device, mesh=mesh, in_specs=in_specs, out_specs=out_specs, check_vma=False
    )
```

```python
import functools
import math

import jax
import jax.numpy as jnp
from jax import lax
from jax.experimental import pallas as pl
from jax.experimental.pallas import tpu as pltpu
from jax.sharding import PartitionSpec as P

DISP = 128
P_SMALL = 0.5
P_LARGE = 2.0
BIG = 3.0e38
CH = 64
EDGE = 8
LANES = 128
BATCH = 2
PARTS = 1
BLOCKS = 4


def plan(width):
    unit = 16 * PARTS
    totals = [-(-width // unit) * unit]
    for _ in range(3):
        totals.append(-(-(totals[-1] + 2 * EDGE) // unit) * unit)
    return totals[::-1]


def feature_stacks(stacks, w1_ref, wt_ref, row_low, row_high):
    def inside(test, base, count, lanes, halo, lane0):
        position = lax.broadcasted_iota(jnp.int32, (count, lanes), 0) + base
        row = (lax.broadcasted_iota(jnp.int32, (count, lanes), 1) + lane0) // CH - halo
        return test(position) & (row >= row_low) & (row < row_high)

    def first(index, carry):
        for pix_ref, bufs, test, flipped in stacks:
            chunk = bufs[0].shape[0] // PARTS
            start = pl.multiple_of(index * chunk, 16)
            value = jnp.dot(pix_ref[pl.ds(start, chunk), :], w1_ref[...], preferred_element_type=jnp.float32)
            keep = inside(test, start - 3 * EDGE, chunk, bufs[0].shape[1], 3, 0)
            bufs[0][pl.ds(start, chunk), :] = jnp.where(keep, jnp.maximum(value, 0.0), 0.0).astype(jnp.bfloat16)
        return carry

    lax.fori_loop(0, PARTS, first, 0)

    for layer in range(1, 4):

        def convolve(index, carry, layer=layer):
            halo = 3 - layer
            for pix_ref, bufs, test, flipped in stacks:
                source, target = bufs[layer - 1], bufs[layer]
                out_rows = target.shape[1] // CH
                chunk = target.shape[0] // PARTS
                reach = chunk + 2 * EDGE
                start = pl.multiple_of(index * chunk, 16)
                for group in range(0, out_rows, 4):
                    count = min(4, out_rows - group)
                    wide, deep = count * CH, (count + 2) * CH
                    block = source[pl.ds(start, reach), group * CH : group * CH + deep]
                    parts = [
                        jnp.dot(block, wt_ref[layer - 1, dx, :deep, :wide], preferred_element_type=jnp.float32)
                        for dx in range(3)
                    ]
                    before, after = (parts[2], parts[0]) if flipped else (parts[0], parts[2])
                    value = pltpu.roll(before, 1, 0) + parts[1] + pltpu.roll(after, reach - 1, 0)
                    value = value[EDGE : EDGE + chunk]
                    if layer < 3:
                        value = jnp.maximum(value, 0.0)
                    keep = inside(test, start - halo * EDGE, chunk, wide, halo, group * CH)
                    value = jnp.where(keep, value, 0.0).astype(jnp.bfloat16)
                    target[pl.ds(start, chunk), group * CH : group * CH + wide] = value
            return carry

        lax.fori_loop(0, PARTS, convolve, 0)


def packs(per_group):
    return per_group % 16 == 0 and LANES % per_group == 0


def cost_kernel(dims, where_ref, left_ref, right_ref, mask_ref, w1_ref, wt_ref, cost_ref, *rest):
    rows, cols, total_rows, total_cols, per_group = dims
    payload_ref, bufs = (rest[0], rest[1:]) if len(rest) % 2 else (None, rest)
    first_row, first_col = where_ref[0], where_ref[1]
    row_low, row_high = -first_row, total_rows - first_row
    left_bufs, right_bufs = bufs[:4], bufs[4:]

    def left_col(position):
        col = position + first_col
        return (col >= 0) & (col < total_cols)

    def right_col(position):
        col = first_col + cols - 1 - position
        return (col >= 0) & (col < total_cols)

    feature_stacks(
        [(left_ref, left_bufs, left_col, False), (right_ref, right_bufs, right_col, True)],
        w1_ref, wt_ref, row_low, row_high,
    )
    left, right = left_bufs[3], right_bufs[3]
    for row in range(rows):
        pair = row // 2 * LANES
        lane = lax.broadcasted_iota(jnp.int32, (LANES, LANES), 1)
        own = (lane // CH) == row % 2

        def block(index, carry, pair=pair, own=own, row=row):
            start = pl.multiple_of(index * LANES, LANES)
            window = pl.multiple_of(cols - LANES - start, LANES)
            scale = mask_ref[pl.ds(start, LANES), pair : pair + LANES]
            a = jnp.where(own, left[pl.ds(start, LANES), pair : pair + LANES] * scale, jnp.zeros((), jnp.bfloat16))
            b = right[pl.ds(window, 2 * LANES), pair : pair + LANES]
            product = lax.dot_general(a, b, (((1,), (1,)), ((), ())), preferred_element_type=jnp.float32)
            skewed = pltpu.roll(product, LANES + 1, 1, stride=1, stride_axis=0)
            skewed = skewed[:, :LANES]
            cost_ref[row, pl.ds(start, LANES), :] = skewed
            if payload_ref is not None:
                for k in range(LANES // per_group):
                    piece = skewed[k * per_group : (k + 1) * per_group].astype(jnp.bfloat16)
                    group = index * (LANES // per_group) + k
                    payload_ref[group, row * per_group : (row + 1) * per_group, :] = piece
            return carry

        lax.fori_loop(0, cols // LANES, block, 0, unroll=BLOCKS)


def cost_volume(left_stack, right_stack, mask, w1, wt, place, rows, cols, total_rows, total_cols, per_group):
    bufs = []
    for width in (cols, cols + DISP):
        sizes = plan(width)
        for layer in range(4):
            out_rows = rows + 2 * (3 - layer)
            length = sizes[layer]
            bufs.append(pltpu.VMEM((length, out_rows * CH), jnp.bfloat16))
    vmem = pl.BlockSpec(memory_space=pltpu.VMEM)
    shapes = [jax.ShapeDtypeStruct((rows, cols, DISP), jnp.float32)]
    if packs(per_group):
        shapes.append(jax.ShapeDtypeStruct((cols // per_group, rows * per_group, DISP), jnp.bfloat16))
    return pl.pallas_call(
        functools.partial(cost_kernel, (rows, cols, total_rows, total_cols, per_group)),
        out_shape=tuple(shapes),
        in_specs=[pl.BlockSpec(memory_space=pltpu.SMEM)] + [vmem] * 5,
        out_specs=(vmem,) * len(shapes),
        scratch_shapes=bufs,
        compiler_params=pltpu.CompilerParams(vmem_limit_bytes=40 << 20),
        cost_estimate=pl.CostEstimate(flops=8_000_000_000, bytes_accessed=6_000_000, transcendentals=0),
    )(place, left_stack, right_stack, mask, w1, wt)


def row_scan_kernel(dims, has_sum, place_ref, cost_ref, state_ref, *rest):
    rows, cols, flip, batch = dims
    if has_sum:
        lead_ref, rest = rest[0], rest[1:]
    out_ref, end_ref, tile_ref, turn_ref, pick_ref, split_a, split_b, even_ref, odd_ref, path_ref, low_ref = rest
    width = LANES // rows
    count = cols // width
    forward = place_ref[2] == (1 if flip else 0)
    lane = lax.broadcasted_iota(jnp.int32, (8, LANES), 1)
    sublane = lax.broadcasted_iota(jnp.int32, (8, LANES), 0)
    lane_col = lane % width

    def build_pick(pair, carry):
        k = lax.broadcasted_iota(jnp.int32, (2 * LANES, 2 * LANES), 0) % LANES
        n = lax.broadcasted_iota(jnp.int32, (2 * LANES, 2 * LANES), 1)
        wanted = n % LANES // width * width + 2 * pair + n // LANES
        pick_ref[pair] = jnp.where(k == wanted, 1.0, 0.0).astype(jnp.bfloat16)
        return carry

    lax.fori_loop(0, width // 2, build_pick, 0)

    def lowest(state):
        level = list(state)
        while len(level) > 1:
            level = [jnp.minimum(level[i], level[i + 1]) for i in range(0, len(level), 2)]
        low = level[0]
        for shift in (4, 2, 1):
            low = jnp.minimum(low, pltpu.roll(low, shift, 0))
        return low

    def chunk_start(index):
        chunk = jnp.where(forward, index, count - 1 - index)
        return pl.multiple_of(chunk * width, width)

    def split(index, target):
        start = chunk_start(jnp.minimum(index, count - 1))
        tile = jnp.concatenate([cost_ref[row, pl.ds(start, width), :] for row in range(rows)], axis=0)
        tile_ref[...] = tile.T
        for v in range(0, 16, 2):
            plane = jnp.concatenate(
                [tile_ref[pl.ds(v, 8, stride=16), :], tile_ref[pl.ds(v + 1, 8, stride=16), :]], axis=0
            )
            high = plane.astype(jnp.bfloat16)
            low = (plane - high.astype(jnp.float32)).astype(jnp.bfloat16)
            target[v * 8 : v * 8 + 16, :LANES] = high
            target[v * 8 : v * 8 + 16, LANES:] = low

    def spread(source, target, pair):
        both = jnp.dot(source[...], pick_ref[pair], preferred_element_type=jnp.float32)
        for slot in range(batch):
            target[slot, 2 * pair] = both[slot * LANES : slot * LANES + LANES, :LANES]
            target[slot, 2 * pair + 1] = both[slot * LANES : slot * LANES + LANES, LANES:]

    def emit(index):
        start = chunk_start(jnp.maximum(index, 0))
        low = low_ref[...]
        for v in range(16):
            turn_ref[pl.ds(v, 8, stride=16), :] = path_ref[v] - low
        done = turn_ref[...].T
        for row in range(rows):
            piece = done[row * width : (row + 1) * width]
            if has_sum:
                piece = piece + lead_ref[row, pl.ds(start, width), :]
            out_ref[row, pl.ds(start, width), :] = piece

    def advance(state, low, slot, step, current):
        col = jnp.where(forward, step, width - 1 - step)
        mask = lane_col == col
        bound = low + P_LARGE
        above = jnp.where(sublane == 7, BIG, pltpu.roll(state[0], 7, 0))
        below = jnp.where(sublane == 0, BIG, pltpu.roll(state[15], 1, 0))
        padded = [below] + list(state) + [above]
        fresh = []
        for v in range(16):
            near = jnp.minimum(padded[v], padded[v + 2]) + P_SMALL
            best = jnp.minimum(jnp.minimum(state[v], near), bound)
            value = current[slot, col, v * 8 : v * 8 + 8, :] + best
            pltpu.store(path_ref.at[v], value, mask=mask)
            fresh.append(value)
        pltpu.store(low_ref, low, mask=mask)
        return fresh

    def one_batch(number, state, current, coming, ready, filling):
        base = number * batch
        pairs = width // 2 // batch

        def one_chunk(slot, state):
            emit(base + slot - 1)
            split(base + 2 * batch + slot, filling.at[pl.ds(pl.multiple_of(slot * LANES, LANES), LANES)])
            low = lowest(state)
            state = [value - low for value in state]
            low = jnp.zeros_like(low)
            for step in range(width):
                if step % (2 * batch) == 0:
                    spread(ready, coming, slot * pairs + step // (2 * batch))
                if step:
                    low = lowest(state)
                state = advance(state, low, slot, step, current)
            return tuple(state)

        return lax.fori_loop(0, batch, one_chunk, state)

    for slot in range(batch):
        split(slot, split_a.at[pl.ds(slot * LANES, LANES)])
        split(batch + slot, split_b.at[pl.ds(slot * LANES, LANES)])

    def first(group, carry):
        for k in range(4):
            spread(split_a, even_ref, group * 4 + k)
        return carry

    lax.fori_loop(0, width // 8, first, 0)

    def two_batches(index, state):
        state = one_batch(2 * index, state, even_ref, odd_ref, split_b, split_a)
        return one_batch(2 * index + 1, state, odd_ref, even_ref, split_a, split_b)

    state = tuple(state_ref[v] for v in range(16))
    state = lax.fori_loop(0, count // batch // 2, two_batches, state)
    emit(count - 1)
    for v in range(16):
        end_ref[v] = state[v]


def row_scan(place, cost, state, lead, flip):
    rows, cols, _ = cost.shape
    width = LANES // rows
    batch = math.gcd(cols // width // 2, BATCH)
    vmem = pl.BlockSpec(memory_space=pltpu.VMEM)
    args = [place, cost, state] + ([] if lead is None else [lead])
    return pl.pallas_call(
        functools.partial(row_scan_kernel, (rows, cols, flip, batch), lead is not None),
        out_shape=(
            jax.ShapeDtypeStruct(cost.shape, jnp.float32),
            jax.ShapeDtypeStruct((16, 8, LANES), jnp.float32),
        ),
        in_specs=[pl.BlockSpec(memory_space=pltpu.SMEM)] + [vmem] * (len(args) - 1),
        out_specs=(vmem, vmem),
        scratch_shapes=[
            pltpu.VMEM((LANES, LANES), jnp.float32),
            pltpu.VMEM((LANES, LANES), jnp.float32),
            pltpu.VMEM((width // 2, 2 * LANES, 2 * LANES), jnp.bfloat16),
            pltpu.VMEM((batch * LANES, 2 * LANES), jnp.bfloat16),
            pltpu.VMEM((batch * LANES, 2 * LANES), jnp.bfloat16),
            pltpu.VMEM((batch, width, LANES, LANES), jnp.float32),
            pltpu.VMEM((batch, width, LANES, LANES), jnp.float32),
            pltpu.VMEM((16, 8, LANES), jnp.float32),
            pltpu.VMEM((8, LANES), jnp.float32),
        ],
        compiler_params=pltpu.CompilerParams(vmem_limit_bytes=20 << 20),
        cost_estimate=pl.CostEstimate(flops=2_000_000_000, bytes_accessed=30_000_000, transcendentals=0),
    )(*args)


def column_kernel(cost_ref, out_ref, sum_ref):
    length, width, _ = cost_ref.shape
    lane = lax.broadcasted_iota(jnp.int32, (width, DISP), 1)

    def step(state, index):
        cost = cost_ref[index].astype(jnp.float32)
        low = jnp.min(state, axis=1, keepdims=True)
        above = jnp.where(lane == DISP - 1, BIG, pltpu.roll(state, DISP - 1, 1))
        below = jnp.where(lane == 0, BIG, pltpu.roll(state, 1, 1))
        near = jnp.minimum(above, below) + P_SMALL
        return cost + jnp.minimum(jnp.minimum(state, near), low + P_LARGE) - low

    def first(index, states):
        down = step(states[0], index)
        up = step(states[1], length - 1 - index)
        sum_ref[index] = down
        sum_ref[length - 1 - index] = up
        return down, up

    def second(index, states):
        down = step(states[0], index)
        up = step(states[1], length - 1 - index)
        out_ref[index] = (sum_ref[index] + down).astype(jnp.bfloat16)
        out_ref[length - 1 - index] = (sum_ref[length - 1 - index] + up).astype(jnp.bfloat16)
        return down, up

    zero = jnp.zeros((width, DISP), jnp.float32)
    states = lax.fori_loop(0, length // 2, first, (zero, zero))
    lax.fori_loop(length // 2, length, second, states)


def column_scan(columns):
    vmem = pl.BlockSpec(memory_space=pltpu.VMEM)
    return pl.pallas_call(
        column_kernel,
        out_shape=jax.ShapeDtypeStruct(columns.shape, jnp.bfloat16),
        in_specs=[vmem],
        out_specs=vmem,
        scratch_shapes=[pltpu.VMEM(columns.shape, jnp.float32)],
        compiler_params=pltpu.CompilerParams(vmem_limit_bytes=12 << 20),
        cost_estimate=pl.CostEstimate(flops=200_000_000, bytes_accessed=2_000_000, transcendentals=0),
    )(columns)


def add_kernel(across_ref, down_ref, out_ref):
    cols = across_ref.shape[1]
    out_ref[0] = across_ref[0] + down_ref[...].reshape(cols, DISP).astype(jnp.float32)


def add_vertical(horizontal, vertical):
    rows, cols, _ = horizontal.shape
    groups, _, per_group, _ = vertical.shape
    if not packs(per_group):
        return horizontal + jnp.swapaxes(vertical, 0, 1).reshape(rows, cols, DISP).astype(jnp.float32)
    whole = pl.BlockSpec((1, cols, DISP), lambda row: (row, 0, 0))
    return pl.pallas_call(
        add_kernel,
        out_shape=jax.ShapeDtypeStruct(horizontal.shape, jnp.float32),
        grid=(rows,),
        in_specs=[whole, pl.BlockSpec((groups, None, per_group, DISP), lambda row: (0, row, 0, 0))],
        out_specs=whole,
        cost_estimate=pl.CostEstimate(flops=300_000, bytes_accessed=2_600_000, transcendentals=0),
    )(horizontal, vertical)


def normalize(image_pixels):
    return (image_pixels.astype(jnp.float32) / 1024.0 - 2.0).astype(jnp.bfloat16)


def weights_kernel(rows, base_ref, first_ref, wt_ref, w1_ref):
    wt_ref[...] = jnp.zeros_like(wt_ref)
    layers, taps = base_ref.shape[0], base_ref.shape[1]
    for layer in range(layers):
        for dy in range(taps):
            for dx in range(taps):
                block = base_ref[layer, dy, dx].astype(jnp.float32).T.astype(jnp.bfloat16)
                for out in range(wt_ref.shape[3] // CH):
                    top = (out + dy) * CH
                    wt_ref[layer, dx, top : top + CH, out * CH : (out + 1) * CH] = block
    shape = w1_ref.shape
    row = lax.broadcasted_iota(jnp.int32, shape, 0)
    tall = rows + 8
    dx_at, dy_at = row // tall, row % tall - lax.broadcasted_iota(jnp.int32, shape, 1) // CH
    value = jnp.zeros(shape, jnp.float32)
    for dy in range(taps):
        for dx in range(taps):
            line = first_ref[dy * taps + dx : dy * taps + dx + 1, :]
            value = jnp.where((dx_at == dx) & (dy_at == dy), line, value)
    w1_ref[...] = value.astype(jnp.bfloat16)


def banded_weights(first_weight, conv_weights, rows):
    base = jnp.transpose(conv_weights, (0, 3, 4, 1, 2))
    lines = jnp.transpose(first_weight, (1, 2, 3, 0)).reshape(9, CH).astype(jnp.float32)
    lines = jnp.tile(lines, (1, rows + 6))
    vmem = pl.BlockSpec(memory_space=pltpu.VMEM)
    return pl.pallas_call(
        functools.partial(weights_kernel, rows),
        out_shape=(
            jax.ShapeDtypeStruct((base.shape[0], 3, 6 * CH, 4 * CH), jnp.bfloat16),
            jax.ShapeDtypeStruct((LANES, (rows + 6) * CH), jnp.bfloat16),
        ),
        in_specs=[vmem, vmem],
        out_specs=(vmem, vmem),
        compiler_params=pltpu.CompilerParams(vmem_limit_bytes=12 << 20),
        cost_estimate=pl.CostEstimate(flops=10_000_000, bytes_accessed=2_500_000, transcendentals=0),
    )(base, lines)


def neighbours(pair, row_axis, strip_axis):
    groups, strips = lax.axis_size(row_axis), lax.axis_size(strip_axis)
    above = lax.ppermute(pair, row_axis, [(i, i + 1) for i in range(groups - 1)])
    below = lax.ppermute(pair, row_axis, [(i + 1, i) for i in range(groups - 1)])
    own = jnp.concatenate([above, pair, below], axis=1)
    other = lax.ppermute(own, strip_axis, [(i, i ^ 1) for i in range(strips)])
    first = lax.axis_index(strip_axis) == 0
    return jnp.concatenate([jnp.where(first, own, other), jnp.where(first, other, own)], axis=2)


def stacked(image, start, length, flipped):
    part = lax.dynamic_slice_in_dim(image, start - 1, length + 2, 1)
    if flipped:
        part = part[:, ::-1]
    shifts = [part[:, dx : dx + length] for dx in ((2, 1, 0) if flipped else (0, 1, 2))]
    joined = jnp.concatenate(shifts, axis=0)
    joined = jnp.pad(joined, ((0, LANES - joined.shape[0]), (0, 0)))
    return joined.T


def per_device(left_pixels, right_pixels, valid_mask, first_weight, conv_weights):
    rows, cols = left_pixels.shape
    groups, strips = lax.axis_size("rows"), lax.axis_size("strips")
    group, strip = lax.axis_index("rows"), lax.axis_index("strips")
    total_rows, total_cols = rows * groups, cols * strips

    wt, w1 = banded_weights(first_weight, conv_weights, rows)
    pair = jnp.stack([normalize(left_pixels), normalize(right_pixels)])
    band = neighbours(pair, "rows", "strips")[:, rows - 4 : 2 * rows + 4]
    left_length, right_length = plan(cols)[0], plan(cols + DISP)[0]
    margin = right_length + 8
    band = jnp.pad(band, ((0, 0), (0, 0), (margin, margin)))
    first_col = strip * cols
    left_stack = stacked(band[0], margin + first_col - 3 * EDGE, left_length, False)
    right_start = first_col + cols - 1 + 3 * EDGE - (right_length - 1)
    right_stack = stacked(band[1], margin + right_start, right_length, True)
    scale = -1.0 / math.sqrt(CH)
    mask = jnp.repeat((valid_mask.astype(jnp.float32) * scale).astype(jnp.bfloat16).T, CH, axis=1)
    place = jnp.stack([group * rows, first_col, strip]).astype(jnp.int32)

    per_group = cols // groups
    cost, *packed = cost_volume(
        left_stack, right_stack, mask, w1, wt, place, rows, cols, total_rows, total_cols, per_group
    )
    if packed:
        grouped = packed[0].reshape(groups, rows, per_group, DISP)
    else:
        grouped = jnp.swapaxes(cost.astype(jnp.bfloat16).reshape(rows, groups, per_group, DISP), 0, 1)
    columns = lax.all_to_all(grouped, "rows", split_axis=0, concat_axis=0, tiled=True)
    columns = columns.reshape(total_rows, per_group, DISP)

    zero = jnp.zeros((16, 8, LANES), jnp.float32)
    leading, end = row_scan(place, cost, zero, None, False)
    columns, end = lax.optimization_barrier((columns, end))
    column_sum = column_scan(columns)
    received = lax.ppermute(end, "strips", [(i, i ^ 1) for i in range(strips)])
    vertical = lax.all_to_all(
        column_sum.reshape(groups, rows, per_group, DISP), "rows", split_axis=0, concat_axis=0, tiled=True
    )
    horizontal, _ = row_scan(place, cost, received, leading, True)
    return add_vertical(horizontal, vertical)


def solution(mesh):
    in_specs = (P("rows", "strips"), P("rows", "strips"), P("rows", "strips"), P(), P())
    out_specs = P("rows", "strips", None)
    return jax.shard_map(
        per_device, mesh=mesh, in_specs=in_specs, out_specs=out_specs, check_vma=False
    )
```

```python
import functools
import math

import jax
import jax.numpy as jnp
from jax import lax
from jax.experimental import pallas as pl
from jax.experimental.pallas import tpu as pltpu
from jax.sharding import PartitionSpec as P

DISP = 128
P_SMALL = 0.5
P_LARGE = 2.0
BIG = 3.0e38
CH = 64
EDGE = 8
LANES = 128
BATCH = 2
PARTS = 1
BLOCKS = 4


def plan(width):
    unit = 16 * PARTS
    totals = [-(-width // unit) * unit]
    for _ in range(3):
        totals.append(-(-(totals[-1] + 2 * EDGE) // unit) * unit)
    return totals[::-1]


def feature_stacks(stacks, w1_ref, wt_ref, row_low, row_high):
    def inside(test, base, count, lanes, halo, lane0):
        position = lax.broadcasted_iota(jnp.int32, (count, lanes), 0) + base
        row = (lax.broadcasted_iota(jnp.int32, (count, lanes), 1) + lane0) // CH - halo
        return test(position) & (row >= row_low) & (row < row_high)

    def first(index, carry):
        for pix_ref, bufs, test, flipped in stacks:
            chunk = bufs[0].shape[0] // PARTS
            start = pl.multiple_of(index * chunk, 16)
            value = jnp.dot(pix_ref[pl.ds(start, chunk), :], w1_ref[...], preferred_element_type=jnp.float32)
            keep = inside(test, start - 3 * EDGE, chunk, bufs[0].shape[1], 3, 0)
            bufs[0][pl.ds(start, chunk), :] = jnp.where(keep, jnp.maximum(value, 0.0), 0.0).astype(jnp.bfloat16)
        return carry

    lax.fori_loop(0, PARTS, first, 0)

    for layer in range(1, 4):

        def convolve(index, carry, layer=layer):
            halo = 3 - layer
            for pix_ref, bufs, test, flipped in stacks:
                source, target = bufs[layer - 1], bufs[layer]
                out_rows = target.shape[1] // CH
                chunk = target.shape[0] // PARTS
                reach = chunk + 2 * EDGE
                start = pl.multiple_of(index * chunk, 16)
                for group in range(0, out_rows, 4):
                    count = min(4, out_rows - group)
                    wide, deep = count * CH, (count + 2) * CH
                    block = source[pl.ds(start, reach), group * CH : group * CH + deep]
                    parts = [
                        jnp.dot(block, wt_ref[layer - 1, dx, :deep, :wide], preferred_element_type=jnp.float32)
                        for dx in range(3)
                    ]
                    before, after = (parts[2], parts[0]) if flipped else (parts[0], parts[2])
                    value = pltpu.roll(before, 1, 0) + parts[1] + pltpu.roll(after, reach - 1, 0)
                    value = value[EDGE : EDGE + chunk]
                    if layer < 3:
                        value = jnp.maximum(value, 0.0)
                    keep = inside(test, start - halo * EDGE, chunk, wide, halo, group * CH)
                    value = jnp.where(keep, value, 0.0).astype(jnp.bfloat16)
                    target[pl.ds(start, chunk), group * CH : group * CH + wide] = value
            return carry

        lax.fori_loop(0, PARTS, convolve, 0)


def packs(per_group):
    return per_group % 16 == 0 and LANES % per_group == 0


def cost_kernel(dims, where_ref, left_ref, right_ref, mask_ref, w1_ref, wt_ref, cost_ref, *rest):
    rows, cols, total_rows, total_cols, per_group = dims
    payload_ref, bufs = (rest[0], rest[1:]) if len(rest) % 2 else (None, rest)
    first_row, first_col = where_ref[0], where_ref[1]
    row_low, row_high = -first_row, total_rows - first_row
    left_bufs, right_bufs = bufs[:4], bufs[4:]

    def left_col(position):
        col = position + first_col
        return (col >= 0) & (col < total_cols)

    def right_col(position):
        col = first_col + cols - 1 - position
        return (col >= 0) & (col < total_cols)

    feature_stacks(
        [(left_ref, left_bufs, left_col, False), (right_ref, right_bufs, right_col, True)],
        w1_ref, wt_ref, row_low, row_high,
    )
    left, right = left_bufs[3], right_bufs[3]
    for row in range(rows):
        pair = row // 2 * LANES
        lane = lax.broadcasted_iota(jnp.int32, (LANES, LANES), 1)
        own = (lane // CH) == row % 2

        def block(index, carry, pair=pair, own=own, row=row):
            start = pl.multiple_of(index * LANES, LANES)
            window = pl.multiple_of(cols - LANES - start, LANES)
            scale = mask_ref[pl.ds(start, LANES), pair : pair + LANES]
            a = jnp.where(own, left[pl.ds(start, LANES), pair : pair + LANES] * scale, jnp.zeros((), jnp.bfloat16))
            b = right[pl.ds(window, 2 * LANES), pair : pair + LANES]
            product = lax.dot_general(a, b, (((1,), (1,)), ((), ())), preferred_element_type=jnp.float32)
            skewed = pltpu.roll(product, LANES + 1, 1, stride=1, stride_axis=0)
            skewed = skewed[:, :LANES]
            cost_ref[row, pl.ds(start, LANES), :] = skewed
            if payload_ref is not None:
                skewed = skewed - jnp.mean(skewed, axis=1, keepdims=True)
                for k in range(LANES // per_group):
                    piece = skewed[k * per_group : (k + 1) * per_group].astype(jnp.bfloat16)
                    group = index * (LANES // per_group) + k
                    payload_ref[group, row * per_group : (row + 1) * per_group, :] = piece
            return carry

        lax.fori_loop(0, cols // LANES, block, 0, unroll=BLOCKS)


def cost_volume(left_stack, right_stack, mask, w1, wt, place, rows, cols, total_rows, total_cols, per_group):
    bufs = []
    for width in (cols, cols + DISP):
        sizes = plan(width)
        for layer in range(4):
            out_rows = rows + 2 * (3 - layer)
            length = sizes[layer]
            bufs.append(pltpu.VMEM((length, out_rows * CH), jnp.bfloat16))
    vmem = pl.BlockSpec(memory_space=pltpu.VMEM)
    shapes = [jax.ShapeDtypeStruct((rows, cols, DISP), jnp.float32)]
    if packs(per_group):
        shapes.append(jax.ShapeDtypeStruct((cols // per_group, rows * per_group, DISP), jnp.bfloat16))
    return pl.pallas_call(
        functools.partial(cost_kernel, (rows, cols, total_rows, total_cols, per_group)),
        out_shape=tuple(shapes),
        in_specs=[pl.BlockSpec(memory_space=pltpu.SMEM)] + [vmem] * 5,
        out_specs=(vmem,) * len(shapes),
        scratch_shapes=bufs,
        compiler_params=pltpu.CompilerParams(vmem_limit_bytes=40 << 20),
        cost_estimate=pl.CostEstimate(flops=8_000_000_000, bytes_accessed=6_000_000, transcendentals=0),
    )(place, left_stack, right_stack, mask, w1, wt)


def row_scan_kernel(dims, has_sum, place_ref, cost_ref, state_ref, *rest):
    rows, cols, flip, batch = dims
    if has_sum:
        lead_ref, rest = rest[0], rest[1:]
    out_ref, end_ref, tile_ref, turn_ref, pick_ref, split_a, split_b, even_ref, odd_ref, path_ref, low_ref = rest
    width = LANES // rows
    count = cols // width
    forward = place_ref[2] == (1 if flip else 0)
    lane = lax.broadcasted_iota(jnp.int32, (8, LANES), 1)
    sublane = lax.broadcasted_iota(jnp.int32, (8, LANES), 0)
    lane_col = lane % width

    def build_pick(pair, carry):
        k = lax.broadcasted_iota(jnp.int32, (2 * LANES, 2 * LANES), 0) % LANES
        n = lax.broadcasted_iota(jnp.int32, (2 * LANES, 2 * LANES), 1)
        wanted = n % LANES // width * width + 2 * pair + n // LANES
        pick_ref[pair] = jnp.where(k == wanted, 1.0, 0.0).astype(jnp.bfloat16)
        return carry

    lax.fori_loop(0, width // 2, build_pick, 0)

    def chunk_start(index):
        chunk = jnp.where(forward, index, count - 1 - index)
        return pl.multiple_of(chunk * width, width)

    def split(index, target):
        start = chunk_start(jnp.minimum(index, count - 1))
        tile = jnp.concatenate([cost_ref[row, pl.ds(start, width), :] for row in range(rows)], axis=0)
        tile_ref[...] = tile.T
        for v in range(0, 16, 2):
            plane = jnp.concatenate(
                [tile_ref[pl.ds(v, 8, stride=16), :], tile_ref[pl.ds(v + 1, 8, stride=16), :]], axis=0
            )
            high = plane.astype(jnp.bfloat16)
            low = (plane - high.astype(jnp.float32)).astype(jnp.bfloat16)
            target[v * 8 : v * 8 + 16, :LANES] = high
            target[v * 8 : v * 8 + 16, LANES:] = low

    def spread(source, target, pair):
        both = jnp.dot(source[...], pick_ref[pair], preferred_element_type=jnp.float32)
        for slot in range(batch):
            target[slot, 2 * pair] = both[slot * LANES : slot * LANES + LANES, :LANES]
            target[slot, 2 * pair + 1] = both[slot * LANES : slot * LANES + LANES, LANES:]

    def emit(index):
        start = chunk_start(jnp.maximum(index, 0))
        low = low_ref[...]
        for v in range(16):
            turn_ref[pl.ds(v, 8, stride=16), :] = path_ref[v] - low
        done = turn_ref[...].T
        for row in range(rows):
            piece = done[row * width : (row + 1) * width]
            if has_sum:
                offset = jnp.mean(cost_ref[row, pl.ds(start, width), :], axis=1, keepdims=True)
                piece = piece + (lead_ref[row, pl.ds(start, width), :] + 2.0 * offset)
            out_ref[row, pl.ds(start, width), :] = piece

    def advance(state, low, slot, step, current):
        col = jnp.where(forward, step, width - 1 - step)
        mask = lane_col == col
        bound = low + P_LARGE
        above = jnp.where(sublane == 7, BIG, pltpu.roll(state[0], 7, 0))
        below = jnp.where(sublane == 0, BIG, pltpu.roll(state[15], 1, 0))
        padded = [below] + list(state) + [above]
        fresh = []
        for v in range(16):
            near = jnp.minimum(padded[v], padded[v + 2]) + P_SMALL
            best = jnp.minimum(jnp.minimum(state[v], near), bound)
            value = current[slot, col, v * 8 : v * 8 + 8, :] + best
            pltpu.store(path_ref.at[v], value, mask=mask)
            fresh.append(value)
        pltpu.store(low_ref, low, mask=mask)
        return fresh

    def one_batch(number, state, current, coming, ready, filling):
        base = number * batch
        pairs = width // 2 // batch

        def one_chunk(slot, state):
            emit(base + slot - 1)
            split(base + 2 * batch + slot, filling.at[pl.ds(pl.multiple_of(slot * LANES, LANES), LANES)])
            low = lowest(state)
            state = [value - low for value in state]
            low = jnp.zeros_like(low)
            for step in range(width):
                if step % (2 * batch) == 0:
                    spread(ready, coming, slot * pairs + step // (2 * batch))
                if step:
                    low = lowest(state)
                state = advance(state, low, slot, step, current)
            return tuple(state)

        return lax.fori_loop(0, batch, one_chunk, state)

    for slot in range(batch):
        split(slot, split_a.at[pl.ds(slot * LANES, LANES)])
        split(batch + slot, split_b.at[pl.ds(slot * LANES, LANES)])

    def first(group, carry):
        for k in range(4):
            spread(split_a, even_ref, group * 4 + k)
        return carry

    lax.fori_loop(0, width // 8, first, 0)

    def two_batches(index, state):
        state = one_batch(2 * index, state, even_ref, odd_ref, split_b, split_a)
        return one_batch(2 * index + 1, state, odd_ref, even_ref, split_a, split_b)

    state = tuple(state_ref[v] for v in range(16))
    state = lax.fori_loop(0, count // batch // 2, two_batches, state)
    emit(count - 1)
    for v in range(16):
        end_ref[v] = state[v]


def row_scan(place, cost, state, lead, flip):
    rows, cols, _ = cost.shape
    width = LANES // rows
    batch = math.gcd(cols // width // 2, BATCH)
    vmem = pl.BlockSpec(memory_space=pltpu.VMEM)
    args = [place, cost, state] + ([] if lead is None else [lead])
    return pl.pallas_call(
        functools.partial(row_scan_kernel, (rows, cols, flip, batch), lead is not None),
        out_shape=(
            jax.ShapeDtypeStruct(cost.shape, jnp.float32),
            jax.ShapeDtypeStruct((16, 8, LANES), jnp.float32),
        ),
        in_specs=[pl.BlockSpec(memory_space=pltpu.SMEM)] + [vmem] * (len(args) - 1),
        out_specs=(vmem, vmem),
        scratch_shapes=[
            pltpu.VMEM((LANES, LANES), jnp.float32),
            pltpu.VMEM((LANES, LANES), jnp.float32),
            pltpu.VMEM((width // 2, 2 * LANES, 2 * LANES), jnp.bfloat16),
            pltpu.VMEM((batch * LANES, 2 * LANES), jnp.bfloat16),
            pltpu.VMEM((batch * LANES, 2 * LANES), jnp.bfloat16),
            pltpu.VMEM((batch, width, LANES, LANES), jnp.float32),
            pltpu.VMEM((batch, width, LANES, LANES), jnp.float32),
            pltpu.VMEM((16, 8, LANES), jnp.float32),
            pltpu.VMEM((8, LANES), jnp.float32),
        ],
        compiler_params=pltpu.CompilerParams(vmem_limit_bytes=20 << 20),
        cost_estimate=pl.CostEstimate(flops=2_000_000_000, bytes_accessed=30_000_000, transcendentals=0),
    )(*args)


def column_kernel(cost_ref, out_ref, sum_ref):
    length, width, _ = cost_ref.shape
    lane = lax.broadcasted_iota(jnp.int32, (width, DISP), 1)

    def step(state, index):
        cost = cost_ref[index].astype(jnp.float32)
        low = jnp.min(state, axis=1, keepdims=True)
        above = jnp.where(lane == DISP - 1, BIG, pltpu.roll(state, DISP - 1, 1))
        below = jnp.where(lane == 0, BIG, pltpu.roll(state, 1, 1))
        near = jnp.minimum(above, below) + P_SMALL
        return cost + jnp.minimum(jnp.minimum(state, near), low + P_LARGE) - low

    def first(index, states):
        down = step(states[0], index)
        up = step(states[1], length - 1 - index)
        sum_ref[index] = down
        sum_ref[length - 1 - index] = up
        return down, up

    def second(index, states):
        down = step(states[0], index)
        up = step(states[1], length - 1 - index)
        out_ref[index] = (sum_ref[index] + down).astype(jnp.bfloat16)
        out_ref[length - 1 - index] = (sum_ref[length - 1 - index] + up).astype(jnp.bfloat16)
        return down, up

    zero = jnp.zeros((width, DISP), jnp.float32)
    states = lax.fori_loop(0, length // 2, first, (zero, zero))
    lax.fori_loop(length // 2, length, second, states)


def lowest(state):
    level = list(state)
    while len(level) > 1:
        level = [jnp.minimum(level[i], level[i + 1]) for i in range(0, len(level), 2)]
    low = level[0]
    for shift in (4, 2, 1):
        low = jnp.minimum(low, pltpu.roll(low, shift, 0))
    return low


def column_tiles_kernel(cost_ref, out_ref, tile_ref, split_ref, spread_ref, path_ref, turn_ref, sum_ref):
    length, width, _ = cost_ref.shape
    both = 2 * width
    per = LANES // both
    tiles = length // per
    sublane = lax.broadcasted_iota(jnp.int32, (8, LANES), 0)
    lane_step = lax.broadcasted_iota(jnp.int32, (8, LANES), 1) // both
    k = lax.broadcasted_iota(jnp.int32, (LANES, per * LANES), 0)
    n = lax.broadcasted_iota(jnp.int32, (LANES, per * LANES), 1)
    pick = jnp.where(k == n // LANES * both + n % both, 1.0, 0.0).astype(jnp.bfloat16)

    def places(tile):
        rows = []
        for step in range(per):
            rows += [tile * per + step, length - 1 - (tile * per + step)]
        return rows

    def prepare(index, carry):
        for slot in range(8):
            tile = index * 8 + slot
            block = jnp.concatenate([cost_ref[row] for row in places(tile)], axis=0)
            tile_ref[slot] = block.astype(jnp.float32).T
            for v in range(0, 16, 2):
                plane = jnp.concatenate(
                    [tile_ref[slot, pl.ds(v, 8, stride=16), :], tile_ref[slot, pl.ds(v + 1, 8, stride=16), :]], axis=0
                )
                split_ref[slot * LANES + v * 8 : slot * LANES + v * 8 + 16, :] = plane.astype(jnp.bfloat16)
        spread = jnp.dot(split_ref[...], pick, preferred_element_type=jnp.float32)
        for slot in range(8):
            for step in range(per):
                spread_ref[index * 8 + slot, step] = spread[
                    slot * LANES : slot * LANES + LANES, step * LANES : step * LANES + LANES
                ]
        return carry

    lax.fori_loop(0, tiles // 8, prepare, 0)

    def emit(tile, last):
        tile = jnp.maximum(tile, 0)
        for v in range(16):
            turn_ref[pl.ds(v, 8, stride=16), :] = path_ref[v]
        done = turn_ref[...].T
        for i, row in enumerate(places(tile)):
            piece = done[i * width : (i + 1) * width]
            if last:
                out_ref[row] = (sum_ref[row] + piece).astype(jnp.bfloat16)
            else:
                sum_ref[row] = piece

    def run(tile, state, last):
        emit(tile - 1, last)
        state = list(state)
        for step in range(per):
            low = lowest(state)
            bound = low + P_LARGE
            above = jnp.where(sublane == 7, BIG, pltpu.roll(state[0], 7, 0))
            below = jnp.where(sublane == 0, BIG, pltpu.roll(state[15], 1, 0))
            padded = [below] + state + [above]
            fresh = []
            for v in range(16):
                near = jnp.minimum(padded[v], padded[v + 2]) + P_SMALL
                best = jnp.minimum(jnp.minimum(state[v], near), bound)
                value = spread_ref[tile, step, v * 8 : v * 8 + 8, :] + (best - low)
                if step:
                    pltpu.store(path_ref.at[v], value, mask=lane_step == step)
                else:
                    path_ref[v] = value
                fresh.append(value)
            state = fresh
        return tuple(state)

    def loop(begin, end, state, last):
        return lax.fori_loop(begin, end, lambda tile, carry: run(tile, carry, last), state, unroll=8)

    state = (jnp.zeros((8, LANES), jnp.float32),) * 16
    state = loop(0, tiles // 2, state, False)
    emit(tiles // 2 - 1, False)
    state = loop(tiles // 2, tiles, state, True)
    emit(tiles - 1, True)


def column_scan(columns):
    length, width, _ = columns.shape
    vmem = pl.BlockSpec(memory_space=pltpu.VMEM)
    scratch = [pltpu.VMEM(columns.shape, jnp.float32)]
    kernel = column_kernel
    per = LANES // (2 * width)
    if width % 16 == 0 and LANES % (2 * width) == 0 and length % (16 * per) == 0:
        kernel = column_tiles_kernel
        scratch = [
            pltpu.VMEM((8, LANES, LANES), jnp.float32),
            pltpu.VMEM((8 * LANES, LANES), jnp.bfloat16),
            pltpu.VMEM((length // per, per, LANES, LANES), jnp.float32),
            pltpu.VMEM((16, 8, LANES), jnp.float32),
            pltpu.VMEM((LANES, LANES), jnp.float32),
        ] + scratch
    return pl.pallas_call(
        kernel,
        out_shape=jax.ShapeDtypeStruct(columns.shape, jnp.bfloat16),
        in_specs=[vmem],
        out_specs=vmem,
        scratch_shapes=scratch,
        compiler_params=pltpu.CompilerParams(vmem_limit_bytes=20 << 20),
        cost_estimate=pl.CostEstimate(flops=200_000_000, bytes_accessed=2_000_000, transcendentals=0),
    )(columns)


def add_kernel(across_ref, down_ref, out_ref):
    rows, cols, _ = across_ref.shape
    for row in range(rows):
        out_ref[row] = across_ref[row] + down_ref[:, row].reshape(cols, DISP).astype(jnp.float32)


def add_vertical(horizontal, vertical):
    rows, cols, _ = horizontal.shape
    if not packs(vertical.shape[2]):
        return horizontal + jnp.swapaxes(vertical, 0, 1).reshape(rows, cols, DISP).astype(jnp.float32)
    vmem = pl.BlockSpec(memory_space=pltpu.VMEM)
    return pl.pallas_call(
        add_kernel,
        out_shape=jax.ShapeDtypeStruct(horizontal.shape, jnp.float32),
        in_specs=[vmem, vmem],
        out_specs=vmem,
        compiler_params=pltpu.CompilerParams(vmem_limit_bytes=8 << 20),
        cost_estimate=pl.CostEstimate(flops=300_000, bytes_accessed=2_600_000, transcendentals=0),
    )(horizontal, vertical)


def normalize(image_pixels):
    return (image_pixels.astype(jnp.float32) / 1024.0 - 2.0).astype(jnp.bfloat16)


def weights_kernel(rows, base_ref, first_ref, wt_ref, w1_ref):
    wt_ref[...] = jnp.zeros_like(wt_ref)
    layers, taps = base_ref.shape[0], base_ref.shape[1]
    for layer in range(layers):
        for dy in range(taps):
            for dx in range(taps):
                block = base_ref[layer, dy, dx].astype(jnp.float32).T.astype(jnp.bfloat16)
                for out in range(wt_ref.shape[3] // CH):
                    top = (out + dy) * CH
                    wt_ref[layer, dx, top : top + CH, out * CH : (out + 1) * CH] = block
    shape = w1_ref.shape
    row = lax.broadcasted_iota(jnp.int32, shape, 0)
    tall = rows + 8
    dx_at, dy_at = row // tall, row % tall - lax.broadcasted_iota(jnp.int32, shape, 1) // CH
    value = jnp.zeros(shape, jnp.float32)
    for dy in range(taps):
        for dx in range(taps):
            line = first_ref[dy * taps + dx : dy * taps + dx + 1, :]
            value = jnp.where((dx_at == dx) & (dy_at == dy), line, value)
    w1_ref[...] = value.astype(jnp.bfloat16)


def banded_weights(first_weight, conv_weights, rows):
    base = jnp.transpose(conv_weights, (0, 3, 4, 1, 2))
    lines = jnp.transpose(first_weight, (1, 2, 3, 0)).reshape(9, CH).astype(jnp.float32)
    lines = jnp.tile(lines, (1, rows + 6))
    vmem = pl.BlockSpec(memory_space=pltpu.VMEM)
    return pl.pallas_call(
        functools.partial(weights_kernel, rows),
        out_shape=(
            jax.ShapeDtypeStruct((base.shape[0], 3, 6 * CH, 4 * CH), jnp.bfloat16),
            jax.ShapeDtypeStruct((LANES, (rows + 6) * CH), jnp.bfloat16),
        ),
        in_specs=[vmem, vmem],
        out_specs=(vmem, vmem),
        compiler_params=pltpu.CompilerParams(vmem_limit_bytes=12 << 20),
        cost_estimate=pl.CostEstimate(flops=10_000_000, bytes_accessed=2_500_000, transcendentals=0),
    )(base, lines)


def neighbours(pair, weights, row_axis, strip_axis):
    groups, strips = lax.axis_size(row_axis), lax.axis_size(strip_axis)
    above = lax.ppermute(pair, row_axis, [(i, i + 1) for i in range(groups - 1)])
    below = lax.ppermute(pair, row_axis, [(i + 1, i) for i in range(groups - 1)])
    above, below, weights = lax.optimization_barrier((above, below, weights))
    own = jnp.concatenate([above, pair, below], axis=1)
    other = lax.ppermute(own, strip_axis, [(i, i ^ 1) for i in range(strips)])
    first = lax.axis_index(strip_axis) == 0
    return jnp.concatenate([jnp.where(first, own, other), jnp.where(first, other, own)], axis=2), weights


def stacked(image, start, length, flipped):
    part = lax.dynamic_slice_in_dim(image, start - 1, length + 2, 1)
    if flipped:
        part = lax.optimization_barrier(part[:, ::-1])
    shifts = [part[:, dx : dx + length] for dx in ((2, 1, 0) if flipped else (0, 1, 2))]
    joined = jnp.concatenate(shifts, axis=0)
    joined = jnp.pad(joined, ((0, LANES - joined.shape[0]), (0, 0)))
    return joined.T


def per_device(left_pixels, right_pixels, valid_mask, first_weight, conv_weights):
    rows, cols = left_pixels.shape
    groups, strips = lax.axis_size("rows"), lax.axis_size("strips")
    group, strip = lax.axis_index("rows"), lax.axis_index("strips")
    total_rows, total_cols = rows * groups, cols * strips

    wt, w1 = banded_weights(first_weight, conv_weights, rows)
    pair = jnp.stack([normalize(left_pixels), normalize(right_pixels)])
    band, (wt, w1) = neighbours(pair, (wt, w1), "rows", "strips")
    band = band[:, rows - 4 : 2 * rows + 4]
    left_length, right_length = plan(cols)[0], plan(cols + DISP)[0]
    margin = right_length + 8
    band = jnp.pad(band, ((0, 0), (0, 0), (margin, margin)))
    first_col = strip * cols
    left_stack = stacked(band[0], margin + first_col - 3 * EDGE, left_length, False)
    right_start = first_col + cols - 1 + 3 * EDGE - (right_length - 1)
    right_stack = stacked(band[1], margin + right_start, right_length, True)
    scale = -1.0 / math.sqrt(CH)
    mask = jnp.repeat((valid_mask.astype(jnp.float32) * scale).astype(jnp.bfloat16).T, CH, axis=1)
    place = jnp.stack([group * rows, first_col, strip]).astype(jnp.int32)

    per_group = cols // groups
    cost, *packed = cost_volume(
        left_stack, right_stack, mask, w1, wt, place, rows, cols, total_rows, total_cols, per_group
    )
    if packed:
        grouped = packed[0].reshape(groups, rows, per_group, DISP)
    else:
        centred = (cost - jnp.mean(cost, axis=2, keepdims=True)).astype(jnp.bfloat16)
        grouped = jnp.swapaxes(centred.reshape(rows, groups, per_group, DISP), 0, 1)
    columns = lax.all_to_all(grouped, "rows", split_axis=0, concat_axis=0, tiled=True)
    columns = columns.reshape(total_rows, per_group, DISP)

    zero = jnp.zeros((16, 8, LANES), jnp.float32)
    leading, end = row_scan(place, cost, zero, None, False)
    columns, end = lax.optimization_barrier((columns, end))
    column_sum = column_scan(columns)
    received = lax.ppermute(end, "strips", [(i, i ^ 1) for i in range(strips)])
    vertical = lax.all_to_all(
        column_sum.reshape(groups, rows, per_group, DISP), "rows", split_axis=0, concat_axis=0, tiled=True
    )
    horizontal, _ = row_scan(place, cost, received, leading, True)
    return add_vertical(horizontal, vertical)


def solution(mesh):
    in_specs = (P("rows", "strips"), P("rows", "strips"), P("rows", "strips"), P(), P())
    out_specs = P("rows", "strips", None)
    return jax.shard_map(
        per_device, mesh=mesh, in_specs=in_specs, out_specs=out_specs, check_vma=False
    )
```

```python
import functools
import math

import jax
import jax.numpy as jnp
from jax import lax
from jax.experimental import pallas as pl
from jax.experimental.pallas import tpu as pltpu
from jax.sharding import PartitionSpec as P

DISP = 128
P_SMALL = 0.5
P_LARGE = 2.0
BIG = 3.0e38
CH = 64
EDGE = 8
LANES = 128
BATCH = 2
PARTS = 1
BLOCKS = 4


def plan(width):
    unit = 16 * PARTS
    totals = [-(-width // unit) * unit]
    for _ in range(3):
        totals.append(-(-(totals[-1] + 2 * EDGE) // unit) * unit)
    return totals[::-1]


def feature_stacks(stacks, w1_ref, wt_ref, row_low, row_high):
    def inside(test, base, count, lanes, halo, lane0):
        position = lax.broadcasted_iota(jnp.int32, (count, lanes), 0) + base
        row = (lax.broadcasted_iota(jnp.int32, (count, lanes), 1) + lane0) // CH - halo
        return test(position) & (row >= row_low) & (row < row_high)

    def first(index, carry):
        for pix_ref, bufs, test, flipped in stacks:
            chunk = bufs[0].shape[0] // PARTS
            start = pl.multiple_of(index * chunk, 16)
            value = jnp.dot(pix_ref[pl.ds(start, chunk), :], w1_ref[...], preferred_element_type=jnp.float32)
            keep = inside(test, start - 3 * EDGE, chunk, bufs[0].shape[1], 3, 0)
            bufs[0][pl.ds(start, chunk), :] = jnp.where(keep, jnp.maximum(value, 0.0), 0.0).astype(jnp.bfloat16)
        return carry

    lax.fori_loop(0, PARTS, first, 0)

    for layer in range(1, 4):

        def convolve(index, carry, layer=layer):
            halo = 3 - layer
            for pix_ref, bufs, test, flipped in stacks:
                source, target = bufs[layer - 1], bufs[layer]
                out_rows = target.shape[1] // CH
                chunk = target.shape[0] // PARTS
                reach = chunk + 2 * EDGE
                start = pl.multiple_of(index * chunk, 16)
                for group in range(0, out_rows, 4):
                    count = min(4, out_rows - group)
                    wide, deep = count * CH, (count + 2) * CH
                    block = source[pl.ds(start, reach), group * CH : group * CH + deep]
                    parts = [
                        jnp.dot(block, wt_ref[layer - 1, dx, :deep, :wide], preferred_element_type=jnp.float32)
                        for dx in range(3)
                    ]
                    before, after = (parts[2], parts[0]) if flipped else (parts[0], parts[2])
                    value = pltpu.roll(before, 1, 0) + parts[1] + pltpu.roll(after, reach - 1, 0)
                    value = value[EDGE : EDGE + chunk]
                    if layer < 3:
                        value = jnp.maximum(value, 0.0)
                    keep = inside(test, start - halo * EDGE, chunk, wide, halo, group * CH)
                    value = jnp.where(keep, value, 0.0).astype(jnp.bfloat16)
                    target[pl.ds(start, chunk), group * CH : group * CH + wide] = value
            return carry

        lax.fori_loop(0, PARTS, convolve, 0)


def offsets(costs):
    even = jnp.full((DISP, DISP), 1.0 / DISP, jnp.bfloat16)
    return jnp.dot(costs.astype(jnp.bfloat16), even, preferred_element_type=jnp.float32)


def packs(per_group):
    return per_group % 16 == 0 and LANES % per_group == 0


def cost_kernel(dims, where_ref, left_ref, right_ref, mask_ref, w1_ref, wt_ref, out_ref, *rest):
    rows, cols, total_rows, total_cols, per_group = dims
    payload_ref, rest = (rest[0], rest[1:]) if packs(per_group) else (None, rest)
    cost_ref, sems, *bufs = rest
    first_row, first_col = where_ref[0], where_ref[1]
    row_low, row_high = -first_row, total_rows - first_row
    left_bufs, right_bufs = bufs[:4], bufs[4:]

    def left_col(position):
        col = position + first_col
        return (col >= 0) & (col < total_cols)

    def right_col(position):
        col = first_col + cols - 1 - position
        return (col >= 0) & (col < total_cols)

    feature_stacks(
        [(left_ref, left_bufs, left_col, False), (right_ref, right_bufs, right_col, True)],
        w1_ref, wt_ref, row_low, row_high,
    )
    left, right = left_bufs[3], right_bufs[3]
    for row in range(rows):
        pair = row // 2 * LANES
        lane = lax.broadcasted_iota(jnp.int32, (LANES, LANES), 1)
        own = (lane // CH) == row % 2

        def block(index, carry, pair=pair, own=own, row=row):
            start = pl.multiple_of(index * LANES, LANES)
            window = pl.multiple_of(cols - LANES - start, LANES)
            scale = mask_ref[pl.ds(start, LANES), pair : pair + LANES]
            a = jnp.where(own, left[pl.ds(start, LANES), pair : pair + LANES] * scale, jnp.zeros((), jnp.bfloat16))
            b = right[pl.ds(window, 2 * LANES), pair : pair + LANES]
            product = lax.dot_general(a, b, (((1,), (1,)), ((), ())), preferred_element_type=jnp.float32)
            skewed = pltpu.roll(product, LANES + 1, 1, stride=1, stride_axis=0)
            skewed = skewed[:, :LANES]
            cost_ref[row, pl.ds(start, LANES), :] = skewed
            if payload_ref is not None:
                skewed = skewed - offsets(skewed)
                for k in range(LANES // per_group):
                    piece = skewed[k * per_group : (k + 1) * per_group].astype(jnp.bfloat16)
                    group = index * (LANES // per_group) + k
                    payload_ref[group, row * per_group : (row + 1) * per_group, :] = piece
            return carry

        lax.fori_loop(0, cols // LANES, block, 0, unroll=BLOCKS)
        pltpu.make_async_copy(cost_ref.at[row], out_ref.at[row], sems.at[row]).start()
    for row in range(rows):
        pltpu.make_async_copy(cost_ref.at[row], out_ref.at[row], sems.at[row]).wait()


def cost_volume(left_stack, right_stack, mask, w1, wt, place, rows, cols, total_rows, total_cols, per_group):
    bufs = [pltpu.VMEM((rows, cols, DISP), jnp.float32), pltpu.SemaphoreType.DMA((rows,))]
    for width in (cols, cols + DISP):
        sizes = plan(width)
        for layer in range(4):
            out_rows = rows + 2 * (3 - layer)
            length = sizes[layer]
            bufs.append(pltpu.VMEM((length, out_rows * CH), jnp.bfloat16))
    vmem = pl.BlockSpec(memory_space=pltpu.VMEM)
    shapes = [jax.ShapeDtypeStruct((rows, cols, DISP), jnp.float32)]
    if packs(per_group):
        shapes.append(jax.ShapeDtypeStruct((cols // per_group, rows * per_group, DISP), jnp.bfloat16))
    return pl.pallas_call(
        functools.partial(cost_kernel, (rows, cols, total_rows, total_cols, per_group)),
        out_shape=tuple(shapes),
        in_specs=[pl.BlockSpec(memory_space=pltpu.SMEM)] + [vmem] * 5,
        out_specs=(pl.BlockSpec(memory_space=pltpu.HBM), vmem)[: len(shapes)],
        scratch_shapes=bufs,
        compiler_params=pltpu.CompilerParams(vmem_limit_bytes=40 << 20),
        cost_estimate=pl.CostEstimate(flops=8_000_000_000, bytes_accessed=6_000_000, transcendentals=0),
    )(place, left_stack, right_stack, mask, w1, wt)


def row_scan_kernel(dims, has_sum, place_ref, cost_hbm, state_ref, *rest):
    rows, cols, flip, batch = dims
    if has_sum:
        lead_hbm, out_ref, end_ref, lead_ref, lead_sem, *rest = rest
    else:
        out_hbm, end_ref, out_ref, out_sems, *rest = rest
    cost_ref, cost_sems, tile_ref, turn_ref, pick_ref, split_a, split_b, even_ref, odd_ref, path_ref, low_ref = rest
    width = LANES // rows
    count = cols // width
    forward = place_ref[2] == (1 if flip else 0)
    lane = lax.broadcasted_iota(jnp.int32, (8, LANES), 1)
    sublane = lax.broadcasted_iota(jnp.int32, (8, LANES), 0)
    lane_col = lane % width

    def copy_in(index):
        part = pl.ds(chunk_start(index), width)
        return pltpu.make_async_copy(cost_hbm.at[:, part], cost_ref.at[:, part], cost_sems.at[index])

    rounds = count // batch // 2
    early = max(rounds // 2 * 2 * batch - 1, 0)

    def copy_out(part):
        length = (early, count - early)[part] * width
        begin = jnp.where(forward, (0, early * width)[part], ((count - early) * width, 0)[part])
        cut = pl.ds(pl.multiple_of(begin, width), length)
        return pltpu.make_async_copy(out_ref.at[:, cut], out_hbm.at[:, cut], out_sems.at[part])

    def chunk_start(index):
        chunk = jnp.where(forward, index, count - 1 - index)
        return pl.multiple_of(chunk * width, width)

    for index in range(count):
        copy_in(index).start()
    if has_sum:
        copy_lead = pltpu.make_async_copy(lead_hbm, lead_ref, lead_sem)
        copy_lead.start()

    def build_pick(pair, carry):
        k = lax.broadcasted_iota(jnp.int32, (2 * LANES, 2 * LANES), 0) % LANES
        n = lax.broadcasted_iota(jnp.int32, (2 * LANES, 2 * LANES), 1)
        wanted = n % LANES // width * width + 2 * pair + n // LANES
        pick_ref[pair] = jnp.where(k == wanted, 1.0, 0.0).astype(jnp.bfloat16)
        return carry

    lax.fori_loop(0, width // 2, build_pick, 0)

    def split(index, target):
        start = chunk_start(jnp.minimum(index, count - 1))
        tile = jnp.concatenate([cost_ref[row, pl.ds(start, width), :] for row in range(rows)], axis=0)
        tile_ref[...] = tile.T
        for v in range(0, 16, 2):
            plane = jnp.concatenate(
                [tile_ref[pl.ds(v, 8, stride=16), :], tile_ref[pl.ds(v + 1, 8, stride=16), :]], axis=0
            )
            high = plane.astype(jnp.bfloat16)
            low = (plane - high.astype(jnp.float32)).astype(jnp.bfloat16)
            target[v * 8 : v * 8 + 16, :LANES] = high
            target[v * 8 : v * 8 + 16, LANES:] = low

    def spread(source, target, pair):
        both = jnp.dot(source[...], pick_ref[pair], preferred_element_type=jnp.float32)
        for slot in range(batch):
            target[slot, 2 * pair] = both[slot * LANES : slot * LANES + LANES, :LANES]
            target[slot, 2 * pair + 1] = both[slot * LANES : slot * LANES + LANES, LANES:]

    def emit(index):
        start = chunk_start(jnp.maximum(index, 0))
        low = low_ref[...]
        for v in range(16):
            turn_ref[pl.ds(v, 8, stride=16), :] = path_ref[v] - low
        done = turn_ref[...].T
        if has_sum:
            tile = jnp.concatenate([cost_ref[row, pl.ds(start, width), :] for row in range(rows)], axis=0)
            done = done + 2.0 * offsets(tile)
        for row in range(rows):
            piece = done[row * width : (row + 1) * width]
            if has_sum:
                piece = piece + lead_ref[row, pl.ds(start, width), :]
            out_ref[row, pl.ds(start, width), :] = piece

    def advance(state, low, slot, step, current):
        col = jnp.where(forward, step, width - 1 - step)
        mask = lane_col == col
        bound = low + P_LARGE
        above = jnp.where(sublane == 7, BIG, pltpu.roll(state[0], 7, 0))
        below = jnp.where(sublane == 0, BIG, pltpu.roll(state[15], 1, 0))
        padded = [below] + list(state) + [above]
        fresh = []
        for v in range(16):
            near = jnp.minimum(padded[v], padded[v + 2]) + P_SMALL
            best = jnp.minimum(jnp.minimum(state[v], near), bound)
            value = current[slot, col, v * 8 : v * 8 + 8, :] + best
            pltpu.store(path_ref.at[v], value, mask=mask)
            fresh.append(value)
        pltpu.store(low_ref, low, mask=mask)
        return fresh

    def one_batch(number, state, current, coming, ready, filling):
        base = number * batch
        pairs = width // 2 // batch

        def one_chunk(slot, state):
            emit(base + slot - 1)
            split(base + 2 * batch + slot, filling.at[pl.ds(pl.multiple_of(slot * LANES, LANES), LANES)])
            low = lowest(state)
            state = [value - low for value in state]
            low = jnp.zeros_like(low)
            for step in range(width):
                if step % (2 * batch) == 0:
                    spread(ready, coming, slot * pairs + step // (2 * batch))
                if step:
                    low = lowest(state)
                state = advance(state, low, slot, step, current)
            return tuple(state)

        return lax.fori_loop(0, batch, one_chunk, state)

    for index in range(2 * batch):
        copy_in(index).wait()
    for slot in range(batch):
        split(slot, split_a.at[pl.ds(slot * LANES, LANES)])
        split(batch + slot, split_b.at[pl.ds(slot * LANES, LANES)])

    def first(group, carry):
        for k in range(4):
            spread(split_a, even_ref, group * 4 + k)
        return carry

    lax.fori_loop(0, width // 8, first, 0)

    for index in range(2 * batch, count):
        copy_in(index).wait()
    if has_sum:
        copy_lead.wait()

    def two_batches(index, state):
        state = one_batch(2 * index, state, even_ref, odd_ref, split_b, split_a)
        state = one_batch(2 * index + 1, state, odd_ref, even_ref, split_a, split_b)
        if not has_sum and early:

            @pl.when(index == rounds // 2 - 1)
            def _():
                copy_out(0).start()

        return state

    state = tuple(state_ref[v] for v in range(16))
    state = lax.fori_loop(0, rounds, two_batches, state)
    emit(count - 1)
    if not has_sum:
        copy_out(1).start()
    for v in range(16):
        end_ref[v] = state[v]
    if not has_sum:
        for part in range(2 if early else 1):
            copy_out(1 - part).wait()


def row_scan(place, cost, state, lead, flip):
    rows, cols, _ = cost.shape
    width = LANES // rows
    count = cols // width
    batch = math.gcd(count // 2, BATCH)
    vmem = pl.BlockSpec(memory_space=pltpu.VMEM)
    hbm = pl.BlockSpec(memory_space=pltpu.HBM)
    has_sum = lead is not None
    args = [place, cost, state] + ([lead] if has_sum else [])
    whole = pltpu.VMEM(cost.shape, jnp.float32)
    moved = [whole, pltpu.SemaphoreType.DMA(() if has_sum else (2,))]
    return pl.pallas_call(
        functools.partial(row_scan_kernel, (rows, cols, flip, batch), has_sum),
        out_shape=(
            jax.ShapeDtypeStruct(cost.shape, jnp.float32),
            jax.ShapeDtypeStruct((16, 8, LANES), jnp.float32),
        ),
        in_specs=[pl.BlockSpec(memory_space=pltpu.SMEM), hbm, vmem] + ([hbm] if has_sum else []),
        out_specs=(vmem if has_sum else hbm, vmem),
        scratch_shapes=moved
        + [
            whole,
            pltpu.SemaphoreType.DMA((count,)),
            pltpu.VMEM((LANES, LANES), jnp.float32),
            pltpu.VMEM((LANES, LANES), jnp.float32),
            pltpu.VMEM((width // 2, 2 * LANES, 2 * LANES), jnp.bfloat16),
            pltpu.VMEM((batch * LANES, 2 * LANES), jnp.bfloat16),
            pltpu.VMEM((batch * LANES, 2 * LANES), jnp.bfloat16),
            pltpu.VMEM((batch, width, LANES, LANES), jnp.float32),
            pltpu.VMEM((batch, width, LANES, LANES), jnp.float32),
            pltpu.VMEM((16, 8, LANES), jnp.float32),
            pltpu.VMEM((8, LANES), jnp.float32),
        ],
        compiler_params=pltpu.CompilerParams(vmem_limit_bytes=24 << 20),
        cost_estimate=pl.CostEstimate(flops=2_000_000_000, bytes_accessed=30_000_000, transcendentals=0),
    )(*args)


def column_kernel(cost_ref, out_ref, sum_ref):
    length, width, _ = cost_ref.shape
    lane = lax.broadcasted_iota(jnp.int32, (width, DISP), 1)

    def step(state, index):
        cost = cost_ref[index].astype(jnp.float32)
        low = jnp.min(state, axis=1, keepdims=True)
        above = jnp.where(lane == DISP - 1, BIG, pltpu.roll(state, DISP - 1, 1))
        below = jnp.where(lane == 0, BIG, pltpu.roll(state, 1, 1))
        near = jnp.minimum(above, below) + P_SMALL
        return cost + jnp.minimum(jnp.minimum(state, near), low + P_LARGE) - low

    def first(index, states):
        down = step(states[0], index)
        up = step(states[1], length - 1 - index)
        sum_ref[index] = down
        sum_ref[length - 1 - index] = up
        return down, up

    def second(index, states):
        down = step(states[0], index)
        up = step(states[1], length - 1 - index)
        out_ref[index] = (sum_ref[index] + down).astype(jnp.bfloat16)
        out_ref[length - 1 - index] = (sum_ref[length - 1 - index] + up).astype(jnp.bfloat16)
        return down, up

    zero = jnp.zeros((width, DISP), jnp.float32)
    states = lax.fori_loop(0, length // 2, first, (zero, zero))
    lax.fori_loop(length // 2, length, second, states)


def lowest(state):
    level = list(state)
    while len(level) > 1:
        level = [jnp.minimum(level[i], level[i + 1]) for i in range(0, len(level), 2)]
    low = level[0]
    for shift in (4, 2, 1):
        low = jnp.minimum(low, pltpu.roll(low, shift, 0))
    return low


def column_tiles_kernel(cost_ref, out_ref, tile_ref, split_ref, spread_ref, path_ref, turn_ref, sum_ref):
    length, width, _ = cost_ref.shape
    both = 2 * width
    per = LANES // both
    tiles = length // per
    sublane = lax.broadcasted_iota(jnp.int32, (8, LANES), 0)
    lane_step = lax.broadcasted_iota(jnp.int32, (8, LANES), 1) // both
    k = lax.broadcasted_iota(jnp.int32, (LANES, per * LANES), 0)
    n = lax.broadcasted_iota(jnp.int32, (LANES, per * LANES), 1)
    pick = jnp.where(k == n // LANES * both + n % both, 1.0, 0.0).astype(jnp.bfloat16)

    def places(tile):
        rows = []
        for step in range(per):
            rows += [tile * per + step, length - 1 - (tile * per + step)]
        return rows

    def prepare(index, carry):
        for slot in range(8):
            tile = index * 8 + slot
            block = jnp.concatenate([cost_ref[row] for row in places(tile)], axis=0)
            tile_ref[slot] = block.astype(jnp.float32).T
            for v in range(0, 16, 2):
                plane = jnp.concatenate(
                    [tile_ref[slot, pl.ds(v, 8, stride=16), :], tile_ref[slot, pl.ds(v + 1, 8, stride=16), :]], axis=0
                )
                split_ref[slot * LANES + v * 8 : slot * LANES + v * 8 + 16, :] = plane.astype(jnp.bfloat16)
        spread = jnp.dot(split_ref[...], pick, preferred_element_type=jnp.float32)
        for slot in range(8):
            for step in range(per):
                spread_ref[index * 8 + slot, step] = spread[
                    slot * LANES : slot * LANES + LANES, step * LANES : step * LANES + LANES
                ]
        return carry

    lax.fori_loop(0, tiles // 8, prepare, 0)

    def emit(tile, last):
        tile = jnp.maximum(tile, 0)
        for v in range(16):
            turn_ref[pl.ds(v, 8, stride=16), :] = path_ref[v]
        done = turn_ref[...].T
        for i, row in enumerate(places(tile)):
            piece = done[i * width : (i + 1) * width]
            if last:
                out_ref[row] = (sum_ref[row] + piece).astype(jnp.bfloat16)
            else:
                sum_ref[row] = piece

    def run(tile, state, last):
        emit(tile - 1, last)
        state = list(state)
        for step in range(per):
            low = lowest(state)
            bound = low + P_LARGE
            above = jnp.where(sublane == 7, BIG, pltpu.roll(state[0], 7, 0))
            below = jnp.where(sublane == 0, BIG, pltpu.roll(state[15], 1, 0))
            padded = [below] + state + [above]
            fresh = []
            for v in range(16):
                near = jnp.minimum(padded[v], padded[v + 2]) + P_SMALL
                best = jnp.minimum(jnp.minimum(state[v], near), bound)
                value = spread_ref[tile, step, v * 8 : v * 8 + 8, :] + (best - low)
                if step:
                    pltpu.store(path_ref.at[v], value, mask=lane_step == step)
                else:
                    path_ref[v] = value
                fresh.append(value)
            state = fresh
        return tuple(state)

    def loop(begin, end, state, last):
        return lax.fori_loop(begin, end, lambda tile, carry: run(tile, carry, last), state, unroll=8)

    state = (jnp.zeros((8, LANES), jnp.float32),) * 16
    state = loop(0, tiles // 2, state, False)
    emit(tiles // 2 - 1, False)
    state = loop(tiles // 2, tiles, state, True)
    emit(tiles - 1, True)


def column_scan(columns):
    length, width, _ = columns.shape
    vmem = pl.BlockSpec(memory_space=pltpu.VMEM)
    scratch = [pltpu.VMEM(columns.shape, jnp.float32)]
    kernel = column_kernel
    per = LANES // (2 * width)
    if width % 16 == 0 and LANES % (2 * width) == 0 and length % (16 * per) == 0:
        kernel = column_tiles_kernel
        scratch = [
            pltpu.VMEM((8, LANES, LANES), jnp.float32),
            pltpu.VMEM((8 * LANES, LANES), jnp.bfloat16),
            pltpu.VMEM((length // per, per, LANES, LANES), jnp.float32),
            pltpu.VMEM((16, 8, LANES), jnp.float32),
            pltpu.VMEM((LANES, LANES), jnp.float32),
        ] + scratch
    return pl.pallas_call(
        kernel,
        out_shape=jax.ShapeDtypeStruct(columns.shape, jnp.bfloat16),
        in_specs=[vmem],
        out_specs=vmem,
        scratch_shapes=scratch,
        compiler_params=pltpu.CompilerParams(vmem_limit_bytes=20 << 20),
        cost_estimate=pl.CostEstimate(flops=200_000_000, bytes_accessed=2_000_000, transcendentals=0),
    )(columns)


def add_kernel(across_ref, down_ref, out_ref):
    rows, cols, _ = across_ref.shape
    for row in range(rows):
        out_ref[row] = across_ref[row] + down_ref[:, row].reshape(cols, DISP).astype(jnp.float32)


def add_vertical(horizontal, vertical):
    rows, cols, _ = horizontal.shape
    if not packs(vertical.shape[2]):
        return horizontal + jnp.swapaxes(vertical, 0, 1).reshape(rows, cols, DISP).astype(jnp.float32)
    vmem = pl.BlockSpec(memory_space=pltpu.VMEM)
    return pl.pallas_call(
        add_kernel,
        out_shape=jax.ShapeDtypeStruct(horizontal.shape, jnp.float32),
        in_specs=[vmem, vmem],
        out_specs=vmem,
        compiler_params=pltpu.CompilerParams(vmem_limit_bytes=8 << 20),
        cost_estimate=pl.CostEstimate(flops=300_000, bytes_accessed=2_600_000, transcendentals=0),
    )(horizontal, vertical)


def normalize(image_pixels):
    return (image_pixels.astype(jnp.float32) / 1024.0 - 2.0).astype(jnp.bfloat16)


def weights_kernel(rows, base_ref, first_ref, wt_ref, w1_ref):
    wt_ref[...] = jnp.zeros_like(wt_ref)
    layers, taps = base_ref.shape[0], base_ref.shape[1]
    for layer in range(layers):
        for dy in range(taps):
            for dx in range(taps):
                block = base_ref[layer, dy, dx].astype(jnp.float32).T.astype(jnp.bfloat16)
                for out in range(wt_ref.shape[3] // CH):
                    top = (out + dy) * CH
                    wt_ref[layer, dx, top : top + CH, out * CH : (out + 1) * CH] = block
    shape = w1_ref.shape
    row = lax.broadcasted_iota(jnp.int32, shape, 0)
    tall = rows + 8
    dx_at, dy_at = row // tall, row % tall - lax.broadcasted_iota(jnp.int32, shape, 1) // CH
    value = jnp.zeros(shape, jnp.float32)
    for dy in range(taps):
        for dx in range(taps):
            line = first_ref[dy * taps + dx : dy * taps + dx + 1, :]
            value = jnp.where((dx_at == dx) & (dy_at == dy), line, value)
    w1_ref[...] = value.astype(jnp.bfloat16)


def banded_weights(first_weight, conv_weights, rows):
    base = jnp.transpose(conv_weights, (0, 3, 4, 1, 2))
    lines = jnp.transpose(first_weight, (1, 2, 3, 0)).reshape(9, CH).astype(jnp.float32)
    lines = jnp.tile(lines, (1, rows + 6))
    vmem = pl.BlockSpec(memory_space=pltpu.VMEM)
    return pl.pallas_call(
        functools.partial(weights_kernel, rows),
        out_shape=(
            jax.ShapeDtypeStruct((base.shape[0], 3, 6 * CH, 4 * CH), jnp.bfloat16),
            jax.ShapeDtypeStruct((LANES, (rows + 6) * CH), jnp.bfloat16),
        ),
        in_specs=[vmem, vmem],
        out_specs=(vmem, vmem),
        compiler_params=pltpu.CompilerParams(vmem_limit_bytes=12 << 20),
        cost_estimate=pl.CostEstimate(flops=10_000_000, bytes_accessed=2_500_000, transcendentals=0),
    )(base, lines)


def neighbours(pair, weights, row_axis, strip_axis):
    groups, strips = lax.axis_size(row_axis), lax.axis_size(strip_axis)
    above = lax.ppermute(pair, row_axis, [(i, i + 1) for i in range(groups - 1)])
    below = lax.ppermute(pair, row_axis, [(i + 1, i) for i in range(groups - 1)])
    above, below, weights = lax.optimization_barrier((above, below, weights))
    own = jnp.concatenate([above, pair, below], axis=1)
    other = lax.ppermute(own, strip_axis, [(i, i ^ 1) for i in range(strips)])
    first = lax.axis_index(strip_axis) == 0
    return jnp.concatenate([jnp.where(first, own, other), jnp.where(first, other, own)], axis=2), weights


def stacked(image, start, length, flipped):
    part = lax.dynamic_slice_in_dim(image, start - 1, length + 2, 1)
    if flipped:
        part = lax.optimization_barrier(part[:, ::-1])
    shifts = [part[:, dx : dx + length] for dx in ((2, 1, 0) if flipped else (0, 1, 2))]
    joined = jnp.concatenate(shifts, axis=0)
    joined = jnp.pad(joined, ((0, LANES - joined.shape[0]), (0, 0)))
    return joined.T


def per_device(left_pixels, right_pixels, valid_mask, first_weight, conv_weights):
    rows, cols = left_pixels.shape
    groups, strips = lax.axis_size("rows"), lax.axis_size("strips")
    group, strip = lax.axis_index("rows"), lax.axis_index("strips")
    total_rows, total_cols = rows * groups, cols * strips

    wt, w1 = banded_weights(first_weight, conv_weights, rows)
    pair = jnp.stack([normalize(left_pixels), normalize(right_pixels)])
    band, (wt, w1) = neighbours(pair, (wt, w1), "rows", "strips")
    band = band[:, rows - 4 : 2 * rows + 4]
    left_length, right_length = plan(cols)[0], plan(cols + DISP)[0]
    margin = right_length + 8
    band = jnp.pad(band, ((0, 0), (0, 0), (margin, margin)))
    first_col = strip * cols
    left_stack = stacked(band[0], margin + first_col - 3 * EDGE, left_length, False)
    right_start = first_col + cols - 1 + 3 * EDGE - (right_length - 1)
    right_stack = stacked(band[1], margin + right_start, right_length, True)
    scale = -1.0 / math.sqrt(CH)
    mask = jnp.repeat((valid_mask.astype(jnp.float32) * scale).astype(jnp.bfloat16).T, CH, axis=1)
    place = jnp.stack([group * rows, first_col, strip]).astype(jnp.int32)

    per_group = cols // groups
    cost, *packed = cost_volume(
        left_stack, right_stack, mask, w1, wt, place, rows, cols, total_rows, total_cols, per_group
    )
    if packed:
        grouped = packed[0].reshape(groups, rows, per_group, DISP)
    else:
        centred = (cost - offsets(cost.reshape(-1, DISP)).reshape(cost.shape)).astype(jnp.bfloat16)
        grouped = jnp.swapaxes(centred.reshape(rows, groups, per_group, DISP), 0, 1)
    columns = lax.all_to_all(grouped, "rows", split_axis=0, concat_axis=0, tiled=True)
    columns = columns.reshape(total_rows, per_group, DISP)

    zero = jnp.zeros((16, 8, LANES), jnp.float32)
    leading, end = row_scan(place, cost, zero, None, False)
    columns, end = lax.optimization_barrier((columns, end))
    column_sum = column_scan(columns)
    received = lax.ppermute(end, "strips", [(i, i ^ 1) for i in range(strips)])
    vertical = lax.all_to_all(
        column_sum.reshape(groups, rows, per_group, DISP), "rows", split_axis=0, concat_axis=0, tiled=True
    )
    horizontal, _ = row_scan(place, cost, received, leading, True)
    return add_vertical(horizontal, vertical)


def solution(mesh):
    in_specs = (P("rows", "strips"), P("rows", "strips"), P("rows", "strips"), P(), P())
    out_specs = P("rows", "strips", None)
    return jax.shard_map(
        per_device, mesh=mesh, in_specs=in_specs, out_specs=out_specs, check_vma=False
    )
```

```python
import functools
import math

import jax
import jax.numpy as jnp
from jax import lax
from jax.experimental import pallas as pl
from jax.experimental.pallas import tpu as pltpu
from jax.sharding import PartitionSpec as P

DISP = 128
P_SMALL = 0.5
P_LARGE = 2.0
BIG = 3.0e38
CH = 64
EDGE = 8
LANES = 128
BATCH = 2
PARTS = 1
COST_ROOM = 60_000_000
SCAN_ROOM = 62_600_000
ADD_ROOM = 62_450_000


def plan(width):
    unit = 16 * PARTS
    totals = [-(-width // unit) * unit]
    for _ in range(3):
        totals.append(-(-(totals[-1] + 2 * EDGE) // unit) * unit)
    return totals[::-1]


def feature_stacks(stacks, w1_ref, wt_ref, weights_of, row_low, row_high):
    def inside(test, base, count, lanes, halo, lane0):
        position = lax.broadcasted_iota(jnp.int32, (count, lanes), 0) + base
        row = (lax.broadcasted_iota(jnp.int32, (count, lanes), 1) + lane0) // CH - halo
        return test(position) & (row >= row_low) & (row < row_high)

    def first(index, carry):
        for pix_ref, bufs, test, flipped in stacks:
            chunk = bufs[0].shape[0] // PARTS
            start = index * chunk
            value = jnp.dot(pix_ref[pl.ds(start, chunk), :], w1_ref[...], preferred_element_type=jnp.float32)
            keep = inside(test, start - 3 * EDGE, chunk, bufs[0].shape[1], 3, 0)
            bufs[0][pl.ds(start, chunk), :] = jnp.where(keep, jnp.maximum(value, 0.0), 0.0).astype(jnp.bfloat16)
        return carry

    for index in range(PARTS):
        first(index, 0)

    for layer in range(1, 4):

        def convolve(index, carry, layer=layer):
            halo = 3 - layer
            for pix_ref, bufs, test, flipped in stacks:
                source, target = bufs[layer - 1], bufs[layer]
                out_rows = target.shape[1] // CH
                chunk = target.shape[0] // PARTS
                reach = chunk + 2 * EDGE
                start = index * chunk
                for group in range(0, out_rows, 4):
                    count = min(4, out_rows - group)
                    wide, deep = count * CH, (count + 2) * CH
                    block = source[pl.ds(start, reach), group * CH : group * CH + deep]
                    parts = [
                        jnp.dot(block, wt_ref[layer - 1, dx, :deep, :wide], preferred_element_type=jnp.float32)
                        for dx in range(3)
                    ]
                    before, after = (parts[2], parts[0]) if flipped else (parts[0], parts[2])
                    value = pltpu.roll(before, 1, 0) + parts[1] + pltpu.roll(after, reach - 1, 0)
                    value = value[EDGE : EDGE + chunk]
                    if layer < 3:
                        value = jnp.maximum(value, 0.0)
                    keep = inside(test, start - halo * EDGE, chunk, wide, halo, group * CH)
                    value = jnp.where(keep, value, 0.0).astype(jnp.bfloat16)
                    target[pl.ds(start, chunk), group * CH : group * CH + wide] = value
            return carry

        weights_of(layer - 1).wait()
        for index in range(PARTS):
            convolve(index, 0)


def offsets(costs):
    even = jnp.full((DISP, DISP), 1.0 / DISP, jnp.bfloat16)
    return jnp.dot(costs.astype(jnp.bfloat16), even, preferred_element_type=jnp.float32)


def packs(per_group):
    return per_group % 16 == 0 and LANES % per_group == 0


def cost_kernel(dims, where_ref, left_ref, right_ref, mask_ref, w1_ref, wt_hbm, out_ref, *rest):
    rows, cols, total_rows, total_cols, per_group = dims
    payload_ref, rest = (rest[0], rest[1:]) if packs(per_group) else (None, rest)
    cost_ref, sems, wt_ref, wt_sems, *bufs = rest

    def weights_of(layer):
        return pltpu.make_async_copy(wt_hbm.at[layer], wt_ref.at[layer], wt_sems.at[layer])

    for layer in range(3):
        weights_of(layer).start()
    first_row, first_col = where_ref[0], where_ref[1]
    row_low, row_high = -first_row, total_rows - first_row
    left_bufs, right_bufs = bufs[:4], bufs[4:]

    def left_col(position):
        col = position + first_col
        return (col >= 0) & (col < total_cols)

    def right_col(position):
        col = first_col + cols - 1 - position
        return (col >= 0) & (col < total_cols)

    feature_stacks(
        [(left_ref, left_bufs, left_col, False), (right_ref, right_bufs, right_col, True)],
        w1_ref, wt_ref, weights_of, row_low, row_high,
    )
    left, right = left_bufs[3], right_bufs[3]
    for row in range(rows):
        pair = row // 2 * LANES
        lane = lax.broadcasted_iota(jnp.int32, (LANES, LANES), 1)
        own = (lane // CH) == row % 2

        for index in range(cols // LANES):
            start = index * LANES
            window = cols - LANES - start
            scale = mask_ref[start : start + LANES, pair : pair + LANES]
            a = jnp.where(own, left[start : start + LANES, pair : pair + LANES] * scale, jnp.zeros((), jnp.bfloat16))
            b = right[window : window + 2 * LANES, pair : pair + LANES]
            product = lax.dot_general(a, b, (((1,), (1,)), ((), ())), preferred_element_type=jnp.float32)
            skewed = pltpu.roll(product, LANES + 1, 1, stride=1, stride_axis=0)[:, :LANES]
            cost_ref[row, start : start + LANES, :] = skewed
            if payload_ref is not None:
                skewed = skewed - offsets(skewed)
                for k in range(LANES // per_group):
                    piece = skewed[k * per_group : (k + 1) * per_group].astype(jnp.bfloat16)
                    group = index * (LANES // per_group) + k
                    payload_ref[group, row * per_group : (row + 1) * per_group, :] = piece
        pltpu.make_async_copy(cost_ref.at[row], out_ref.at[row], sems.at[row]).start()
    for row in range(rows):
        pltpu.make_async_copy(cost_ref.at[row], out_ref.at[row], sems.at[row]).wait()


def cost_volume(left_stack, right_stack, mask, w1, wt, place, rows, cols, total_rows, total_cols, per_group):
    bufs = [pltpu.VMEM((rows, cols, DISP), jnp.float32), pltpu.SemaphoreType.DMA((rows,))]
    bufs += [pltpu.VMEM(wt.shape, wt.dtype), pltpu.SemaphoreType.DMA((3,))]
    for width in (cols, cols + DISP):
        sizes = plan(width)
        for layer in range(4):
            out_rows = rows + 2 * (3 - layer)
            length = sizes[layer]
            bufs.append(pltpu.VMEM((length, out_rows * CH), jnp.bfloat16))
    vmem = pl.BlockSpec(memory_space=pltpu.VMEM)
    shapes = [jax.ShapeDtypeStruct((rows, cols, DISP), jnp.float32)]
    if packs(per_group):
        shapes.append(jax.ShapeDtypeStruct((cols // per_group, rows * per_group, DISP), jnp.bfloat16))
    return pl.pallas_call(
        functools.partial(cost_kernel, (rows, cols, total_rows, total_cols, per_group)),
        out_shape=tuple(shapes),
        in_specs=[pl.BlockSpec(memory_space=pltpu.SMEM)] + [vmem] * 4 + [pl.BlockSpec(memory_space=pltpu.HBM)],
        out_specs=(pl.BlockSpec(memory_space=pltpu.HBM), vmem)[: len(shapes)],
        scratch_shapes=bufs,
        compiler_params=pltpu.CompilerParams(vmem_limit_bytes=COST_ROOM),
        cost_estimate=pl.CostEstimate(flops=8_000_000_000, bytes_accessed=6_000_000, transcendentals=0),
    )(place, left_stack, right_stack, mask, w1, wt)


def row_scan_kernel(dims, has_sum, place_ref, cost_hbm, state_ref, *rest):
    rows, cols, flip, batch = dims
    if has_sum:
        lead_hbm, out_hbm, end_ref, lead_ref, lead_sem, *rest = rest
    else:
        out_hbm, end_ref, *rest = rest
    out_ref, out_sems, cost_ref, cost_sems, tile_ref, turn_ref, pick_ref, split_a, split_b, even_ref, odd_ref, path_ref, low_ref = rest
    width = LANES // rows
    count = cols // width
    forward = place_ref[2] == (1 if flip else 0)
    lane = lax.broadcasted_iota(jnp.int32, (8, LANES), 1)
    sublane = lax.broadcasted_iota(jnp.int32, (8, LANES), 0)
    lane_col = lane % width

    def copy_in(index):
        part = pl.ds(chunk_start(index), width)
        return pltpu.make_async_copy(cost_hbm.at[:, part], cost_ref.at[:, part], cost_sems.at[index])

    rounds = count // batch // 2
    early = max(rounds // 2 * 2 * batch - 1, 0)

    def copy_out(part):
        length = (early, count - early)[part] * width
        begin = jnp.where(forward, (0, early * width)[part], ((count - early) * width, 0)[part])
        cut = pl.ds(pl.multiple_of(begin, width), length)
        return pltpu.make_async_copy(out_ref.at[:, cut], out_hbm.at[:, cut], out_sems.at[part])

    def chunk_start(index):
        chunk = jnp.where(forward, index, count - 1 - index)
        return pl.multiple_of(chunk * width, width)

    for index in range(count):
        copy_in(index).start()
    if has_sum:
        copy_lead = pltpu.make_async_copy(lead_hbm, lead_ref, lead_sem)
        copy_lead.start()

    def build_pick(pair, carry):
        k = lax.broadcasted_iota(jnp.int32, (2 * LANES, 2 * LANES), 0) % LANES
        n = lax.broadcasted_iota(jnp.int32, (2 * LANES, 2 * LANES), 1)
        wanted = n % LANES // width * width + 2 * pair + n // LANES
        pick_ref[pair] = jnp.where(k == wanted, 1.0, 0.0).astype(jnp.bfloat16)
        return carry

    lax.fori_loop(0, width // 2, build_pick, 0)

    def split(index, target):
        start = chunk_start(jnp.minimum(index, count - 1))
        tile = jnp.concatenate([cost_ref[row, pl.ds(start, width), :] for row in range(rows)], axis=0)
        tile_ref[...] = tile.T
        for v in range(0, 16, 2):
            plane = jnp.concatenate(
                [tile_ref[pl.ds(v, 8, stride=16), :], tile_ref[pl.ds(v + 1, 8, stride=16), :]], axis=0
            )
            high = plane.astype(jnp.bfloat16)
            low = (plane - high.astype(jnp.float32)).astype(jnp.bfloat16)
            target[v * 8 : v * 8 + 16, :LANES] = high
            target[v * 8 : v * 8 + 16, LANES:] = low

    def spread(source, target, pair):
        both = jnp.dot(source[...], pick_ref[pair], preferred_element_type=jnp.float32)
        for slot in range(batch):
            target[slot, 2 * pair] = both[slot * LANES : slot * LANES + LANES, :LANES]
            target[slot, 2 * pair + 1] = both[slot * LANES : slot * LANES + LANES, LANES:]

    def emit(index):
        start = chunk_start(jnp.maximum(index, 0))
        low = low_ref[...]
        for v in range(16):
            turn_ref[pl.ds(v, 8, stride=16), :] = path_ref[v] - low
        done = turn_ref[...].T
        if has_sum:
            tile = jnp.concatenate([cost_ref[row, pl.ds(start, width), :] for row in range(rows)], axis=0)
            done = done + 2.0 * offsets(tile)
        for row in range(rows):
            piece = done[row * width : (row + 1) * width]
            if has_sum:
                piece = piece + lead_ref[row, pl.ds(start, width), :]
            out_ref[row, pl.ds(start, width), :] = piece

    def advance(state, low, slot, step, current):
        col = jnp.where(forward, step, width - 1 - step)
        mask = lane_col == col
        bound = low + P_LARGE
        above = jnp.where(sublane == 7, BIG, pltpu.roll(state[0], 7, 0))
        below = jnp.where(sublane == 0, BIG, pltpu.roll(state[15], 1, 0))
        padded = [below] + list(state) + [above]
        fresh = []
        for v in range(16):
            near = jnp.minimum(padded[v], padded[v + 2]) + P_SMALL
            best = jnp.minimum(jnp.minimum(state[v], near), bound)
            value = current[slot, col, v * 8 : v * 8 + 8, :] + best
            pltpu.store(path_ref.at[v], value, mask=mask)
            fresh.append(value)
        pltpu.store(low_ref, low, mask=mask)
        return fresh

    def one_batch(number, state, current, coming, ready, filling):
        base = number * batch
        pairs = width // 2 // batch

        def one_chunk(slot, state):
            emit(base + slot - 1)
            split(base + 2 * batch + slot, filling.at[pl.ds(pl.multiple_of(slot * LANES, LANES), LANES)])
            low = lowest(state)
            state = [value - low for value in state]
            low = jnp.zeros_like(low)
            for step in range(width):
                if step % (2 * batch) == 0:
                    spread(ready, coming, slot * pairs + step // (2 * batch))
                if step:
                    low = lowest(state)
                state = advance(state, low, slot, step, current)
            return tuple(state)

        return lax.fori_loop(0, batch, one_chunk, state)

    for index in range(2 * batch):
        copy_in(index).wait()
    for slot in range(batch):
        split(slot, split_a.at[pl.ds(slot * LANES, LANES)])
        split(batch + slot, split_b.at[pl.ds(slot * LANES, LANES)])

    def first(group, carry):
        for k in range(4):
            spread(split_a, even_ref, group * 4 + k)
        return carry

    lax.fori_loop(0, width // 8, first, 0)

    for index in range(2 * batch, count):
        copy_in(index).wait()
    if has_sum:
        copy_lead.wait()

    def two_batches(index, state):
        state = one_batch(2 * index, state, even_ref, odd_ref, split_b, split_a)
        state = one_batch(2 * index + 1, state, odd_ref, even_ref, split_a, split_b)
        if early:

            @pl.when(index == rounds // 2 - 1)
            def _():
                copy_out(0).start()

        return state

    state = tuple(state_ref[v] for v in range(16))
    state = lax.fori_loop(0, rounds, two_batches, state)
    emit(count - 1)
    copy_out(1).start()
    for v in range(16):
        end_ref[v] = state[v]
    for part in range(2 if early else 1):
        copy_out(1 - part).wait()


def row_scan(place, cost, state, lead, flip):
    rows, cols, _ = cost.shape
    width = LANES // rows
    count = cols // width
    batch = math.gcd(count // 2, BATCH)
    vmem = pl.BlockSpec(memory_space=pltpu.VMEM)
    hbm = pl.BlockSpec(memory_space=pltpu.HBM)
    has_sum = lead is not None
    args = [place, cost, state] + ([lead] if has_sum else [])
    whole = pltpu.VMEM(cost.shape, jnp.float32)
    moved = [whole, pltpu.SemaphoreType.DMA(())] if has_sum else []
    return pl.pallas_call(
        functools.partial(row_scan_kernel, (rows, cols, flip, batch), has_sum),
        out_shape=(
            jax.ShapeDtypeStruct(cost.shape, jnp.float32),
            jax.ShapeDtypeStruct((16, 8, LANES), jnp.float32),
        ),
        in_specs=[pl.BlockSpec(memory_space=pltpu.SMEM), hbm, vmem] + ([hbm] if has_sum else []),
        out_specs=(hbm, vmem),
        scratch_shapes=moved
        + [
            whole,
            pltpu.SemaphoreType.DMA((2,)),
            whole,
            pltpu.SemaphoreType.DMA((count,)),
            pltpu.VMEM((LANES, LANES), jnp.float32),
            pltpu.VMEM((LANES, LANES), jnp.float32),
            pltpu.VMEM((width // 2, 2 * LANES, 2 * LANES), jnp.bfloat16),
            pltpu.VMEM((batch * LANES, 2 * LANES), jnp.bfloat16),
            pltpu.VMEM((batch * LANES, 2 * LANES), jnp.bfloat16),
            pltpu.VMEM((batch, width, LANES, LANES), jnp.float32),
            pltpu.VMEM((batch, width, LANES, LANES), jnp.float32),
            pltpu.VMEM((16, 8, LANES), jnp.float32),
            pltpu.VMEM((8, LANES), jnp.float32),
        ],
        compiler_params=pltpu.CompilerParams(vmem_limit_bytes=SCAN_ROOM),
        cost_estimate=pl.CostEstimate(flops=2_000_000_000, bytes_accessed=30_000_000, transcendentals=0),
    )(*args)


def column_kernel(cost_ref, out_ref, sum_ref):
    length, width, _ = cost_ref.shape
    lane = lax.broadcasted_iota(jnp.int32, (width, DISP), 1)

    def step(state, index):
        cost = cost_ref[index].astype(jnp.float32)
        low = jnp.min(state, axis=1, keepdims=True)
        above = jnp.where(lane == DISP - 1, BIG, pltpu.roll(state, DISP - 1, 1))
        below = jnp.where(lane == 0, BIG, pltpu.roll(state, 1, 1))
        near = jnp.minimum(above, below) + P_SMALL
        return cost + jnp.minimum(jnp.minimum(state, near), low + P_LARGE) - low

    def first(index, states):
        down = step(states[0], index)
        up = step(states[1], length - 1 - index)
        sum_ref[index] = down
        sum_ref[length - 1 - index] = up
        return down, up

    def second(index, states):
        down = step(states[0], index)
        up = step(states[1], length - 1 - index)
        out_ref[index] = (sum_ref[index] + down).astype(jnp.bfloat16)
        out_ref[length - 1 - index] = (sum_ref[length - 1 - index] + up).astype(jnp.bfloat16)
        return down, up

    zero = jnp.zeros((width, DISP), jnp.float32)
    states = lax.fori_loop(0, length // 2, first, (zero, zero))
    lax.fori_loop(length // 2, length, second, states)


def lowest(state):
    level = list(state)
    while len(level) > 1:
        level = [jnp.minimum(level[i], level[i + 1]) for i in range(0, len(level), 2)]
    low = level[0]
    for shift in (4, 2, 1):
        low = jnp.minimum(low, pltpu.roll(low, shift, 0))
    return low


def column_tiles_kernel(cost_ref, out_ref, tile_ref, split_ref, spread_ref, path_ref, turn_ref, sum_ref):
    length, width, _ = cost_ref.shape
    both = 2 * width
    per = LANES // both
    tiles = length // per
    sublane = lax.broadcasted_iota(jnp.int32, (8, LANES), 0)
    lane_step = lax.broadcasted_iota(jnp.int32, (8, LANES), 1) // both
    k = lax.broadcasted_iota(jnp.int32, (LANES, per * LANES), 0)
    n = lax.broadcasted_iota(jnp.int32, (LANES, per * LANES), 1)
    pick = jnp.where(k == n // LANES * both + n % both, 1.0, 0.0).astype(jnp.bfloat16)

    def places(tile):
        rows = []
        for step in range(per):
            rows += [tile * per + step, length - 1 - (tile * per + step)]
        return rows

    def prepare(index, carry):
        for slot in range(8):
            tile = index * 8 + slot
            block = jnp.concatenate([cost_ref[row] for row in places(tile)], axis=0)
            tile_ref[slot] = block.astype(jnp.float32).T
            for v in range(0, 16, 2):
                plane = jnp.concatenate(
                    [tile_ref[slot, pl.ds(v, 8, stride=16), :], tile_ref[slot, pl.ds(v + 1, 8, stride=16), :]], axis=0
                )
                split_ref[slot * LANES + v * 8 : slot * LANES + v * 8 + 16, :] = plane.astype(jnp.bfloat16)
        spread = jnp.dot(split_ref[...], pick, preferred_element_type=jnp.float32)
        for slot in range(8):
            for step in range(per):
                spread_ref[index * 8 + slot, step] = spread[
                    slot * LANES : slot * LANES + LANES, step * LANES : step * LANES + LANES
                ]
        return carry

    lax.fori_loop(0, tiles // 8, prepare, 0)

    def emit(tile, last):
        tile = jnp.maximum(tile, 0)
        for v in range(16):
            turn_ref[pl.ds(v, 8, stride=16), :] = path_ref[v]
        done = turn_ref[...].T
        for i, row in enumerate(places(tile)):
            piece = done[i * width : (i + 1) * width]
            if last:
                out_ref[row] = (sum_ref[row] + piece).astype(jnp.bfloat16)
            else:
                sum_ref[row] = piece

    def run(tile, state, last):
        emit(tile - 1, last)
        state = list(state)
        for step in range(per):
            low = lowest(state)
            bound = low + P_LARGE
            above = jnp.where(sublane == 7, BIG, pltpu.roll(state[0], 7, 0))
            below = jnp.where(sublane == 0, BIG, pltpu.roll(state[15], 1, 0))
            padded = [below] + state + [above]
            fresh = []
            for v in range(16):
                near = jnp.minimum(padded[v], padded[v + 2]) + P_SMALL
                best = jnp.minimum(jnp.minimum(state[v], near), bound)
                value = spread_ref[tile, step, v * 8 : v * 8 + 8, :] + (best - low)
                if step:
                    pltpu.store(path_ref.at[v], value, mask=lane_step == step)
                else:
                    path_ref[v] = value
                fresh.append(value)
            state = fresh
        return tuple(state)

    def loop(begin, end, state, last):
        return lax.fori_loop(begin, end, lambda tile, carry: run(tile, carry, last), state, unroll=8)

    state = (jnp.zeros((8, LANES), jnp.float32),) * 16
    state = loop(0, tiles // 2, state, False)
    emit(tiles // 2 - 1, False)
    state = loop(tiles // 2, tiles, state, True)
    emit(tiles - 1, True)


def column_scan(columns):
    length, width, _ = columns.shape
    vmem = pl.BlockSpec(memory_space=pltpu.VMEM)
    scratch = [pltpu.VMEM(columns.shape, jnp.float32)]
    kernel = column_kernel
    per = LANES // (2 * width)
    if width % 16 == 0 and LANES % (2 * width) == 0 and length % (16 * per) == 0:
        kernel = column_tiles_kernel
        scratch = [
            pltpu.VMEM((8, LANES, LANES), jnp.float32),
            pltpu.VMEM((8 * LANES, LANES), jnp.bfloat16),
            pltpu.VMEM((length // per, per, LANES, LANES), jnp.float32),
            pltpu.VMEM((16, 8, LANES), jnp.float32),
            pltpu.VMEM((LANES, LANES), jnp.float32),
        ] + scratch
    return pl.pallas_call(
        kernel,
        out_shape=jax.ShapeDtypeStruct(columns.shape, jnp.bfloat16),
        in_specs=[vmem],
        out_specs=vmem,
        scratch_shapes=scratch,
        compiler_params=pltpu.CompilerParams(vmem_limit_bytes=20 << 20),
        cost_estimate=pl.CostEstimate(flops=200_000_000, bytes_accessed=2_000_000, transcendentals=0),
    )(columns)


def add_kernel(across_hbm, down_hbm, out_hbm, across_ref, down_ref, sems):
    rows, cols, _ = across_ref.shape

    def moves(row):
        return (
            pltpu.make_async_copy(across_hbm.at[row], across_ref.at[row], sems.at[0, row]),
            pltpu.make_async_copy(down_hbm.at[:, row], down_ref.at[row], sems.at[1, row]),
            pltpu.make_async_copy(across_ref.at[row], out_hbm.at[row], sems.at[2, row]),
        )

    for row in range(rows):
        moves(row)[0].start()
        moves(row)[1].start()
    for row in range(rows):
        moves(row)[0].wait()
        moves(row)[1].wait()
        across_ref[row] += down_ref[row].reshape(cols, DISP).astype(jnp.float32)
        moves(row)[2].start()
    for row in range(rows):
        moves(row)[2].wait()


def add_vertical(horizontal, vertical):
    rows, cols, _ = horizontal.shape
    groups, _, per_group, _ = vertical.shape
    if not packs(per_group):
        return horizontal + jnp.swapaxes(vertical, 0, 1).reshape(rows, cols, DISP).astype(jnp.float32)
    hbm = pl.BlockSpec(memory_space=pltpu.HBM)
    return pl.pallas_call(
        add_kernel,
        out_shape=jax.ShapeDtypeStruct(horizontal.shape, jnp.float32),
        in_specs=[hbm, hbm],
        out_specs=hbm,
        scratch_shapes=[
            pltpu.VMEM(horizontal.shape, jnp.float32),
            pltpu.VMEM((rows, groups, per_group, DISP), jnp.bfloat16),
            pltpu.SemaphoreType.DMA((3, rows)),
        ],
        compiler_params=pltpu.CompilerParams(vmem_limit_bytes=ADD_ROOM),
        cost_estimate=pl.CostEstimate(flops=300_000, bytes_accessed=2_600_000, transcendentals=0),
    )(horizontal, vertical)


def normalize(image_pixels):
    return (image_pixels.astype(jnp.float32) / 1024.0 - 2.0).astype(jnp.bfloat16)


def weights_kernel(rows, base_ref, first_ref, wt_ref, w1_ref):
    wt_ref[...] = jnp.zeros_like(wt_ref)
    layers, taps = base_ref.shape[0], base_ref.shape[1]
    for layer in range(layers):
        for dy in range(taps):
            for dx in range(taps):
                block = base_ref[layer, dy, dx].astype(jnp.float32).T.astype(jnp.bfloat16)
                for out in range(wt_ref.shape[3] // CH):
                    top = (out + dy) * CH
                    wt_ref[layer, dx, top : top + CH, out * CH : (out + 1) * CH] = block
    shape = w1_ref.shape
    row = lax.broadcasted_iota(jnp.int32, shape, 0)
    tall = rows + 8
    dx_at, dy_at = row // tall, row % tall - lax.broadcasted_iota(jnp.int32, shape, 1) // CH
    value = jnp.zeros(shape, jnp.float32)
    for dy in range(taps):
        for dx in range(taps):
            line = first_ref[dy * taps + dx : dy * taps + dx + 1, :]
            value = jnp.where((dx_at == dx) & (dy_at == dy), line, value)
    w1_ref[...] = value.astype(jnp.bfloat16)


def banded_weights(first_weight, conv_weights, rows):
    base = jnp.transpose(conv_weights, (0, 3, 4, 1, 2))
    lines = jnp.transpose(first_weight, (1, 2, 3, 0)).reshape(9, CH).astype(jnp.float32)
    lines = jnp.tile(lines, (1, rows + 6))
    vmem = pl.BlockSpec(memory_space=pltpu.VMEM)
    return pl.pallas_call(
        functools.partial(weights_kernel, rows),
        out_shape=(
            jax.ShapeDtypeStruct((base.shape[0], 3, 6 * CH, 4 * CH), jnp.bfloat16),
            jax.ShapeDtypeStruct((LANES, (rows + 6) * CH), jnp.bfloat16),
        ),
        in_specs=[vmem, vmem],
        out_specs=(vmem, vmem),
        compiler_params=pltpu.CompilerParams(vmem_limit_bytes=12 << 20),
        cost_estimate=pl.CostEstimate(flops=10_000_000, bytes_accessed=2_500_000, transcendentals=0),
    )(base, lines)


def neighbours(pair, weights, row_axis, strip_axis):
    groups, strips = lax.axis_size(row_axis), lax.axis_size(strip_axis)
    above = lax.ppermute(pair, row_axis, [(i, i + 1) for i in range(groups - 1)])
    below = lax.ppermute(pair, row_axis, [(i + 1, i) for i in range(groups - 1)])
    above, below, weights = lax.optimization_barrier((above, below, weights))
    own = jnp.concatenate([above, pair, below], axis=1)
    other = lax.ppermute(own, strip_axis, [(i, i ^ 1) for i in range(strips)])
    first = lax.axis_index(strip_axis) == 0
    return jnp.concatenate([jnp.where(first, own, other), jnp.where(first, other, own)], axis=2), weights


def stacked(image, start, length, flipped):
    part = lax.dynamic_slice_in_dim(image, start - 1, length + 2, 1)
    if flipped:
        part = lax.optimization_barrier(part[:, ::-1])
    shifts = [part[:, dx : dx + length] for dx in ((2, 1, 0) if flipped else (0, 1, 2))]
    joined = jnp.concatenate(shifts, axis=0)
    joined = jnp.pad(joined, ((0, LANES - joined.shape[0]), (0, 0)))
    return joined.T


def per_device(left_pixels, right_pixels, valid_mask, first_weight, conv_weights):
    rows, cols = left_pixels.shape
    groups, strips = lax.axis_size("rows"), lax.axis_size("strips")
    group, strip = lax.axis_index("rows"), lax.axis_index("strips")
    total_rows, total_cols = rows * groups, cols * strips

    wt, w1 = banded_weights(first_weight, conv_weights, rows)
    pair = jnp.stack([normalize(left_pixels), normalize(right_pixels)])
    band, (wt, w1) = neighbours(pair, (wt, w1), "rows", "strips")
    band = band[:, rows - 4 : 2 * rows + 4]
    left_length, right_length = plan(cols)[0], plan(cols + DISP)[0]
    margin = right_length + 8
    band = jnp.pad(band, ((0, 0), (0, 0), (margin, margin)))
    first_col = strip * cols
    left_stack = stacked(band[0], margin + first_col - 3 * EDGE, left_length, False)
    right_start = first_col + cols - 1 + 3 * EDGE - (right_length - 1)
    right_stack = stacked(band[1], margin + right_start, right_length, True)
    scale = -1.0 / math.sqrt(CH)
    mask = jnp.repeat((valid_mask.astype(jnp.float32) * scale).astype(jnp.bfloat16).T, CH, axis=1)
    place = jnp.stack([group * rows, first_col, strip]).astype(jnp.int32)

    per_group = cols // groups
    cost, *packed = cost_volume(
        left_stack, right_stack, mask, w1, wt, place, rows, cols, total_rows, total_cols, per_group
    )
    if packed:
        grouped = packed[0].reshape(groups, rows, per_group, DISP)
    else:
        centred = (cost - offsets(cost.reshape(-1, DISP)).reshape(cost.shape)).astype(jnp.bfloat16)
        grouped = jnp.swapaxes(centred.reshape(rows, groups, per_group, DISP), 0, 1)
    columns = lax.all_to_all(grouped, "rows", split_axis=0, concat_axis=0, tiled=True)
    columns = columns.reshape(total_rows, per_group, DISP)

    zero = jnp.zeros((16, 8, LANES), jnp.float32)
    leading, end = row_scan(place, cost, zero, None, False)
    columns, end = lax.optimization_barrier((columns, end))
    column_sum = column_scan(columns)
    received = lax.ppermute(end, "strips", [(i, i ^ 1) for i in range(strips)])
    vertical = lax.all_to_all(
        column_sum.reshape(groups, rows, per_group, DISP), "rows", split_axis=0, concat_axis=0, tiled=True
    )
    horizontal, _ = row_scan(place, cost, received, leading, True)
    return add_vertical(horizontal, vertical)


def solution(mesh):
    in_specs = (P("rows", "strips"), P("rows", "strips"), P("rows", "strips"), P(), P())
    out_specs = P("rows", "strips", None)
    return jax.shard_map(
        per_device, mesh=mesh, in_specs=in_specs, out_specs=out_specs, check_vma=False
    )
```

```python
import functools
import math

import jax
import jax.numpy as jnp
from jax import lax
from jax.experimental import pallas as pl
from jax.experimental.pallas import tpu as pltpu
from jax.sharding import PartitionSpec as P

DISP = 128
P_SMALL = 0.5
P_LARGE = 2.0
BIG = 3.0e38
CH = 64
EDGE = 8
LANES = 128
BATCH = 2
PARTS = 1
SCAN_ROOM = 62_600_000
SUM_ROOM = 24 << 20


def plan(width):
    unit = 16 * PARTS
    totals = [-(-width // unit) * unit]
    for _ in range(3):
        totals.append(-(-(totals[-1] + 2 * EDGE) // unit) * unit)
    return totals[::-1]


def feature_stacks(stacks, w1_ref, wt_ref, row_low, row_high):
    def inside(test, base, count, lanes, halo, lane0):
        position = lax.broadcasted_iota(jnp.int32, (count, lanes), 0) + base
        row = (lax.broadcasted_iota(jnp.int32, (count, lanes), 1) + lane0) // CH - halo
        return test(position) & (row >= row_low) & (row < row_high)

    def first(index, carry):
        for pix_ref, bufs, test, flipped in stacks:
            chunk = bufs[0].shape[0] // PARTS
            start = index * chunk
            value = jnp.dot(pix_ref[pl.ds(start, chunk), :], w1_ref[...], preferred_element_type=jnp.float32)
            keep = inside(test, start - 3 * EDGE, chunk, bufs[0].shape[1], 3, 0)
            bufs[0][pl.ds(start, chunk), :] = jnp.where(keep, jnp.maximum(value, 0.0), 0.0).astype(jnp.bfloat16)
        return carry

    for index in range(PARTS):
        first(index, 0)

    for layer in range(1, 4):

        def convolve(index, carry, layer=layer):
            halo = 3 - layer
            for pix_ref, bufs, test, flipped in stacks:
                source, target = bufs[layer - 1], bufs[layer]
                out_rows = target.shape[1] // CH
                chunk = target.shape[0] // PARTS
                reach = chunk + 2 * EDGE
                start = index * chunk
                for group in range(0, out_rows, 4):
                    count = min(4, out_rows - group)
                    wide, deep = count * CH, (count + 2) * CH
                    block = source[pl.ds(start, reach), group * CH : group * CH + deep]
                    parts = [
                        jnp.dot(block, wt_ref[layer - 1, dx, :deep, :wide], preferred_element_type=jnp.float32)
                        for dx in range(3)
                    ]
                    before, after = (parts[2], parts[0]) if flipped else (parts[0], parts[2])
                    value = pltpu.roll(before, 1, 0) + parts[1] + pltpu.roll(after, reach - 1, 0)
                    value = value[EDGE : EDGE + chunk]
                    if layer < 3:
                        value = jnp.maximum(value, 0.0)
                    keep = inside(test, start - halo * EDGE, chunk, wide, halo, group * CH)
                    value = jnp.where(keep, value, 0.0).astype(jnp.bfloat16)
                    target[pl.ds(start, chunk), group * CH : group * CH + wide] = value
            return carry

        for index in range(PARTS):
            convolve(index, 0)


def packs(per_group):
    return per_group % 16 == 0 and LANES % per_group == 0


def cost_kernel(dims, where_ref, left_ref, right_ref, mask_ref, w1_ref, wt_ref, cost_ref, off_ref, *rest):
    rows, cols, total_rows, total_cols, per_group = dims
    payload_ref, rest = (rest[0], rest[1:]) if packs(per_group) else (None, rest)
    bufs = rest
    first_row, first_col = where_ref[0], where_ref[1]
    row_low, row_high = -first_row, total_rows - first_row
    left_bufs, right_bufs = bufs[:4], bufs[4:]

    def left_col(position):
        col = position + first_col
        return (col >= 0) & (col < total_cols)

    def right_col(position):
        col = first_col + cols - 1 - position
        return (col >= 0) & (col < total_cols)

    feature_stacks(
        [(left_ref, left_bufs, left_col, False), (right_ref, right_bufs, right_col, True)],
        w1_ref, wt_ref, row_low, row_high,
    )
    left, right = left_bufs[3], right_bufs[3]
    for row in range(rows):
        pair = row // 2 * LANES
        lane = lax.broadcasted_iota(jnp.int32, (LANES, LANES), 1)
        own = (lane // CH) == row % 2

        for index in range(cols // LANES):
            start = index * LANES
            window = cols - LANES - start
            scale = mask_ref[start : start + LANES, pair : pair + LANES]
            a = jnp.where(own, left[start : start + LANES, pair : pair + LANES] * scale, jnp.zeros((), jnp.bfloat16))
            b = right[window : window + 2 * LANES, pair : pair + LANES]
            mean = jnp.mean(b.astype(jnp.float32), axis=0, keepdims=True).astype(jnp.bfloat16)
            mean = jnp.broadcast_to(mean, (LANES, LANES))
            product = lax.dot_general(
                a, jnp.concatenate([b, mean], axis=0), (((1,), (1,)), ((), ())), preferred_element_type=jnp.float32
            )
            off_ref[row, index] = lax.dot_general(
                mean[:16], a, (((1,), (1,)), ((), ())), preferred_element_type=jnp.float32
            )[:8]
            skewed = pltpu.roll(product[:, : 2 * LANES], LANES + 1, 1, stride=1, stride_axis=0)[:, :LANES]
            cost_ref[row, start : start + LANES, :] = skewed
            if payload_ref is not None:
                skewed = skewed - product[:, 2 * LANES :]
                for k in range(LANES // per_group):
                    piece = skewed[k * per_group : (k + 1) * per_group].astype(jnp.bfloat16)
                    group = index * (LANES // per_group) + k
                    payload_ref[group, row * per_group : (row + 1) * per_group, :] = piece


def cost_volume(left_stack, right_stack, mask, w1, wt, place, rows, cols, total_rows, total_cols, per_group):
    bufs = []
    for width in (cols, cols + DISP):
        sizes = plan(width)
        for layer in range(4):
            out_rows = rows + 2 * (3 - layer)
            length = sizes[layer]
            bufs.append(pltpu.VMEM((length, out_rows * CH), jnp.bfloat16))
    vmem = pl.BlockSpec(memory_space=pltpu.VMEM)
    shapes = [jax.ShapeDtypeStruct((rows, cols, DISP), jnp.float32)]
    shapes.append(jax.ShapeDtypeStruct((rows, cols // LANES, 8, LANES), jnp.float32))
    if packs(per_group):
        shapes.append(jax.ShapeDtypeStruct((cols // per_group, rows * per_group, DISP), jnp.bfloat16))
    return pl.pallas_call(
        functools.partial(cost_kernel, (rows, cols, total_rows, total_cols, per_group)),
        out_shape=tuple(shapes),
        in_specs=[pl.BlockSpec(memory_space=pltpu.SMEM)] + [vmem] * 5,
        out_specs=(vmem,) * len(shapes),
        scratch_shapes=bufs,
        compiler_params=pltpu.CompilerParams(vmem_limit_bytes=40 << 20),
        cost_estimate=pl.CostEstimate(flops=8_000_000_000, bytes_accessed=6_000_000, transcendentals=0),
    )(place, left_stack, right_stack, mask, w1, wt)


def row_scan_kernel(dims, has_sum, place_ref, cost_hbm, state_ref, *rest):
    rows, cols, flip, batch = dims
    if has_sum:
        lead_hbm, off_ref, out_ref, end_ref, lead_ref, lead_sem, shift_ref, *rest = rest
    else:
        out_hbm, end_ref, out_ref, out_sems, *rest = rest
    cost_ref, cost_sems, tile_ref, turn_ref, pick_ref, split_a, split_b, even_ref, odd_ref, path_ref, low_ref = rest
    width = LANES // rows
    count = cols // width
    forward = place_ref[2] == (1 if flip else 0)
    lane = lax.broadcasted_iota(jnp.int32, (8, LANES), 1)
    sublane = lax.broadcasted_iota(jnp.int32, (8, LANES), 0)
    lane_col = lane % width

    def copy_in(index):
        part = pl.ds(chunk_start(index), width)
        return pltpu.make_async_copy(cost_hbm.at[:, part], cost_ref.at[:, part], cost_sems.at[index])

    rounds = count // batch // 2
    early = max(rounds // 2 * 2 * batch - 1, 0)

    def copy_out(part):
        length = (early, count - early)[part] * width
        begin = jnp.where(forward, (0, early * width)[part], ((count - early) * width, 0)[part])
        cut = pl.ds(pl.multiple_of(begin, width), length)
        return pltpu.make_async_copy(out_ref.at[:, cut], out_hbm.at[:, cut], out_sems.at[part])

    def chunk_of(index):
        return jnp.where(forward, index, count - 1 - index)

    def chunk_start(index):
        return pl.multiple_of(chunk_of(index) * width, width)

    for index in range(count):
        copy_in(index).start()
    if has_sum:
        copy_lead = pltpu.make_async_copy(lead_hbm, lead_ref, lead_sem)
        copy_lead.start()
        for chunk in range(count):
            block, within = divmod(chunk * width, LANES)
            twice = jnp.zeros((8, LANES), jnp.float32)
            for row in range(rows):
                value = pltpu.roll(off_ref[row, block], (row * width - within) % LANES, 1)
                twice = jnp.where(lane // width == row, 2.0 * value, twice)
            shift_ref[chunk] = twice

    def build_pick(pair, carry):
        k = lax.broadcasted_iota(jnp.int32, (2 * LANES, 2 * LANES), 0) % LANES
        n = lax.broadcasted_iota(jnp.int32, (2 * LANES, 2 * LANES), 1)
        wanted = n % LANES // width * width + 2 * pair + n // LANES
        pick_ref[pair] = jnp.where(k == wanted, 1.0, 0.0).astype(jnp.bfloat16)
        return carry

    lax.fori_loop(0, width // 2, build_pick, 0)

    def split(index, target):
        start = chunk_start(jnp.minimum(index, count - 1))
        tile = jnp.concatenate([cost_ref[row, pl.ds(start, width), :] for row in range(rows)], axis=0)
        tile_ref[...] = tile.T
        for v in range(0, 16, 2):
            plane = jnp.concatenate(
                [tile_ref[pl.ds(v, 8, stride=16), :], tile_ref[pl.ds(v + 1, 8, stride=16), :]], axis=0
            )
            high = plane.astype(jnp.bfloat16)
            low = (plane - high.astype(jnp.float32)).astype(jnp.bfloat16)
            target[v * 8 : v * 8 + 16, :LANES] = high
            target[v * 8 : v * 8 + 16, LANES:] = low

    def spread(source, target, pair):
        both = jnp.dot(source[...], pick_ref[pair], preferred_element_type=jnp.float32)
        for slot in range(batch):
            target[slot, 2 * pair] = both[slot * LANES : slot * LANES + LANES, :LANES]
            target[slot, 2 * pair + 1] = both[slot * LANES : slot * LANES + LANES, LANES:]

    def emit(index):
        start = chunk_start(jnp.maximum(index, 0))
        low = low_ref[...]
        if has_sum:
            low = low - shift_ref[chunk_of(jnp.maximum(index, 0))]
        for v in range(16):
            turn_ref[pl.ds(v, 8, stride=16), :] = path_ref[v] - low
        done = turn_ref[...].T
        for row in range(rows):
            piece = done[row * width : (row + 1) * width]
            if has_sum:
                piece = piece + lead_ref[row, pl.ds(start, width), :]
            out_ref[row, pl.ds(start, width), :] = piece

    def advance(state, low, slot, step, current):
        col = jnp.where(forward, step, width - 1 - step)
        mask = lane_col == col
        bound = low + P_LARGE
        above = jnp.where(sublane == 7, BIG, pltpu.roll(state[0], 7, 0))
        below = jnp.where(sublane == 0, BIG, pltpu.roll(state[15], 1, 0))
        padded = [below] + list(state) + [above]
        fresh = []
        for v in range(16):
            near = jnp.minimum(padded[v], padded[v + 2]) + P_SMALL
            best = jnp.minimum(jnp.minimum(state[v], near), bound)
            value = current[slot, col, v * 8 : v * 8 + 8, :] + best
            pltpu.store(path_ref.at[v], value, mask=mask)
            fresh.append(value)
        pltpu.store(low_ref, low, mask=mask)
        return fresh

    def one_batch(number, state, current, coming, ready, filling):
        base = number * batch
        pairs = width // 2 // batch

        def one_chunk(slot, state):
            emit(base + slot - 1)
            split(base + 2 * batch + slot, filling.at[pl.ds(pl.multiple_of(slot * LANES, LANES), LANES)])
            low = lowest(state)
            state = [value - low for value in state]
            low = jnp.zeros_like(low)
            for step in range(width):
                if step % (2 * batch) == 0:
                    spread(ready, coming, slot * pairs + step // (2 * batch))
                if step:
                    low = lowest(state)
                state = advance(state, low, slot, step, current)
            return tuple(state)

        return lax.fori_loop(0, batch, one_chunk, state)

    for index in range(2 * batch):
        copy_in(index).wait()
    for slot in range(batch):
        split(slot, split_a.at[pl.ds(slot * LANES, LANES)])
        split(batch + slot, split_b.at[pl.ds(slot * LANES, LANES)])

    def first(group, carry):
        for k in range(4):
            spread(split_a, even_ref, group * 4 + k)
        return carry

    lax.fori_loop(0, width // 8, first, 0)

    for index in range(2 * batch, count):
        copy_in(index).wait()
    if has_sum:
        copy_lead.wait()

    def two_batches(index, state):
        state = one_batch(2 * index, state, even_ref, odd_ref, split_b, split_a)
        state = one_batch(2 * index + 1, state, odd_ref, even_ref, split_a, split_b)
        if not has_sum and early:

            @pl.when(index == rounds // 2 - 1)
            def _():
                copy_out(0).start()

        return state

    state = tuple(state_ref[v] for v in range(16))
    state = lax.fori_loop(0, rounds, two_batches, state)
    emit(count - 1)
    if not has_sum:
        copy_out(1).start()
    for v in range(16):
        end_ref[v] = state[v]
    if not has_sum:
        for part in range(2 if early else 1):
            copy_out(1 - part).wait()


def row_scan(place, cost, state, lead, off, flip):
    rows, cols, _ = cost.shape
    width = LANES // rows
    count = cols // width
    batch = math.gcd(count // 2, BATCH)
    vmem = pl.BlockSpec(memory_space=pltpu.VMEM)
    hbm = pl.BlockSpec(memory_space=pltpu.HBM)
    has_sum = lead is not None
    args = [place, cost, state] + ([lead, off] if has_sum else [])
    whole = pltpu.VMEM(cost.shape, jnp.float32)
    moved = [whole, pltpu.SemaphoreType.DMA(() if has_sum else (2,))]
    if has_sum:
        moved.append(pltpu.VMEM((count, 8, LANES), jnp.float32))
    return pl.pallas_call(
        functools.partial(row_scan_kernel, (rows, cols, flip, batch), has_sum),
        out_shape=(
            jax.ShapeDtypeStruct(cost.shape, jnp.float32),
            jax.ShapeDtypeStruct((16, 8, LANES), jnp.float32),
        ),
        in_specs=[pl.BlockSpec(memory_space=pltpu.SMEM), hbm, vmem] + ([hbm, vmem] if has_sum else []),
        out_specs=(vmem if has_sum else hbm, vmem),
        scratch_shapes=moved
        + [
            whole,
            pltpu.SemaphoreType.DMA((count,)),
            pltpu.VMEM((LANES, LANES), jnp.float32),
            pltpu.VMEM((LANES, LANES), jnp.float32),
            pltpu.VMEM((width // 2, 2 * LANES, 2 * LANES), jnp.bfloat16),
            pltpu.VMEM((batch * LANES, 2 * LANES), jnp.bfloat16),
            pltpu.VMEM((batch * LANES, 2 * LANES), jnp.bfloat16),
            pltpu.VMEM((batch, width, LANES, LANES), jnp.float32),
            pltpu.VMEM((batch, width, LANES, LANES), jnp.float32),
            pltpu.VMEM((16, 8, LANES), jnp.float32),
            pltpu.VMEM((8, LANES), jnp.float32),
        ],
        compiler_params=pltpu.CompilerParams(vmem_limit_bytes=SUM_ROOM if has_sum else SCAN_ROOM),
        cost_estimate=pl.CostEstimate(flops=2_000_000_000, bytes_accessed=30_000_000, transcendentals=0),
    )(*args)


def column_kernel(cost_ref, out_ref, sum_ref):
    length, width, _ = cost_ref.shape
    lane = lax.broadcasted_iota(jnp.int32, (width, DISP), 1)

    def step(state, index):
        cost = cost_ref[index].astype(jnp.float32)
        low = jnp.min(state, axis=1, keepdims=True)
        above = jnp.where(lane == DISP - 1, BIG, pltpu.roll(state, DISP - 1, 1))
        below = jnp.where(lane == 0, BIG, pltpu.roll(state, 1, 1))
        near = jnp.minimum(above, below) + P_SMALL
        return cost + jnp.minimum(jnp.minimum(state, near), low + P_LARGE) - low

    def first(index, states):
        down = step(states[0], index)
        up = step(states[1], length - 1 - index)
        sum_ref[index] = down
        sum_ref[length - 1 - index] = up
        return down, up

    def second(index, states):
        down = step(states[0], index)
        up = step(states[1], length - 1 - index)
        out_ref[index] = (sum_ref[index] + down).astype(jnp.bfloat16)
        out_ref[length - 1 - index] = (sum_ref[length - 1 - index] + up).astype(jnp.bfloat16)
        return down, up

    zero = jnp.zeros((width, DISP), jnp.float32)
    states = lax.fori_loop(0, length // 2, first, (zero, zero))
    lax.fori_loop(length // 2, length, second, states)


def lowest(state):
    level = list(state)
    while len(level) > 1:
        level = [jnp.minimum(level[i], level[i + 1]) for i in range(0, len(level), 2)]
    low = level[0]
    for shift in (4, 2, 1):
        low = jnp.minimum(low, pltpu.roll(low, shift, 0))
    return low


def column_tiles_kernel(cost_ref, out_ref, tile_ref, split_ref, spread_ref, path_ref, turn_ref, sum_ref):
    length, width, _ = cost_ref.shape
    both = 2 * width
    per = LANES // both
    tiles = length // per
    sublane = lax.broadcasted_iota(jnp.int32, (8, LANES), 0)
    lane_step = lax.broadcasted_iota(jnp.int32, (8, LANES), 1) // both
    k = lax.broadcasted_iota(jnp.int32, (LANES, per * LANES), 0)
    n = lax.broadcasted_iota(jnp.int32, (LANES, per * LANES), 1)
    pick = jnp.where(k == n // LANES * both + n % both, 1.0, 0.0).astype(jnp.bfloat16)

    def places(tile):
        rows = []
        for step in range(per):
            rows += [tile * per + step, length - 1 - (tile * per + step)]
        return rows

    def prepare(index, carry):
        for slot in range(8):
            tile = index * 8 + slot
            block = jnp.concatenate([cost_ref[row] for row in places(tile)], axis=0)
            tile_ref[slot] = block.astype(jnp.float32).T
            for v in range(0, 16, 2):
                plane = jnp.concatenate(
                    [tile_ref[slot, pl.ds(v, 8, stride=16), :], tile_ref[slot, pl.ds(v + 1, 8, stride=16), :]], axis=0
                )
                split_ref[slot * LANES + v * 8 : slot * LANES + v * 8 + 16, :] = plane.astype(jnp.bfloat16)
        spread = jnp.dot(split_ref[...], pick, preferred_element_type=jnp.float32)
        for slot in range(8):
            for step in range(per):
                spread_ref[index * 8 + slot, step] = spread[
                    slot * LANES : slot * LANES + LANES, step * LANES : step * LANES + LANES
                ]
        return carry

    lax.fori_loop(0, tiles // 8, prepare, 0)

    def emit(tile, last):
        tile = jnp.maximum(tile, 0)
        for v in range(16):
            turn_ref[pl.ds(v, 8, stride=16), :] = path_ref[v]
        done = turn_ref[...].T
        for i, row in enumerate(places(tile)):
            piece = done[i * width : (i + 1) * width]
            if last:
                out_ref[row] = (sum_ref[row] + piece).astype(jnp.bfloat16)
            else:
                sum_ref[row] = piece

    def run(tile, state, last):
        emit(tile - 1, last)
        state = list(state)
        for step in range(per):
            low = lowest(state)
            bound = low + P_LARGE
            above = jnp.where(sublane == 7, BIG, pltpu.roll(state[0], 7, 0))
            below = jnp.where(sublane == 0, BIG, pltpu.roll(state[15], 1, 0))
            padded = [below] + state + [above]
            fresh = []
            for v in range(16):
                near = jnp.minimum(padded[v], padded[v + 2]) + P_SMALL
                best = jnp.minimum(jnp.minimum(state[v], near), bound)
                value = spread_ref[tile, step, v * 8 : v * 8 + 8, :] + (best - low)
                if step:
                    pltpu.store(path_ref.at[v], value, mask=lane_step == step)
                else:
                    path_ref[v] = value
                fresh.append(value)
            state = fresh
        return tuple(state)

    def loop(begin, end, state, last):
        return lax.fori_loop(begin, end, lambda tile, carry: run(tile, carry, last), state, unroll=8)

    state = (jnp.zeros((8, LANES), jnp.float32),) * 16
    state = loop(0, tiles // 2, state, False)
    emit(tiles // 2 - 1, False)
    state = loop(tiles // 2, tiles, state, True)
    emit(tiles - 1, True)


def column_scan(columns):
    length, width, _ = columns.shape
    vmem = pl.BlockSpec(memory_space=pltpu.VMEM)
    scratch = [pltpu.VMEM(columns.shape, jnp.float32)]
    kernel = column_kernel
    per = LANES // (2 * width)
    if width % 16 == 0 and LANES % (2 * width) == 0 and length % (16 * per) == 0:
        kernel = column_tiles_kernel
        scratch = [
            pltpu.VMEM((8, LANES, LANES), jnp.float32),
            pltpu.VMEM((8 * LANES, LANES), jnp.bfloat16),
            pltpu.VMEM((length // per, per, LANES, LANES), jnp.float32),
            pltpu.VMEM((16, 8, LANES), jnp.float32),
            pltpu.VMEM((LANES, LANES), jnp.float32),
        ] + scratch
    return pl.pallas_call(
        kernel,
        out_shape=jax.ShapeDtypeStruct(columns.shape, jnp.bfloat16),
        in_specs=[vmem],
        out_specs=vmem,
        scratch_shapes=scratch,
        compiler_params=pltpu.CompilerParams(vmem_limit_bytes=20 << 20),
        cost_estimate=pl.CostEstimate(flops=200_000_000, bytes_accessed=2_000_000, transcendentals=0),
    )(columns)


def add_kernel(across_ref, down_ref, out_ref):
    rows, cols, _ = across_ref.shape
    for row in range(rows):
        out_ref[row] = across_ref[row] + down_ref[:, row].reshape(cols, DISP).astype(jnp.float32)


def add_vertical(horizontal, vertical):
    rows, cols, _ = horizontal.shape
    if not packs(vertical.shape[2]):
        return horizontal + jnp.swapaxes(vertical, 0, 1).reshape(rows, cols, DISP).astype(jnp.float32)
    vmem = pl.BlockSpec(memory_space=pltpu.VMEM)
    return pl.pallas_call(
        add_kernel,
        out_shape=jax.ShapeDtypeStruct(horizontal.shape, jnp.float32),
        in_specs=[vmem, vmem],
        out_specs=vmem,
        compiler_params=pltpu.CompilerParams(vmem_limit_bytes=8 << 20),
        cost_estimate=pl.CostEstimate(flops=300_000, bytes_accessed=2_600_000, transcendentals=0),
    )(horizontal, vertical)


def normalize(image_pixels):
    return (image_pixels.astype(jnp.float32) / 1024.0 - 2.0).astype(jnp.bfloat16)


def weights_kernel(rows, base_ref, first_ref, wt_ref, w1_ref):
    wt_ref[...] = jnp.zeros_like(wt_ref)
    layers, taps = base_ref.shape[0], base_ref.shape[1]
    for layer in range(layers):
        for dy in range(taps):
            for dx in range(taps):
                block = base_ref[layer, dy, dx].astype(jnp.float32).T.astype(jnp.bfloat16)
                for out in range(wt_ref.shape[3] // CH):
                    top = (out + dy) * CH
                    wt_ref[layer, dx, top : top + CH, out * CH : (out + 1) * CH] = block
    shape = w1_ref.shape
    row = lax.broadcasted_iota(jnp.int32, shape, 0)
    tall = rows + 8
    dx_at, dy_at = row // tall, row % tall - lax.broadcasted_iota(jnp.int32, shape, 1) // CH
    value = jnp.zeros(shape, jnp.float32)
    for dy in range(taps):
        for dx in range(taps):
            line = first_ref[dy * taps + dx : dy * taps + dx + 1, :]
            value = jnp.where((dx_at == dx) & (dy_at == dy), line, value)
    w1_ref[...] = value.astype(jnp.bfloat16)


def banded_weights(first_weight, conv_weights, rows):
    base = jnp.transpose(conv_weights, (0, 3, 4, 1, 2))
    lines = jnp.transpose(first_weight, (1, 2, 3, 0)).reshape(9, CH).astype(jnp.float32)
    lines = jnp.tile(lines, (1, rows + 6))
    vmem = pl.BlockSpec(memory_space=pltpu.VMEM)
    return pl.pallas_call(
        functools.partial(weights_kernel, rows),
        out_shape=(
            jax.ShapeDtypeStruct((base.shape[0], 3, 6 * CH, 4 * CH), jnp.bfloat16),
            jax.ShapeDtypeStruct((LANES, (rows + 6) * CH), jnp.bfloat16),
        ),
        in_specs=[vmem, vmem],
        out_specs=(vmem, vmem),
        compiler_params=pltpu.CompilerParams(vmem_limit_bytes=12 << 20),
        cost_estimate=pl.CostEstimate(flops=10_000_000, bytes_accessed=2_500_000, transcendentals=0),
    )(base, lines)


def neighbours(pair, weights, row_axis, strip_axis):
    groups, strips = lax.axis_size(row_axis), lax.axis_size(strip_axis)
    above = lax.ppermute(pair, row_axis, [(i, i + 1) for i in range(groups - 1)])
    below = lax.ppermute(pair, row_axis, [(i + 1, i) for i in range(groups - 1)])
    above, below, weights = lax.optimization_barrier((above, below, weights))
    own = jnp.concatenate([above, pair, below], axis=1)
    other = lax.ppermute(own, strip_axis, [(i, i ^ 1) for i in range(strips)])
    first = lax.axis_index(strip_axis) == 0
    return jnp.concatenate([jnp.where(first, own, other), jnp.where(first, other, own)], axis=2), weights


def stacked(image, start, length, flipped):
    part = lax.dynamic_slice_in_dim(image, start - 1, length + 2, 1)
    if flipped:
        part = lax.optimization_barrier(part[:, ::-1])
    shifts = [part[:, dx : dx + length] for dx in ((2, 1, 0) if flipped else (0, 1, 2))]
    joined = jnp.concatenate(shifts, axis=0)
    joined = jnp.pad(joined, ((0, LANES - joined.shape[0]), (0, 0)))
    return joined.T


def per_device(left_pixels, right_pixels, valid_mask, first_weight, conv_weights):
    rows, cols = left_pixels.shape
    groups, strips = lax.axis_size("rows"), lax.axis_size("strips")
    group, strip = lax.axis_index("rows"), lax.axis_index("strips")
    total_rows, total_cols = rows * groups, cols * strips

    wt, w1 = banded_weights(first_weight, conv_weights, rows)
    pair = jnp.stack([normalize(left_pixels), normalize(right_pixels)])
    band, (wt, w1) = neighbours(pair, (wt, w1), "rows", "strips")
    band = band[:, rows - 4 : 2 * rows + 4]
    left_length, right_length = plan(cols)[0], plan(cols + DISP)[0]
    margin = right_length + 8
    band = jnp.pad(band, ((0, 0), (0, 0), (margin, margin)))
    first_col = strip * cols
    left_stack = stacked(band[0], margin + first_col - 3 * EDGE, left_length, False)
    right_start = first_col + cols - 1 + 3 * EDGE - (right_length - 1)
    right_stack = stacked(band[1], margin + right_start, right_length, True)
    scale = -1.0 / math.sqrt(CH)
    mask = jnp.repeat((valid_mask.astype(jnp.float32) * scale).astype(jnp.bfloat16).T, CH, axis=1)
    place = jnp.stack([group * rows, first_col, strip]).astype(jnp.int32)

    per_group = cols // groups
    cost, off, *packed = cost_volume(
        left_stack, right_stack, mask, w1, wt, place, rows, cols, total_rows, total_cols, per_group
    )
    if packed:
        grouped = packed[0].reshape(groups, rows, per_group, DISP)
    else:
        centred = (cost - off[:, :, 0].reshape(rows, cols, 1)).astype(jnp.bfloat16)
        grouped = jnp.swapaxes(centred.reshape(rows, groups, per_group, DISP), 0, 1)
    columns = lax.all_to_all(grouped, "rows", split_axis=0, concat_axis=0, tiled=True)
    columns = columns.reshape(total_rows, per_group, DISP)

    zero = jnp.zeros((16, 8, LANES), jnp.float32)
    leading, end = row_scan(place, cost, zero, None, None, False)
    received = lax.ppermute(end, "strips", [(i, i ^ 1) for i in range(strips)])
    columns, _ = lax.optimization_barrier((columns, end))
    column_sum, received = lax.optimization_barrier((column_scan(columns), received))
    vertical = lax.all_to_all(
        column_sum.reshape(groups, rows, per_group, DISP), "rows", split_axis=0, concat_axis=0, tiled=True
    )
    horizontal, _ = row_scan(place, cost, received, leading, off, True)
    return add_vertical(horizontal, vertical)


def solution(mesh):
    in_specs = (P("rows", "strips"), P("rows", "strips"), P("rows", "strips"), P(), P())
    out_specs = P("rows", "strips", None)
    return jax.shard_map(
        per_device, mesh=mesh, in_specs=in_specs, out_specs=out_specs, check_vma=False
    )
```

```python
import functools
import math

import jax
import jax.numpy as jnp
from jax import lax
from jax.experimental import pallas as pl
from jax.experimental.pallas import tpu as pltpu
from jax.sharding import PartitionSpec as P

DISP = 128
P_SMALL = 0.5
P_LARGE = 2.0
BIG = 3.0e38
CH = 64
EDGE = 8
LANES = 128
BATCH = 2
PARTS = 1
SCAN_ROOM = 62_600_000
SUM_ROOM = 24 << 20


def over(x, n):
    return lax.shift_right_logical(x, n.bit_length() - 1) if n & (n - 1) == 0 else x // n


def within(x, n):
    return x & (n - 1) if n & (n - 1) == 0 else x % n


def plan(width):
    unit = 16 * PARTS
    totals = [-(-width // unit) * unit]
    for _ in range(3):
        totals.append(-(-(totals[-1] + 2 * EDGE) // unit) * unit)
    return totals[::-1]


def feature_stacks(stacks, w1_ref, wt_ref, row_low, row_high):
    def inside(test, base, count, lanes, halo, lane0):
        position = lax.broadcasted_iota(jnp.int32, (count, lanes), 0) + base
        row = over(lax.broadcasted_iota(jnp.int32, (count, lanes), 1) + lane0, CH) - halo
        return test(position) & (row >= row_low) & (row < row_high)

    def first(index, carry):
        for pix_ref, bufs, test, flipped in stacks:
            chunk = bufs[0].shape[0] // PARTS
            start = index * chunk
            value = jnp.dot(pix_ref[pl.ds(start, chunk), :], w1_ref[...], preferred_element_type=jnp.float32)
            keep = inside(test, start - 3 * EDGE, chunk, bufs[0].shape[1], 3, 0)
            bufs[0][pl.ds(start, chunk), :] = jnp.where(keep, jnp.maximum(value, 0.0), 0.0).astype(jnp.bfloat16)
        return carry

    for index in range(PARTS):
        first(index, 0)

    for layer in range(1, 4):

        def convolve(index, carry, layer=layer):
            halo = 3 - layer
            for pix_ref, bufs, test, flipped in stacks:
                source, target = bufs[layer - 1], bufs[layer]
                out_rows = target.shape[1] // CH
                chunk = target.shape[0] // PARTS
                reach = chunk + 2 * EDGE
                start = index * chunk
                for group in range(0, out_rows, 4):
                    count = min(4, out_rows - group)
                    wide, deep = count * CH, (count + 2) * CH
                    block = source[pl.ds(start, reach), group * CH : group * CH + deep]
                    parts = [
                        jnp.dot(block, wt_ref[layer - 1, dx, :deep, :wide], preferred_element_type=jnp.float32)
                        for dx in range(3)
                    ]
                    before, after = (parts[2], parts[0]) if flipped else (parts[0], parts[2])
                    value = pltpu.roll(before, 1, 0) + parts[1] + pltpu.roll(after, reach - 1, 0)
                    value = value[EDGE : EDGE + chunk]
                    if layer < 3:
                        value = jnp.maximum(value, 0.0)
                    keep = inside(test, start - halo * EDGE, chunk, wide, halo, group * CH)
                    value = jnp.where(keep, value, 0.0).astype(jnp.bfloat16)
                    target[pl.ds(start, chunk), group * CH : group * CH + wide] = value
            return carry

        for index in range(PARTS):
            convolve(index, 0)


def offsets(costs):
    even = jnp.full((DISP, DISP), 1.0 / DISP, jnp.bfloat16)
    return jnp.dot(costs.astype(jnp.bfloat16), even, preferred_element_type=jnp.float32)


def packs(per_group):
    return per_group % 16 == 0 and LANES % per_group == 0


def cost_kernel(dims, where_ref, left_ref, right_ref, mask_ref, w1_ref, wt_ref, cost_ref, *rest):
    rows, cols, total_rows, total_cols, per_group = dims
    payload_ref, rest = (rest[0], rest[1:]) if packs(per_group) else (None, rest)
    bufs = rest
    first_row, first_col = where_ref[0], where_ref[1]
    row_low, row_high = -first_row, total_rows - first_row
    left_bufs, right_bufs = bufs[:4], bufs[4:]

    def left_col(position):
        col = position + first_col
        return (col >= 0) & (col < total_cols)

    def right_col(position):
        col = first_col + cols - 1 - position
        return (col >= 0) & (col < total_cols)

    feature_stacks(
        [(left_ref, left_bufs, left_col, False), (right_ref, right_bufs, right_col, True)],
        w1_ref, wt_ref, row_low, row_high,
    )
    left, right = left_bufs[3], right_bufs[3]
    for row in range(rows):
        pair = row // 2 * LANES
        lane = lax.broadcasted_iota(jnp.int32, (LANES, LANES), 1)
        own = over(lane, CH) == row % 2

        for index in range(cols // LANES):
            start = index * LANES
            window = cols - LANES - start
            scale = mask_ref[start : start + LANES, pair : pair + LANES]
            a = jnp.where(own, left[start : start + LANES, pair : pair + LANES] * scale, jnp.zeros((), jnp.bfloat16))
            b = right[window : window + 2 * LANES, pair : pair + LANES]
            product = lax.dot_general(a, b, (((1,), (1,)), ((), ())), preferred_element_type=jnp.float32)
            skewed = pltpu.roll(product, LANES + 1, 1, stride=1, stride_axis=0)[:, :LANES]
            cost_ref[row, start : start + LANES, :] = skewed
            if payload_ref is not None:
                skewed = skewed - offsets(skewed)
                for k in range(LANES // per_group):
                    piece = skewed[k * per_group : (k + 1) * per_group].astype(jnp.bfloat16)
                    group = index * (LANES // per_group) + k
                    payload_ref[group, row * per_group : (row + 1) * per_group, :] = piece


def cost_volume(left_stack, right_stack, mask, w1, wt, place, rows, cols, total_rows, total_cols, per_group):
    bufs = []
    for width in (cols, cols + DISP):
        sizes = plan(width)
        for layer in range(4):
            out_rows = rows + 2 * (3 - layer)
            length = sizes[layer]
            bufs.append(pltpu.VMEM((length, out_rows * CH), jnp.bfloat16))
    vmem = pl.BlockSpec(memory_space=pltpu.VMEM)
    shapes = [jax.ShapeDtypeStruct((rows, cols, DISP), jnp.float32)]
    if packs(per_group):
        shapes.append(jax.ShapeDtypeStruct((cols // per_group, rows * per_group, DISP), jnp.bfloat16))
    return pl.pallas_call(
        functools.partial(cost_kernel, (rows, cols, total_rows, total_cols, per_group)),
        out_shape=tuple(shapes),
        in_specs=[pl.BlockSpec(memory_space=pltpu.SMEM)] + [vmem] * 5,
        out_specs=(vmem,) * len(shapes),
        scratch_shapes=bufs,
        compiler_params=pltpu.CompilerParams(vmem_limit_bytes=40 << 20),
        cost_estimate=pl.CostEstimate(flops=8_000_000_000, bytes_accessed=6_000_000, transcendentals=0),
    )(place, left_stack, right_stack, mask, w1, wt)


def row_scan_kernel(dims, has_sum, place_ref, cost_hbm, *rest):
    rows, cols, flip, batch = dims
    if has_sum:
        state_ref, lead_hbm, out_ref, end_ref, lead_ref, lead_sem, *rest = rest
    else:
        out_hbm, end_ref, out_ref, out_sems, *rest = rest
    cost_ref, cost_sems, tile_ref, turn_ref, pick_ref, split_a, split_b, even_ref, odd_ref, path_ref, low_ref = rest
    width = LANES // rows
    count = cols // width
    forward = place_ref[2] == (1 if flip else 0)
    lane = lax.broadcasted_iota(jnp.int32, (8, LANES), 1)
    sublane = lax.broadcasted_iota(jnp.int32, (8, LANES), 0)
    lane_col = within(lane, width)

    def copy_in(index):
        part = pl.ds(chunk_start(index), width)
        return pltpu.make_async_copy(cost_hbm.at[:, part], cost_ref.at[:, part], cost_sems.at[index])

    rounds = count // batch // 2
    early = max(rounds // 2 * 2 * batch - 1, 0)

    def copy_out(part):
        length = (early, count - early)[part] * width
        begin = jnp.where(forward, (0, early * width)[part], ((count - early) * width, 0)[part])
        cut = pl.ds(pl.multiple_of(begin, width), length)
        return pltpu.make_async_copy(out_ref.at[:, cut], out_hbm.at[:, cut], out_sems.at[part])

    def chunk_of(index):
        return jnp.where(forward, index, count - 1 - index)

    def chunk_start(index):
        return pl.multiple_of(chunk_of(index) * width, width)

    for index in range(count):
        copy_in(index).start()
    if has_sum:
        copy_lead = pltpu.make_async_copy(lead_hbm, lead_ref, lead_sem)
        copy_lead.start()

    def build_pick(pair, carry):
        k = within(lax.broadcasted_iota(jnp.int32, (2 * LANES, 2 * LANES), 0), LANES)
        n = lax.broadcasted_iota(jnp.int32, (2 * LANES, 2 * LANES), 1)
        wanted = over(within(n, LANES), width) * width + 2 * pair + over(n, LANES)
        pick_ref[pair] = jnp.where(k == wanted, 1.0, 0.0).astype(jnp.bfloat16)
        return carry

    lax.fori_loop(0, width // 2, build_pick, 0)

    def split(index, target):
        start = chunk_start(jnp.minimum(index, count - 1))
        tile = jnp.concatenate([cost_ref[row, pl.ds(start, width), :] for row in range(rows)], axis=0)
        tile_ref[...] = tile.T
        for v in range(0, 16, 2):
            plane = jnp.concatenate(
                [tile_ref[pl.ds(v, 8, stride=16), :], tile_ref[pl.ds(v + 1, 8, stride=16), :]], axis=0
            )
            high = plane.astype(jnp.bfloat16)
            low = (plane - high.astype(jnp.float32)).astype(jnp.bfloat16)
            target[v * 8 : v * 8 + 16, :LANES] = high
            target[v * 8 : v * 8 + 16, LANES:] = low

    def spread(source, target, pair):
        both = jnp.dot(source[...], pick_ref[pair], preferred_element_type=jnp.float32)
        for slot in range(batch):
            target[slot, 2 * pair] = both[slot * LANES : slot * LANES + LANES, :LANES]
            target[slot, 2 * pair + 1] = both[slot * LANES : slot * LANES + LANES, LANES:]

    def emit(index):
        start = chunk_start(jnp.maximum(index, 0))
        low = low_ref[...]
        for v in range(16):
            turn_ref[pl.ds(v, 8, stride=16), :] = path_ref[v] - low
        done = turn_ref[...].T
        tile = jnp.concatenate([cost_ref[row, pl.ds(start, width), :] for row in range(rows)], axis=0)
        done = done + offsets(tile)
        for row in range(rows):
            piece = done[row * width : (row + 1) * width]
            if has_sum:
                piece = piece + lead_ref[row, pl.ds(start, width), :]
            out_ref[row, pl.ds(start, width), :] = piece

    def advance(state, low, slot, step, current):
        col = jnp.where(forward, step, width - 1 - step)
        mask = lane_col == col
        bound = low + P_LARGE
        above = jnp.where(sublane == 7, BIG, pltpu.roll(state[0], 7, 0))
        below = jnp.where(sublane == 0, BIG, pltpu.roll(state[15], 1, 0))
        padded = [below] + list(state) + [above]
        fresh = []
        for v in range(16):
            near = jnp.minimum(padded[v], padded[v + 2]) + P_SMALL
            best = jnp.minimum(jnp.minimum(state[v], near), bound)
            value = current[slot, col, v * 8 : v * 8 + 8, :] + best
            pltpu.store(path_ref.at[v], value, mask=mask)
            fresh.append(value)
        pltpu.store(low_ref, low, mask=mask)
        return fresh

    def one_batch(number, state, current, coming, ready, filling):
        base = number * batch
        pairs = width // 2 // batch

        def one_chunk(slot, state):
            emit(base + slot - 1)
            split(base + 2 * batch + slot, filling.at[pl.ds(pl.multiple_of(slot * LANES, LANES), LANES)])
            low = lowest(state)
            state = [value - low for value in state]
            low = jnp.zeros_like(low)
            for step in range(width):
                if step % (2 * batch) == 0:
                    spread(ready, coming, slot * pairs + step // (2 * batch))
                if step:
                    low = lowest(state)
                state = advance(state, low, slot, step, current)
            return tuple(state)

        return lax.fori_loop(0, batch, one_chunk, state)

    for index in range(2 * batch):
        copy_in(index).wait()
    for slot in range(batch):
        split(slot, split_a.at[pl.ds(slot * LANES, LANES)])
        split(batch + slot, split_b.at[pl.ds(slot * LANES, LANES)])

    def first(group, carry):
        for k in range(4):
            spread(split_a, even_ref, group * 4 + k)
        return carry

    lax.fori_loop(0, width // 8, first, 0)

    for index in range(2 * batch, count):
        copy_in(index).wait()
    if has_sum:
        copy_lead.wait()

    def two_batches(index, state):
        state = one_batch(2 * index, state, even_ref, odd_ref, split_b, split_a)
        state = one_batch(2 * index + 1, state, odd_ref, even_ref, split_a, split_b)
        if not has_sum and early:

            @pl.when(index == rounds // 2 - 1)
            def _():
                copy_out(0).start()

        return state

    if has_sum:
        state = tuple(state_ref[v] for v in range(16))
    else:
        state = (jnp.zeros((8, LANES), jnp.float32),) * 16
    state = lax.fori_loop(0, rounds, two_batches, state)
    emit(count - 1)
    if not has_sum:
        copy_out(1).start()
    for v in range(16):
        end_ref[v] = state[v]
    if not has_sum:
        for part in range(2 if early else 1):
            copy_out(1 - part).wait()


def row_scan(place, cost, state, lead, flip):
    rows, cols, _ = cost.shape
    width = LANES // rows
    count = cols // width
    batch = math.gcd(count // 2, BATCH)
    vmem = pl.BlockSpec(memory_space=pltpu.VMEM)
    hbm = pl.BlockSpec(memory_space=pltpu.HBM)
    has_sum = lead is not None
    args = [place, cost] + ([state, lead] if has_sum else [])
    whole = pltpu.VMEM(cost.shape, jnp.float32)
    moved = [whole, pltpu.SemaphoreType.DMA(() if has_sum else (2,))]
    return pl.pallas_call(
        functools.partial(row_scan_kernel, (rows, cols, flip, batch), has_sum),
        out_shape=(
            jax.ShapeDtypeStruct(cost.shape, jnp.float32),
            jax.ShapeDtypeStruct((16, 8, LANES), jnp.float32),
        ),
        in_specs=[pl.BlockSpec(memory_space=pltpu.SMEM), hbm] + ([vmem, hbm] if has_sum else []),
        out_specs=(vmem if has_sum else hbm, vmem),
        scratch_shapes=moved
        + [
            whole,
            pltpu.SemaphoreType.DMA((count,)),
            pltpu.VMEM((LANES, LANES), jnp.float32),
            pltpu.VMEM((LANES, LANES), jnp.float32),
            pltpu.VMEM((width // 2, 2 * LANES, 2 * LANES), jnp.bfloat16),
            pltpu.VMEM((batch * LANES, 2 * LANES), jnp.bfloat16),
            pltpu.VMEM((batch * LANES, 2 * LANES), jnp.bfloat16),
            pltpu.VMEM((batch, width, LANES, LANES), jnp.float32),
            pltpu.VMEM((batch, width, LANES, LANES), jnp.float32),
            pltpu.VMEM((16, 8, LANES), jnp.float32),
            pltpu.VMEM((8, LANES), jnp.float32),
        ],
        compiler_params=pltpu.CompilerParams(vmem_limit_bytes=SUM_ROOM if has_sum else SCAN_ROOM),
        cost_estimate=pl.CostEstimate(flops=2_000_000_000, bytes_accessed=30_000_000, transcendentals=0),
    )(*args)


def column_kernel(cost_ref, out_ref, sum_ref):
    length, width, _ = cost_ref.shape
    lane = lax.broadcasted_iota(jnp.int32, (width, DISP), 1)

    def step(state, index):
        cost = cost_ref[index].astype(jnp.float32)
        low = jnp.min(state, axis=1, keepdims=True)
        above = jnp.where(lane == DISP - 1, BIG, pltpu.roll(state, DISP - 1, 1))
        below = jnp.where(lane == 0, BIG, pltpu.roll(state, 1, 1))
        near = jnp.minimum(above, below) + P_SMALL
        return cost + jnp.minimum(jnp.minimum(state, near), low + P_LARGE) - low

    def first(index, states):
        down = step(states[0], index)
        up = step(states[1], length - 1 - index)
        sum_ref[index] = down
        sum_ref[length - 1 - index] = up
        return down, up

    def second(index, states):
        down = step(states[0], index)
        up = step(states[1], length - 1 - index)
        out_ref[index] = (sum_ref[index] + down).astype(jnp.bfloat16)
        out_ref[length - 1 - index] = (sum_ref[length - 1 - index] + up).astype(jnp.bfloat16)
        return down, up

    zero = jnp.zeros((width, DISP), jnp.float32)
    states = lax.fori_loop(0, length // 2, first, (zero, zero))
    lax.fori_loop(length // 2, length, second, states)


def lowest(state):
    level = list(state)
    while len(level) > 1:
        level = [jnp.minimum(level[i], level[i + 1]) for i in range(0, len(level), 2)]
    low = level[0]
    for shift in (4, 2, 1):
        low = jnp.minimum(low, pltpu.roll(low, shift, 0))
    return low


def column_tiles_kernel(cost_ref, out_ref, tile_ref, split_ref, spread_ref, path_ref, turn_ref, sum_ref):
    length, width, _ = cost_ref.shape
    both = 2 * width
    per = LANES // both
    tiles = length // per
    sublane = lax.broadcasted_iota(jnp.int32, (8, LANES), 0)
    lane_step = over(lax.broadcasted_iota(jnp.int32, (8, LANES), 1), both)
    k = lax.broadcasted_iota(jnp.int32, (LANES, per * LANES), 0)
    n = lax.broadcasted_iota(jnp.int32, (LANES, per * LANES), 1)
    pick = jnp.where(k == over(n, LANES) * both + within(n, both), 1.0, 0.0).astype(jnp.bfloat16)

    def places(tile):
        rows = []
        for step in range(per):
            rows += [tile * per + step, length - 1 - (tile * per + step)]
        return rows

    def prepare(index, carry):
        for slot in range(8):
            tile = index * 8 + slot
            block = jnp.concatenate([cost_ref[row] for row in places(tile)], axis=0)
            tile_ref[slot] = block.astype(jnp.float32).T
            for v in range(0, 16, 2):
                plane = jnp.concatenate(
                    [tile_ref[slot, pl.ds(v, 8, stride=16), :], tile_ref[slot, pl.ds(v + 1, 8, stride=16), :]], axis=0
                )
                split_ref[slot * LANES + v * 8 : slot * LANES + v * 8 + 16, :] = plane.astype(jnp.bfloat16)
        spread = jnp.dot(split_ref[...], pick, preferred_element_type=jnp.float32)
        for slot in range(8):
            for step in range(per):
                spread_ref[index * 8 + slot, step] = spread[
                    slot * LANES : slot * LANES + LANES, step * LANES : step * LANES + LANES
                ]
        return carry

    lax.fori_loop(0, tiles // 8, prepare, 0)

    def emit(tile, last):
        tile = jnp.maximum(tile, 0)
        for v in range(16):
            turn_ref[pl.ds(v, 8, stride=16), :] = path_ref[v]
        done = turn_ref[...].T
        for i, row in enumerate(places(tile)):
            piece = done[i * width : (i + 1) * width]
            if last:
                out_ref[row] = (sum_ref[row] + piece).astype(jnp.bfloat16)
            else:
                sum_ref[row] = piece

    def run(tile, state, last):
        emit(tile - 1, last)
        state = list(state)
        for step in range(per):
            low = lowest(state)
            bound = low + P_LARGE
            above = jnp.where(sublane == 7, BIG, pltpu.roll(state[0], 7, 0))
            below = jnp.where(sublane == 0, BIG, pltpu.roll(state[15], 1, 0))
            padded = [below] + state + [above]
            fresh = []
            for v in range(16):
                near = jnp.minimum(padded[v], padded[v + 2]) + P_SMALL
                best = jnp.minimum(jnp.minimum(state[v], near), bound)
                value = spread_ref[tile, step, v * 8 : v * 8 + 8, :] + (best - low)
                if step:
                    pltpu.store(path_ref.at[v], value, mask=lane_step == step)
                else:
                    path_ref[v] = value
                fresh.append(value)
            state = fresh
        return tuple(state)

    def loop(begin, end, state, last):
        return lax.fori_loop(begin, end, lambda tile, carry: run(tile, carry, last), state, unroll=8)

    state = (jnp.zeros((8, LANES), jnp.float32),) * 16
    state = loop(0, tiles // 2, state, False)
    emit(tiles // 2 - 1, False)
    state = loop(tiles // 2, tiles, state, True)
    emit(tiles - 1, True)


def column_scan(columns):
    length, width, _ = columns.shape
    vmem = pl.BlockSpec(memory_space=pltpu.VMEM)
    scratch = [pltpu.VMEM(columns.shape, jnp.float32)]
    kernel = column_kernel
    per = LANES // (2 * width)
    if width % 16 == 0 and LANES % (2 * width) == 0 and length % (16 * per) == 0:
        kernel = column_tiles_kernel
        scratch = [
            pltpu.VMEM((8, LANES, LANES), jnp.float32),
            pltpu.VMEM((8 * LANES, LANES), jnp.bfloat16),
            pltpu.VMEM((length // per, per, LANES, LANES), jnp.float32),
            pltpu.VMEM((16, 8, LANES), jnp.float32),
            pltpu.VMEM((LANES, LANES), jnp.float32),
        ] + scratch
    return pl.pallas_call(
        kernel,
        out_shape=jax.ShapeDtypeStruct(columns.shape, jnp.bfloat16),
        in_specs=[vmem],
        out_specs=vmem,
        scratch_shapes=scratch,
        compiler_params=pltpu.CompilerParams(vmem_limit_bytes=20 << 20),
        cost_estimate=pl.CostEstimate(flops=200_000_000, bytes_accessed=2_000_000, transcendentals=0),
    )(columns)


def add_kernel(across_ref, down_ref, out_ref):
    rows, cols, _ = across_ref.shape
    for row in range(rows):
        out_ref[row] = across_ref[row] + down_ref[:, row].reshape(cols, DISP).astype(jnp.float32)


def add_vertical(horizontal, vertical):
    rows, cols, _ = horizontal.shape
    if not packs(vertical.shape[2]):
        return horizontal + jnp.swapaxes(vertical, 0, 1).reshape(rows, cols, DISP).astype(jnp.float32)
    vmem = pl.BlockSpec(memory_space=pltpu.VMEM)
    return pl.pallas_call(
        add_kernel,
        out_shape=jax.ShapeDtypeStruct(horizontal.shape, jnp.float32),
        in_specs=[vmem, vmem],
        out_specs=vmem,
        compiler_params=pltpu.CompilerParams(vmem_limit_bytes=8 << 20),
        cost_estimate=pl.CostEstimate(flops=300_000, bytes_accessed=2_600_000, transcendentals=0),
    )(horizontal, vertical)


def normalize(image_pixels):
    return (image_pixels.astype(jnp.float32) / 1024.0 - 2.0).astype(jnp.bfloat16)


def weights_kernel(rows, base_ref, first_ref, wt_ref, w1_ref):
    wt_ref[...] = jnp.zeros_like(wt_ref)
    layers, taps = base_ref.shape[0], base_ref.shape[1]
    for layer in range(layers):
        for dy in range(taps):
            for dx in range(taps):
                block = base_ref[layer, dy, dx].astype(jnp.float32).T.astype(jnp.bfloat16)
                for out in range(wt_ref.shape[3] // CH):
                    top = (out + dy) * CH
                    wt_ref[layer, dx, top : top + CH, out * CH : (out + 1) * CH] = block
    shape = w1_ref.shape
    row = lax.broadcasted_iota(jnp.int32, shape, 0)
    tall = rows + 8
    column = over(lax.broadcasted_iota(jnp.int32, shape, 1), CH)
    value = jnp.zeros(shape, jnp.float32)
    for dy in range(taps):
        for dx in range(taps):
            line = first_ref[dy * taps + dx : dy * taps + dx + 1, :]
            value = jnp.where((row - dx * tall - column == dy) & (row >= dx * tall) & (row < (dx + 1) * tall), line, value)
    w1_ref[...] = value.astype(jnp.bfloat16)


def banded_weights(first_weight, conv_weights, rows):
    base = jnp.transpose(conv_weights, (0, 3, 4, 1, 2))
    lines = jnp.transpose(first_weight, (1, 2, 3, 0)).reshape(9, CH).astype(jnp.float32)
    lines = jnp.tile(lines, (1, rows + 6))
    vmem = pl.BlockSpec(memory_space=pltpu.VMEM)
    return pl.pallas_call(
        functools.partial(weights_kernel, rows),
        out_shape=(
            jax.ShapeDtypeStruct((base.shape[0], 3, 6 * CH, 4 * CH), jnp.bfloat16),
            jax.ShapeDtypeStruct((LANES, (rows + 6) * CH), jnp.bfloat16),
        ),
        in_specs=[vmem, vmem],
        out_specs=(vmem, vmem),
        compiler_params=pltpu.CompilerParams(vmem_limit_bytes=12 << 20),
        cost_estimate=pl.CostEstimate(flops=10_000_000, bytes_accessed=2_500_000, transcendentals=0),
    )(base, lines)


def neighbours(pair, weights, row_axis, strip_axis):
    groups, strips = lax.axis_size(row_axis), lax.axis_size(strip_axis)
    above = lax.ppermute(pair, row_axis, [(i, i + 1) for i in range(groups - 1)])
    below = lax.ppermute(pair, row_axis, [(i + 1, i) for i in range(groups - 1)])
    above, below, weights = lax.optimization_barrier((above, below, weights))
    own = jnp.concatenate([above, pair, below], axis=1)
    other = lax.ppermute(own, strip_axis, [(i, i ^ 1) for i in range(strips)])
    first = lax.axis_index(strip_axis) == 0
    return jnp.concatenate([jnp.where(first, own, other), jnp.where(first, other, own)], axis=2), weights


def stacked(image, start, length, flipped):
    part = lax.dynamic_slice_in_dim(image, start - 1, length + 2, 1)
    if flipped:
        part = lax.optimization_barrier(part[:, ::-1])
    shifts = [part[:, dx : dx + length] for dx in ((2, 1, 0) if flipped else (0, 1, 2))]
    joined = jnp.concatenate(shifts, axis=0)
    joined = jnp.pad(joined, ((0, LANES - joined.shape[0]), (0, 0)))
    return joined.T


def per_device(left_pixels, right_pixels, valid_mask, first_weight, conv_weights):
    rows, cols = left_pixels.shape
    groups, strips = lax.axis_size("rows"), lax.axis_size("strips")
    group, strip = lax.axis_index("rows"), lax.axis_index("strips")
    total_rows, total_cols = rows * groups, cols * strips

    wt, w1 = banded_weights(first_weight, conv_weights, rows)
    pair = jnp.stack([normalize(left_pixels), normalize(right_pixels)])
    band, (wt, w1) = neighbours(pair, (wt, w1), "rows", "strips")
    band = band[:, rows - 4 : 2 * rows + 4]
    left_length, right_length = plan(cols)[0], plan(cols + DISP)[0]
    margin = right_length + 8
    band = jnp.pad(band, ((0, 0), (0, 0), (margin, margin)))
    first_col = strip * cols
    left_stack = stacked(band[0], margin + first_col - 3 * EDGE, left_length, False)
    right_start = first_col + cols - 1 + 3 * EDGE - (right_length - 1)
    right_stack = stacked(band[1], margin + right_start, right_length, True)
    scale = -1.0 / math.sqrt(CH)
    mask = jnp.repeat((valid_mask.astype(jnp.float32) * scale).astype(jnp.bfloat16).T, CH, axis=1)
    place = jnp.stack([group * rows, first_col, strip]).astype(jnp.int32)

    per_group = cols // groups
    cost, *packed = cost_volume(
        left_stack, right_stack, mask, w1, wt, place, rows, cols, total_rows, total_cols, per_group
    )
    if packed:
        grouped = packed[0].reshape(groups, rows, per_group, DISP)
    else:
        centred = (cost - offsets(cost.reshape(-1, DISP)).reshape(cost.shape)).astype(jnp.bfloat16)
        grouped = jnp.swapaxes(centred.reshape(rows, groups, per_group, DISP), 0, 1)
    columns = lax.all_to_all(grouped, "rows", split_axis=0, concat_axis=0, tiled=True)
    columns = columns.reshape(total_rows, per_group, DISP)

    leading, end = row_scan(place, cost, None, None, False)
    received = lax.ppermute(end, "strips", [(i, i ^ 1) for i in range(strips)])
    columns, _ = lax.optimization_barrier((columns, end))
    column_sum, received = lax.optimization_barrier((column_scan(columns), received))
    vertical = lax.all_to_all(
        column_sum.reshape(groups, rows, per_group, DISP), "rows", split_axis=0, concat_axis=0, tiled=True
    )
    horizontal, _ = row_scan(place, cost, received, leading, True)
    return add_vertical(horizontal, vertical)


def solution(mesh):
    in_specs = (P("rows", "strips"), P("rows", "strips"), P("rows", "strips"), P(), P())
    out_specs = P("rows", "strips", None)
    return jax.shard_map(
        per_device, mesh=mesh, in_specs=in_specs, out_specs=out_specs, check_vma=False
    )
```

```python
import functools
import math

import jax
import jax.numpy as jnp
from jax import lax
from jax.experimental import pallas as pl
from jax.experimental.pallas import tpu as pltpu
from jax.sharding import PartitionSpec as P

DISP = 128
P_SMALL = 0.5
P_LARGE = 2.0
BIG = 3.0e38
CH = 64
EDGE = 8
LANES = 128
BATCH = 2
PARTS = 1
SCAN_ROOM = 62_600_000
SUM_ROOM = 24 << 20


def over(x, n):
    return lax.shift_right_logical(x, n.bit_length() - 1) if n & (n - 1) == 0 else x // n


def within(x, n):
    return x & (n - 1) if n & (n - 1) == 0 else x % n


def plan(width):
    unit = 16 * PARTS
    totals = [-(-width // unit) * unit]
    for _ in range(3):
        totals.append(-(-(totals[-1] + 2 * EDGE) // unit) * unit)
    return totals[::-1]


def feature_stacks(stacks, w1_ref, wt_ref, row_low, row_high):
    def inside(test, base, count, lanes, halo, lane0):
        position = lax.broadcasted_iota(jnp.int32, (count, lanes), 0) + base
        row = over(lax.broadcasted_iota(jnp.int32, (count, lanes), 1) + lane0, CH) - halo
        return test(position) & (row >= row_low) & (row < row_high)

    def first(index, carry):
        for pix_ref, bufs, test, flipped in stacks:
            chunk = bufs[0].shape[0] // PARTS
            start = index * chunk
            value = jnp.dot(pix_ref[pl.ds(start, chunk), :], w1_ref[...], preferred_element_type=jnp.float32)
            keep = inside(test, start - 3 * EDGE, chunk, bufs[0].shape[1], 3, 0)
            bufs[0][pl.ds(start, chunk), :] = jnp.where(keep, jnp.maximum(value, 0.0), 0.0).astype(jnp.bfloat16)
        return carry

    for index in range(PARTS):
        first(index, 0)

    for layer in range(1, 4):

        def convolve(index, carry, layer=layer):
            halo = 3 - layer
            for pix_ref, bufs, test, flipped in stacks:
                source, target = bufs[layer - 1], bufs[layer]
                out_rows = target.shape[1] // CH
                chunk = target.shape[0] // PARTS
                reach = chunk + 2 * EDGE
                start = index * chunk
                for group in range(0, out_rows, 4):
                    count = min(4, out_rows - group)
                    wide, deep = count * CH, (count + 2) * CH
                    block = source[pl.ds(start, reach), group * CH : group * CH + deep]
                    parts = [
                        jnp.dot(block, wt_ref[layer - 1, dx, :deep, :wide], preferred_element_type=jnp.float32)
                        for dx in range(3)
                    ]
                    before, after = (parts[2], parts[0]) if flipped else (parts[0], parts[2])
                    value = pltpu.roll(before, 1, 0) + parts[1] + pltpu.roll(after, reach - 1, 0)
                    value = value[EDGE : EDGE + chunk]
                    if layer < 3:
                        value = jnp.maximum(value, 0.0)
                    keep = inside(test, start - halo * EDGE, chunk, wide, halo, group * CH)
                    value = jnp.where(keep, value, 0.0).astype(jnp.bfloat16)
                    target[pl.ds(start, chunk), group * CH : group * CH + wide] = value
            return carry

        for index in range(PARTS):
            convolve(index, 0)


def offsets(costs):
    even = jnp.full((DISP, DISP), 1.0 / DISP, jnp.bfloat16)
    return jnp.dot(costs.astype(jnp.bfloat16), even, preferred_element_type=jnp.float32)


def packs(per_group):
    return per_group % 16 == 0 and LANES % per_group == 0


def cost_kernel(dims, where_ref, left_ref, right_ref, mask_ref, w1_ref, wt_ref, cost_ref, *rest):
    rows, cols, total_rows, total_cols, per_group = dims
    payload_ref, rest = (rest[0], rest[1:]) if packs(per_group) else (None, rest)
    bufs = rest
    first_row, first_col = where_ref[0], where_ref[1]
    row_low, row_high = -first_row, total_rows - first_row
    left_bufs, right_bufs = bufs[:4], bufs[4:]

    def left_col(position):
        col = position + first_col
        return (col >= 0) & (col < total_cols)

    def right_col(position):
        col = first_col + cols - 1 - position
        return (col >= 0) & (col < total_cols)

    feature_stacks(
        [(left_ref, left_bufs, left_col, False), (right_ref, right_bufs, right_col, True)],
        w1_ref, wt_ref, row_low, row_high,
    )
    left, right = left_bufs[3], right_bufs[3]
    for row in range(rows):
        pair = row // 2 * LANES
        lane = lax.broadcasted_iota(jnp.int32, (LANES, LANES), 1)
        own = over(lane, CH) == row % 2

        for index in range(cols // LANES):
            start = index * LANES
            window = cols - LANES - start
            scale = mask_ref[start : start + LANES, pair : pair + LANES]
            a = jnp.where(own, left[start : start + LANES, pair : pair + LANES] * scale, jnp.zeros((), jnp.bfloat16))
            b = right[window : window + 2 * LANES, pair : pair + LANES]
            product = lax.dot_general(a, b, (((1,), (1,)), ((), ())), preferred_element_type=jnp.float32)
            skewed = pltpu.roll(product, LANES + 1, 1, stride=1, stride_axis=0)[:, :LANES]
            cost_ref[row, start : start + LANES, :] = skewed
            if payload_ref is not None:
                skewed = skewed - offsets(skewed)
                for k in range(LANES // per_group):
                    piece = skewed[k * per_group : (k + 1) * per_group].astype(jnp.bfloat16)
                    group = index * (LANES // per_group) + k
                    payload_ref[group, row * per_group : (row + 1) * per_group, :] = piece


def cost_volume(left_stack, right_stack, mask, w1, wt, place, rows, cols, total_rows, total_cols, per_group):
    bufs = []
    for width in (cols, cols + DISP):
        sizes = plan(width)
        for layer in range(4):
            out_rows = rows + 2 * (3 - layer)
            length = sizes[layer]
            bufs.append(pltpu.VMEM((length, out_rows * CH), jnp.bfloat16))
    vmem = pl.BlockSpec(memory_space=pltpu.VMEM)
    shapes = [jax.ShapeDtypeStruct((rows, cols, DISP), jnp.float32)]
    if packs(per_group):
        shapes.append(jax.ShapeDtypeStruct((cols // per_group, rows * per_group, DISP), jnp.bfloat16))
    return pl.pallas_call(
        functools.partial(cost_kernel, (rows, cols, total_rows, total_cols, per_group)),
        out_shape=tuple(shapes),
        in_specs=[pl.BlockSpec(memory_space=pltpu.SMEM)] + [vmem] * 5,
        out_specs=(vmem,) * len(shapes),
        scratch_shapes=bufs,
        compiler_params=pltpu.CompilerParams(vmem_limit_bytes=40 << 20),
        cost_estimate=pl.CostEstimate(flops=8_000_000_000, bytes_accessed=6_000_000, transcendentals=0),
    )(place, left_stack, right_stack, mask, w1, wt)


def row_scan_kernel(dims, has_sum, place_ref, cost_hbm, *rest):
    rows, cols, flip, batch = dims
    if has_sum:
        state_ref, lead_hbm, out_ref, end_ref, lead_ref, lead_sem, *rest = rest
    else:
        out_hbm, end_ref, out_ref, out_sems, *rest = rest
    cost_ref, cost_sems, tile_ref, turn_ref, pick_ref, split_a, split_b, even_ref, odd_ref, path_ref, low_ref = rest
    width = LANES // rows
    count = cols // width
    forward = place_ref[2] == (1 if flip else 0)
    lane = lax.broadcasted_iota(jnp.int32, (8, LANES), 1)
    sublane = lax.broadcasted_iota(jnp.int32, (8, LANES), 0)
    lane_col = within(lane, width)

    def copy_in(index):
        part = pl.ds(chunk_start(index), width)
        return pltpu.make_async_copy(cost_hbm.at[:, part], cost_ref.at[:, part], cost_sems.at[index])

    rounds = count // batch // 2
    early = max(rounds // 2 * 2 * batch - 1, 0)

    def copy_out(part):
        length = (early, count - early)[part] * width
        begin = jnp.where(forward, (0, early * width)[part], ((count - early) * width, 0)[part])
        cut = pl.ds(pl.multiple_of(begin, width), length)
        return pltpu.make_async_copy(out_ref.at[:, cut], out_hbm.at[:, cut], out_sems.at[part])

    def chunk_of(index):
        return jnp.where(forward, index, count - 1 - index)

    def chunk_start(index):
        return pl.multiple_of(chunk_of(index) * width, width)

    for index in range(count):
        copy_in(index).start()
    if has_sum:
        copy_lead = pltpu.make_async_copy(lead_hbm, lead_ref, lead_sem)
        copy_lead.start()

    def build_pick(pair, carry):
        k = within(lax.broadcasted_iota(jnp.int32, (2 * LANES, 2 * LANES), 0), LANES)
        n = lax.broadcasted_iota(jnp.int32, (2 * LANES, 2 * LANES), 1)
        wanted = over(within(n, LANES), width) * width + 2 * pair + over(n, LANES)
        pick_ref[pair] = jnp.where(k == wanted, 1.0, 0.0).astype(jnp.bfloat16)
        return carry

    lax.fori_loop(0, width // 2, build_pick, 0)

    def split(index, target):
        start = chunk_start(jnp.minimum(index, count - 1))
        tile = jnp.concatenate([cost_ref[row, pl.ds(start, width), :] for row in range(rows)], axis=0)
        tile_ref[...] = tile.T
        for v in range(0, 16, 2):
            plane = jnp.concatenate(
                [tile_ref[pl.ds(v, 8, stride=16), :], tile_ref[pl.ds(v + 1, 8, stride=16), :]], axis=0
            )
            high = plane.astype(jnp.bfloat16)
            low = (plane - high.astype(jnp.float32)).astype(jnp.bfloat16)
            target[v * 8 : v * 8 + 16, :LANES] = high
            target[v * 8 : v * 8 + 16, LANES:] = low

    def spread(source, target, pair):
        both = jnp.dot(source[...], pick_ref[pair], preferred_element_type=jnp.float32)
        for slot in range(batch):
            target[slot, 2 * pair] = both[slot * LANES : slot * LANES + LANES, :LANES]
            target[slot, 2 * pair + 1] = both[slot * LANES : slot * LANES + LANES, LANES:]

    def emit(index):
        start = chunk_start(jnp.maximum(index, 0))
        low = low_ref[...]
        for v in range(16):
            turn_ref[pl.ds(v, 8, stride=16), :] = path_ref[v] - low
        done = turn_ref[...].T
        tile = jnp.concatenate([cost_ref[row, pl.ds(start, width), :] for row in range(rows)], axis=0)
        done = done + offsets(tile)
        for row in range(rows):
            piece = done[row * width : (row + 1) * width]
            if has_sum:
                piece = piece + lead_ref[row, pl.ds(start, width), :]
            out_ref[row, pl.ds(start, width), :] = piece

    def advance(state, low, slot, step, current):
        col = jnp.where(forward, step, width - 1 - step)
        mask = lane_col == col
        bound = low + P_LARGE
        above = jnp.where(sublane == 7, BIG, pltpu.roll(state[0], 7, 0))
        below = jnp.where(sublane == 0, BIG, pltpu.roll(state[15], 1, 0))
        padded = [below] + list(state) + [above]
        fresh = []
        for v in range(16):
            near = jnp.minimum(padded[v], padded[v + 2]) + P_SMALL
            best = jnp.minimum(jnp.minimum(state[v], near), bound)
            value = current[slot, col, v * 8 : v * 8 + 8, :] + best
            pltpu.store(path_ref.at[v], value, mask=mask)
            fresh.append(value)
        pltpu.store(low_ref, low, mask=mask)
        return fresh

    def one_batch(number, state, current, coming, ready, filling):
        base = number * batch
        pairs = width // 2 // batch

        def one_chunk(slot, state):
            emit(base + slot - 1)
            split(base + 2 * batch + slot, filling.at[pl.ds(pl.multiple_of(slot * LANES, LANES), LANES)])
            low = lowest(state)
            state = [value - low for value in state]
            low = jnp.zeros_like(low)
            for step in range(width):
                if step % (2 * batch) == 0:
                    spread(ready, coming, slot * pairs + step // (2 * batch))
                if step:
                    low = lowest(state)
                state = advance(state, low, slot, step, current)
            return tuple(state)

        return lax.fori_loop(0, batch, one_chunk, state)

    for index in range(2 * batch):
        copy_in(index).wait()
    for slot in range(batch):
        split(slot, split_a.at[pl.ds(slot * LANES, LANES)])
        split(batch + slot, split_b.at[pl.ds(slot * LANES, LANES)])

    def first(group, carry):
        for k in range(4):
            spread(split_a, even_ref, group * 4 + k)
        return carry

    lax.fori_loop(0, width // 8, first, 0)

    for index in range(2 * batch, count):
        copy_in(index).wait()
    if has_sum:
        copy_lead.wait()

    def two_batches(index, state):
        state = one_batch(2 * index, state, even_ref, odd_ref, split_b, split_a)
        state = one_batch(2 * index + 1, state, odd_ref, even_ref, split_a, split_b)
        if not has_sum and early:

            @pl.when(index == rounds // 2 - 1)
            def _():
                copy_out(0).start()

        return state

    if has_sum:
        state = tuple(state_ref[v] for v in range(16))
    else:
        state = (jnp.zeros((8, LANES), jnp.float32),) * 16
    state = lax.fori_loop(0, rounds, two_batches, state)
    emit(count - 1)
    if not has_sum:
        copy_out(1).start()
    for v in range(16):
        end_ref[v] = state[v]
    if not has_sum:
        for part in range(2 if early else 1):
            copy_out(1 - part).wait()


def row_scan(place, cost, state, lead, flip):
    rows, cols, _ = cost.shape
    width = LANES // rows
    count = cols // width
    batch = math.gcd(count // 2, BATCH)
    vmem = pl.BlockSpec(memory_space=pltpu.VMEM)
    hbm = pl.BlockSpec(memory_space=pltpu.HBM)
    has_sum = lead is not None
    args = [place, cost] + ([state, lead] if has_sum else [])
    whole = pltpu.VMEM(cost.shape, jnp.float32)
    moved = [whole, pltpu.SemaphoreType.DMA(() if has_sum else (2,))]
    return pl.pallas_call(
        functools.partial(row_scan_kernel, (rows, cols, flip, batch), has_sum),
        out_shape=(
            jax.ShapeDtypeStruct(cost.shape, jnp.float32),
            jax.ShapeDtypeStruct((16, 8, LANES), jnp.float32),
        ),
        in_specs=[pl.BlockSpec(memory_space=pltpu.SMEM), hbm] + ([vmem, hbm] if has_sum else []),
        out_specs=(vmem if has_sum else hbm, vmem),
        scratch_shapes=moved
        + [
            whole,
            pltpu.SemaphoreType.DMA((count,)),
            pltpu.VMEM((LANES, LANES), jnp.float32),
            pltpu.VMEM((LANES, LANES), jnp.float32),
            pltpu.VMEM((width // 2, 2 * LANES, 2 * LANES), jnp.bfloat16),
            pltpu.VMEM((batch * LANES, 2 * LANES), jnp.bfloat16),
            pltpu.VMEM((batch * LANES, 2 * LANES), jnp.bfloat16),
            pltpu.VMEM((batch, width, LANES, LANES), jnp.float32),
            pltpu.VMEM((batch, width, LANES, LANES), jnp.float32),
            pltpu.VMEM((16, 8, LANES), jnp.float32),
            pltpu.VMEM((8, LANES), jnp.float32),
        ],
        compiler_params=pltpu.CompilerParams(vmem_limit_bytes=SUM_ROOM if has_sum else SCAN_ROOM),
        cost_estimate=pl.CostEstimate(flops=2_000_000_000, bytes_accessed=30_000_000, transcendentals=0),
    )(*args)


def column_kernel(cost_ref, out_ref, sum_ref):
    length, width, _ = cost_ref.shape
    lane = lax.broadcasted_iota(jnp.int32, (width, DISP), 1)

    def step(state, index):
        cost = cost_ref[index].astype(jnp.float32)
        low = jnp.min(state, axis=1, keepdims=True)
        above = jnp.where(lane == DISP - 1, BIG, pltpu.roll(state, DISP - 1, 1))
        below = jnp.where(lane == 0, BIG, pltpu.roll(state, 1, 1))
        near = jnp.minimum(above, below) + P_SMALL
        return cost + jnp.minimum(jnp.minimum(state, near), low + P_LARGE) - low

    def first(index, states):
        down = step(states[0], index)
        up = step(states[1], length - 1 - index)
        sum_ref[index] = down
        sum_ref[length - 1 - index] = up
        return down, up

    def second(index, states):
        down = step(states[0], index)
        up = step(states[1], length - 1 - index)
        out_ref[index] = (sum_ref[index] + down).astype(jnp.bfloat16)
        out_ref[length - 1 - index] = (sum_ref[length - 1 - index] + up).astype(jnp.bfloat16)
        return down, up

    zero = jnp.zeros((width, DISP), jnp.float32)
    states = lax.fori_loop(0, length // 2, first, (zero, zero))
    lax.fori_loop(length // 2, length, second, states)


def lowest(state):
    level = list(state)
    while len(level) > 1:
        level = [jnp.minimum(level[i], level[i + 1]) for i in range(0, len(level), 2)]
    low = level[0]
    for shift in (4, 2, 1):
        low = jnp.minimum(low, pltpu.roll(low, shift, 0))
    return low


def column_tiles_kernel(cost_ref, out_ref, tile_ref, split_ref, spread_ref, path_ref, turn_ref, sum_ref):
    length, width, _ = cost_ref.shape
    both = 2 * width
    per = LANES // both
    tiles = length // per
    sublane = lax.broadcasted_iota(jnp.int32, (8, LANES), 0)
    lane_step = over(lax.broadcasted_iota(jnp.int32, (8, LANES), 1), both)
    k = lax.broadcasted_iota(jnp.int32, (LANES, per * LANES), 0)
    n = lax.broadcasted_iota(jnp.int32, (LANES, per * LANES), 1)
    pick = jnp.where(k == over(n, LANES) * both + within(n, both), 1.0, 0.0).astype(jnp.bfloat16)

    def places(tile):
        rows = []
        for step in range(per):
            rows += [tile * per + step, length - 1 - (tile * per + step)]
        return rows

    def prepare(index, carry):
        for slot in range(16):
            tile = index * 16 + slot
            block = jnp.concatenate([cost_ref[row] for row in places(tile)], axis=0)
            tile_ref[slot] = block.astype(jnp.float32).T
            for v in range(0, 16, 2):
                plane = jnp.concatenate(
                    [tile_ref[slot, pl.ds(v, 8, stride=16), :], tile_ref[slot, pl.ds(v + 1, 8, stride=16), :]], axis=0
                )
                split_ref[slot * LANES + v * 8 : slot * LANES + v * 8 + 16, :] = plane.astype(jnp.bfloat16)
        spread = jnp.dot(split_ref[...], pick, preferred_element_type=jnp.float32)
        for slot in range(16):
            for step in range(per):
                spread_ref[index * 16 + slot, step] = spread[
                    slot * LANES : slot * LANES + LANES, step * LANES : step * LANES + LANES
                ]
        return carry

    lax.fori_loop(0, tiles // 16, prepare, 0)

    def emit(tile, last):
        tile = jnp.maximum(tile, 0)
        for v in range(16):
            turn_ref[pl.ds(v, 8, stride=16), :] = path_ref[v]
        done = turn_ref[...].T
        for i, row in enumerate(places(tile)):
            piece = done[i * width : (i + 1) * width]
            if last:
                out_ref[row] = (sum_ref[row] + piece).astype(jnp.bfloat16)
            else:
                sum_ref[row] = piece

    def run(tile, state, last):
        emit(tile - 1, last)
        state = list(state)
        for step in range(per):
            low = lowest(state)
            bound = low + P_LARGE
            above = jnp.where(sublane == 7, BIG, pltpu.roll(state[0], 7, 0))
            below = jnp.where(sublane == 0, BIG, pltpu.roll(state[15], 1, 0))
            padded = [below] + state + [above]
            fresh = []
            for v in range(16):
                near = jnp.minimum(padded[v], padded[v + 2]) + P_SMALL
                best = jnp.minimum(jnp.minimum(state[v], near), bound)
                value = spread_ref[tile, step, v * 8 : v * 8 + 8, :] + (best - low)
                if step:
                    pltpu.store(path_ref.at[v], value, mask=lane_step == step)
                else:
                    path_ref[v] = value
                fresh.append(value)
            state = fresh
        return tuple(state)

    def loop(begin, end, state, last):
        return lax.fori_loop(begin, end, lambda tile, carry: run(tile, carry, last), state, unroll=16)

    state = (jnp.zeros((8, LANES), jnp.float32),) * 16
    state = loop(0, tiles // 2, state, False)
    emit(tiles // 2 - 1, False)
    state = loop(tiles // 2, tiles, state, True)
    emit(tiles - 1, True)


def column_scan(columns):
    length, width, _ = columns.shape
    vmem = pl.BlockSpec(memory_space=pltpu.VMEM)
    scratch = [pltpu.VMEM(columns.shape, jnp.float32)]
    kernel = column_kernel
    per = LANES // (2 * width)
    if width % 16 == 0 and LANES % (2 * width) == 0 and length % (32 * per) == 0:
        kernel = column_tiles_kernel
        scratch = [
            pltpu.VMEM((16, LANES, LANES), jnp.float32),
            pltpu.VMEM((16 * LANES, LANES), jnp.bfloat16),
            pltpu.VMEM((length // per, per, LANES, LANES), jnp.float32),
            pltpu.VMEM((16, 8, LANES), jnp.float32),
            pltpu.VMEM((LANES, LANES), jnp.float32),
        ] + scratch
    return pl.pallas_call(
        kernel,
        out_shape=jax.ShapeDtypeStruct(columns.shape, jnp.bfloat16),
        in_specs=[vmem],
        out_specs=vmem,
        scratch_shapes=scratch,
        compiler_params=pltpu.CompilerParams(vmem_limit_bytes=20 << 20),
        cost_estimate=pl.CostEstimate(flops=200_000_000, bytes_accessed=2_000_000, transcendentals=0),
    )(columns)


def add_kernel(across_ref, down_ref, out_ref):
    rows, cols, _ = across_ref.shape
    for row in range(rows):
        out_ref[row] = across_ref[row] + down_ref[:, row].reshape(cols, DISP).astype(jnp.float32)


def add_vertical(horizontal, vertical):
    rows, cols, _ = horizontal.shape
    if not packs(vertical.shape[2]):
        return horizontal + jnp.swapaxes(vertical, 0, 1).reshape(rows, cols, DISP).astype(jnp.float32)
    vmem = pl.BlockSpec(memory_space=pltpu.VMEM)
    return pl.pallas_call(
        add_kernel,
        out_shape=jax.ShapeDtypeStruct(horizontal.shape, jnp.float32),
        in_specs=[vmem, vmem],
        out_specs=vmem,
        compiler_params=pltpu.CompilerParams(vmem_limit_bytes=8 << 20),
        cost_estimate=pl.CostEstimate(flops=300_000, bytes_accessed=2_600_000, transcendentals=0),
    )(horizontal, vertical)


def normalize(image_pixels):
    return (image_pixels.astype(jnp.float32) / 1024.0 - 2.0).astype(jnp.bfloat16)


def weights_kernel(rows, base_ref, first_ref, wt_ref, w1_ref):
    wt_ref[...] = jnp.zeros_like(wt_ref)
    layers, taps = base_ref.shape[0], base_ref.shape[1]
    for layer in range(layers):
        for dy in range(taps):
            for dx in range(taps):
                block = base_ref[layer, dy, dx].astype(jnp.float32).T.astype(jnp.bfloat16)
                for out in range(wt_ref.shape[3] // CH):
                    top = (out + dy) * CH
                    wt_ref[layer, dx, top : top + CH, out * CH : (out + 1) * CH] = block
    shape = w1_ref.shape
    row = lax.broadcasted_iota(jnp.int32, shape, 0)
    tall = rows + 8
    column = over(lax.broadcasted_iota(jnp.int32, shape, 1), CH)
    value = jnp.zeros(shape, jnp.float32)
    for dy in range(taps):
        for dx in range(taps):
            line = first_ref[dy * taps + dx : dy * taps + dx + 1, :]
            value = jnp.where((row - dx * tall - column == dy) & (row >= dx * tall) & (row < (dx + 1) * tall), line, value)
    w1_ref[...] = value.astype(jnp.bfloat16)


def banded_weights(first_weight, conv_weights, rows):
    base = jnp.transpose(conv_weights, (0, 3, 4, 1, 2))
    lines = jnp.transpose(first_weight, (1, 2, 3, 0)).reshape(9, CH).astype(jnp.float32)
    lines = jnp.tile(lines, (1, rows + 6))
    vmem = pl.BlockSpec(memory_space=pltpu.VMEM)
    return pl.pallas_call(
        functools.partial(weights_kernel, rows),
        out_shape=(
            jax.ShapeDtypeStruct((base.shape[0], 3, 6 * CH, 4 * CH), jnp.bfloat16),
            jax.ShapeDtypeStruct((LANES, (rows + 6) * CH), jnp.bfloat16),
        ),
        in_specs=[vmem, vmem],
        out_specs=(vmem, vmem),
        compiler_params=pltpu.CompilerParams(vmem_limit_bytes=12 << 20),
        cost_estimate=pl.CostEstimate(flops=10_000_000, bytes_accessed=2_500_000, transcendentals=0),
    )(base, lines)


def neighbours(pair, weights, row_axis, strip_axis):
    groups, strips = lax.axis_size(row_axis), lax.axis_size(strip_axis)
    above = lax.ppermute(pair, row_axis, [(i, i + 1) for i in range(groups - 1)])
    below = lax.ppermute(pair, row_axis, [(i + 1, i) for i in range(groups - 1)])
    above, below, weights = lax.optimization_barrier((above, below, weights))
    own = jnp.concatenate([above, pair, below], axis=1)
    other = lax.ppermute(own, strip_axis, [(i, i ^ 1) for i in range(strips)])
    first = lax.axis_index(strip_axis) == 0
    return jnp.concatenate([jnp.where(first, own, other), jnp.where(first, other, own)], axis=2), weights


def stacked(image, start, length, flipped):
    part = lax.dynamic_slice_in_dim(image, start - 1, length + 2, 1)
    if flipped:
        part = lax.optimization_barrier(part[:, ::-1])
    shifts = [part[:, dx : dx + length] for dx in ((2, 1, 0) if flipped else (0, 1, 2))]
    joined = jnp.concatenate(shifts, axis=0)
    joined = jnp.pad(joined, ((0, LANES - joined.shape[0]), (0, 0)))
    return joined.T


def per_device(left_pixels, right_pixels, valid_mask, first_weight, conv_weights):
    rows, cols = left_pixels.shape
    groups, strips = lax.axis_size("rows"), lax.axis_size("strips")
    group, strip = lax.axis_index("rows"), lax.axis_index("strips")
    total_rows, total_cols = rows * groups, cols * strips

    wt, w1 = banded_weights(first_weight, conv_weights, rows)
    pair = jnp.stack([normalize(left_pixels), normalize(right_pixels)])
    band, (wt, w1) = neighbours(pair, (wt, w1), "rows", "strips")
    band = band[:, rows - 4 : 2 * rows + 4]
    left_length, right_length = plan(cols)[0], plan(cols + DISP)[0]
    margin = right_length + 8
    band = jnp.pad(band, ((0, 0), (0, 0), (margin, margin)))
    first_col = strip * cols
    left_stack = stacked(band[0], margin + first_col - 3 * EDGE, left_length, False)
    right_start = first_col + cols - 1 + 3 * EDGE - (right_length - 1)
    right_stack = stacked(band[1], margin + right_start, right_length, True)
    scale = -1.0 / math.sqrt(CH)
    mask = jnp.repeat((valid_mask.astype(jnp.float32) * scale).astype(jnp.bfloat16).T, CH, axis=1)
    place = jnp.stack([group * rows, first_col, strip]).astype(jnp.int32)

    per_group = cols // groups
    cost, *packed = cost_volume(
        left_stack, right_stack, mask, w1, wt, place, rows, cols, total_rows, total_cols, per_group
    )
    if packed:
        grouped = packed[0].reshape(groups, rows, per_group, DISP)
    else:
        centred = (cost - offsets(cost.reshape(-1, DISP)).reshape(cost.shape)).astype(jnp.bfloat16)
        grouped = jnp.swapaxes(centred.reshape(rows, groups, per_group, DISP), 0, 1)
    columns = lax.all_to_all(grouped, "rows", split_axis=0, concat_axis=0, tiled=True)
    columns = columns.reshape(total_rows, per_group, DISP)

    leading, end = row_scan(place, cost, None, None, False)
    received = lax.ppermute(end, "strips", [(i, i ^ 1) for i in range(strips)])
    columns, _ = lax.optimization_barrier((columns, end))
    column_sum, received = lax.optimization_barrier((column_scan(columns), received))
    vertical = lax.all_to_all(
        column_sum.reshape(groups, rows, per_group, DISP), "rows", split_axis=0, concat_axis=0, tiled=True
    )
    horizontal, _ = row_scan(place, cost, received, leading, True)
    return add_vertical(horizontal, vertical)


def solution(mesh):
    in_specs = (P("rows", "strips"), P("rows", "strips"), P("rows", "strips"), P(), P())
    out_specs = P("rows", "strips", None)
    return jax.shard_map(
        per_device, mesh=mesh, in_specs=in_specs, out_specs=out_specs, check_vma=False
    )
```

```python
import functools
import math

import jax
import jax.numpy as jnp
from jax import lax
from jax.experimental import pallas as pl
from jax.experimental.pallas import tpu as pltpu
from jax.sharding import PartitionSpec as P

DISP = 128
P_SMALL = 0.5
P_LARGE = 2.0
BIG = 3.0e38
CH = 64
EDGE = 8
LANES = 128
BATCH = 2
PARTS = 1
SCAN_ROOM = 62_600_000
SUM_ROOM = 24 << 20


def over(x, n):
    return lax.shift_right_logical(x, n.bit_length() - 1) if n & (n - 1) == 0 else x // n


def within(x, n):
    return x & (n - 1) if n & (n - 1) == 0 else x % n


def plan(width):
    unit = 16 * PARTS
    totals = [-(-width // unit) * unit]
    for _ in range(3):
        totals.append(-(-(totals[-1] + 2 * EDGE) // unit) * unit)
    return totals[::-1]


def feature_stacks(stacks, w1_ref, wt_ref, row_low, row_high):
    def inside(test, base, count, lanes, halo, lane0):
        position = lax.broadcasted_iota(jnp.int32, (count, lanes), 0) + base
        row = over(lax.broadcasted_iota(jnp.int32, (count, lanes), 1) + lane0, CH) - halo
        return test(position) & (row >= row_low) & (row < row_high)

    def first(index, carry):
        for pix_ref, bufs, test, flipped in stacks:
            chunk = bufs[0].shape[0] // PARTS
            start = index * chunk
            value = jnp.dot(pix_ref[pl.ds(start, chunk), :], w1_ref[...], preferred_element_type=jnp.float32)
            keep = inside(test, start - 3 * EDGE, chunk, bufs[0].shape[1], 3, 0)
            bufs[0][pl.ds(start, chunk), :] = jnp.where(keep, jnp.maximum(value, 0.0), 0.0).astype(jnp.bfloat16)
        return carry

    for index in range(PARTS):
        first(index, 0)

    for layer in range(1, 4):

        def convolve(index, carry, layer=layer):
            halo = 3 - layer
            for pix_ref, bufs, test, flipped in stacks:
                source, target = bufs[layer - 1], bufs[layer]
                out_rows = target.shape[1] // CH
                chunk = target.shape[0] // PARTS
                reach = chunk + 2 * EDGE
                start = index * chunk
                for group in range(0, out_rows, 4):
                    count = min(4, out_rows - group)
                    wide, deep = count * CH, (count + 2) * CH
                    block = source[pl.ds(start, reach), group * CH : group * CH + deep]
                    parts = [
                        jnp.dot(block, wt_ref[layer - 1, dx, :deep, :wide], preferred_element_type=jnp.float32)
                        for dx in range(3)
                    ]
                    before, after = (parts[2], parts[0]) if flipped else (parts[0], parts[2])
                    value = pltpu.roll(before, 1, 0) + parts[1] + pltpu.roll(after, reach - 1, 0)
                    value = value[EDGE : EDGE + chunk]
                    if layer < 3:
                        value = jnp.maximum(value, 0.0)
                    keep = inside(test, start - halo * EDGE, chunk, wide, halo, group * CH)
                    value = jnp.where(keep, value, 0.0).astype(jnp.bfloat16)
                    target[pl.ds(start, chunk), group * CH : group * CH + wide] = value
            return carry

        for index in range(PARTS):
            convolve(index, 0)


def offsets(costs):
    even = jnp.full((DISP, DISP), 1.0 / DISP, jnp.bfloat16)
    return jnp.dot(costs.astype(jnp.bfloat16), even, preferred_element_type=jnp.float32)


def packs(per_group):
    return per_group % 16 == 0 and LANES % per_group == 0


def cost_kernel(dims, where_ref, left_ref, right_ref, mask_ref, w1_ref, wt_ref, cost_ref, *rest):
    rows, cols, total_rows, total_cols, per_group = dims
    payload_ref, rest = (rest[0], rest[1:]) if packs(per_group) else (None, rest)
    bufs = rest
    first_row, first_col = where_ref[0], where_ref[1]
    row_low, row_high = -first_row, total_rows - first_row
    left_bufs, right_bufs = bufs[:4], bufs[4:]

    def left_col(position):
        col = position + first_col
        return (col >= 0) & (col < total_cols)

    def right_col(position):
        col = first_col + cols - 1 - position
        return (col >= 0) & (col < total_cols)

    feature_stacks(
        [(left_ref, left_bufs, left_col, False), (right_ref, right_bufs, right_col, True)],
        w1_ref, wt_ref, row_low, row_high,
    )
    left, right = left_bufs[3], right_bufs[3]
    for row in range(rows):
        pair = row // 2 * LANES
        lane = lax.broadcasted_iota(jnp.int32, (LANES, LANES), 1)
        own = over(lane, CH) == row % 2

        for index in range(cols // LANES):
            start = index * LANES
            window = cols - LANES - start
            scale = mask_ref[start : start + LANES, pair : pair + LANES]
            a = jnp.where(own, left[start : start + LANES, pair : pair + LANES] * scale, jnp.zeros((), jnp.bfloat16))
            b = right[window : window + 2 * LANES, pair : pair + LANES]
            product = lax.dot_general(a, b, (((1,), (1,)), ((), ())), preferred_element_type=jnp.float32)
            skewed = pltpu.roll(product, LANES + 1, 1, stride=1, stride_axis=0)[:, :LANES]
            cost_ref[row, start : start + LANES, :] = skewed
            if payload_ref is not None:
                skewed = skewed - offsets(skewed)
                for k in range(LANES // per_group):
                    piece = skewed[k * per_group : (k + 1) * per_group].astype(jnp.bfloat16)
                    group = index * (LANES // per_group) + k
                    payload_ref[group, row * per_group : (row + 1) * per_group, :] = piece


def cost_volume(left_stack, right_stack, mask, w1, wt, place, rows, cols, total_rows, total_cols, per_group):
    bufs = []
    for width in (cols, cols + DISP):
        sizes = plan(width)
        for layer in range(4):
            out_rows = rows + 2 * (3 - layer)
            length = sizes[layer]
            bufs.append(pltpu.VMEM((length, out_rows * CH), jnp.bfloat16))
    vmem = pl.BlockSpec(memory_space=pltpu.VMEM)
    shapes = [jax.ShapeDtypeStruct((rows, cols, DISP), jnp.float32)]
    if packs(per_group):
        shapes.append(jax.ShapeDtypeStruct((cols // per_group, rows * per_group, DISP), jnp.bfloat16))
    return pl.pallas_call(
        functools.partial(cost_kernel, (rows, cols, total_rows, total_cols, per_group)),
        out_shape=tuple(shapes),
        in_specs=[pl.BlockSpec(memory_space=pltpu.SMEM)] + [vmem] * 5,
        out_specs=(vmem,) * len(shapes),
        scratch_shapes=bufs,
        compiler_params=pltpu.CompilerParams(vmem_limit_bytes=40 << 20),
        cost_estimate=pl.CostEstimate(flops=8_000_000_000, bytes_accessed=6_000_000, transcendentals=0),
    )(place, left_stack, right_stack, mask, w1, wt)


def row_scan_kernel(dims, has_sum, place_ref, cost_hbm, *rest):
    rows, cols, flip, batch = dims
    if has_sum:
        state_ref, lead_hbm, out_ref, end_ref, lead_ref, lead_sem, *rest = rest
    else:
        out_hbm, end_ref, out_ref, out_sems, *rest = rest
    cost_ref, cost_sems, tile_ref, turn_ref, pick_ref, split_a, split_b, even_ref, odd_ref, path_ref, low_ref = rest
    width = LANES // rows
    count = cols // width
    forward = place_ref[2] == (1 if flip else 0)
    lane = lax.broadcasted_iota(jnp.int32, (8, LANES), 1)
    sublane = lax.broadcasted_iota(jnp.int32, (8, LANES), 0)
    lane_col = within(lane, width)

    def copy_in(index):
        part = pl.ds(chunk_start(index), width)
        return pltpu.make_async_copy(cost_hbm.at[:, part], cost_ref.at[:, part], cost_sems.at[index])

    rounds = count // batch // 2
    early = max(rounds // 2 * 2 * batch - 1, 0)

    def copy_out(part):
        length = (early, count - early)[part] * width
        begin = jnp.where(forward, (0, early * width)[part], ((count - early) * width, 0)[part])
        cut = pl.ds(pl.multiple_of(begin, width), length)
        return pltpu.make_async_copy(out_ref.at[:, cut], out_hbm.at[:, cut], out_sems.at[part])

    def chunk_of(index):
        return jnp.where(forward, index, count - 1 - index)

    def chunk_start(index):
        return pl.multiple_of(chunk_of(index) * width, width)

    for index in range(count):
        copy_in(index).start()
    if has_sum:
        copy_lead = pltpu.make_async_copy(lead_hbm, lead_ref, lead_sem)
        copy_lead.start()

    def build_pick(pair, carry):
        k = within(lax.broadcasted_iota(jnp.int32, (2 * LANES, 2 * LANES), 0), LANES)
        n = lax.broadcasted_iota(jnp.int32, (2 * LANES, 2 * LANES), 1)
        wanted = over(within(n, LANES), width) * width + 2 * pair + over(n, LANES)
        pick_ref[pair] = jnp.where(k == wanted, 1.0, 0.0).astype(jnp.bfloat16)
        return carry

    lax.fori_loop(0, width // 2, build_pick, 0, unroll=4)

    def split(index, target):
        start = chunk_start(jnp.minimum(index, count - 1))
        tile = jnp.concatenate([cost_ref[row, pl.ds(start, width), :] for row in range(rows)], axis=0)
        tile_ref[...] = tile.T
        for v in range(0, 16, 2):
            plane = jnp.concatenate(
                [tile_ref[pl.ds(v, 8, stride=16), :], tile_ref[pl.ds(v + 1, 8, stride=16), :]], axis=0
            )
            high = plane.astype(jnp.bfloat16)
            low = (plane - high.astype(jnp.float32)).astype(jnp.bfloat16)
            target[v * 8 : v * 8 + 16, :LANES] = high
            target[v * 8 : v * 8 + 16, LANES:] = low

    def spread(source, target, pair):
        both = jnp.dot(source[...], pick_ref[pair], preferred_element_type=jnp.float32)
        for slot in range(batch):
            target[slot, 2 * pair] = both[slot * LANES : slot * LANES + LANES, :LANES]
            target[slot, 2 * pair + 1] = both[slot * LANES : slot * LANES + LANES, LANES:]

    def emit(index):
        start = chunk_start(jnp.maximum(index, 0))
        low = low_ref[...]
        for v in range(16):
            turn_ref[pl.ds(v, 8, stride=16), :] = path_ref[v] - low
        done = turn_ref[...].T
        tile = jnp.concatenate([cost_ref[row, pl.ds(start, width), :] for row in range(rows)], axis=0)
        done = done + offsets(tile)
        for row in range(rows):
            piece = done[row * width : (row + 1) * width]
            if has_sum:
                piece = piece + lead_ref[row, pl.ds(start, width), :]
            out_ref[row, pl.ds(start, width), :] = piece

    def advance(state, low, slot, step, current):
        col = jnp.where(forward, step, width - 1 - step)
        mask = lane_col == col
        bound = low + P_LARGE
        above = jnp.where(sublane == 7, BIG, pltpu.roll(state[0], 7, 0))
        below = jnp.where(sublane == 0, BIG, pltpu.roll(state[15], 1, 0))
        padded = [below] + list(state) + [above]
        fresh = []
        for v in range(16):
            near = jnp.minimum(padded[v], padded[v + 2]) + P_SMALL
            best = jnp.minimum(jnp.minimum(state[v], near), bound)
            value = current[slot, col, v * 8 : v * 8 + 8, :] + best
            pltpu.store(path_ref.at[v], value, mask=mask)
            fresh.append(value)
        pltpu.store(low_ref, low, mask=mask)
        return fresh

    def one_batch(number, state, current, coming, ready, filling):
        base = number * batch
        pairs = width // 2 // batch

        def one_chunk(slot, state):
            emit(base + slot - 1)
            split(base + 2 * batch + slot, filling.at[pl.ds(pl.multiple_of(slot * LANES, LANES), LANES)])
            low = lowest(state)
            state = [value - low for value in state]
            low = jnp.zeros_like(low)
            for step in range(width):
                if step % (2 * batch) == 0:
                    spread(ready, coming, slot * pairs + step // (2 * batch))
                if step:
                    low = lowest(state)
                state = advance(state, low, slot, step, current)
            return tuple(state)

        return lax.fori_loop(0, batch, one_chunk, state)

    for index in range(2 * batch):
        copy_in(index).wait()
    for slot in range(batch):
        split(slot, split_a.at[pl.ds(slot * LANES, LANES)])
        split(batch + slot, split_b.at[pl.ds(slot * LANES, LANES)])

    def first(group, carry):
        for k in range(8):
            spread(split_a, even_ref, group * 8 + k)
        return carry

    lax.fori_loop(0, width // 16, first, 0)

    for index in range(2 * batch, count):
        copy_in(index).wait()
    if has_sum:
        copy_lead.wait()

    def two_batches(index, state):
        state = one_batch(2 * index, state, even_ref, odd_ref, split_b, split_a)
        state = one_batch(2 * index + 1, state, odd_ref, even_ref, split_a, split_b)
        if not has_sum and early:

            @pl.when(index == rounds // 2 - 1)
            def _():
                copy_out(0).start()

        return state

    if has_sum:
        state = tuple(state_ref[v] for v in range(16))
    else:
        state = (jnp.zeros((8, LANES), jnp.float32),) * 16
    state = lax.fori_loop(0, rounds, two_batches, state)
    emit(count - 1)
    if not has_sum:
        copy_out(1).start()
    for v in range(16):
        end_ref[v] = state[v]
    if not has_sum:
        for part in range(2 if early else 1):
            copy_out(1 - part).wait()


def row_scan(place, cost, state, lead, flip):
    rows, cols, _ = cost.shape
    width = LANES // rows
    count = cols // width
    batch = math.gcd(count // 2, BATCH)
    vmem = pl.BlockSpec(memory_space=pltpu.VMEM)
    hbm = pl.BlockSpec(memory_space=pltpu.HBM)
    has_sum = lead is not None
    args = [place, cost] + ([state, lead] if has_sum else [])
    whole = pltpu.VMEM(cost.shape, jnp.float32)
    moved = [whole, pltpu.SemaphoreType.DMA(() if has_sum else (2,))]
    return pl.pallas_call(
        functools.partial(row_scan_kernel, (rows, cols, flip, batch), has_sum),
        out_shape=(
            jax.ShapeDtypeStruct(cost.shape, jnp.float32),
            jax.ShapeDtypeStruct((16, 8, LANES), jnp.float32),
        ),
        in_specs=[pl.BlockSpec(memory_space=pltpu.SMEM), hbm] + ([vmem, hbm] if has_sum else []),
        out_specs=(vmem if has_sum else hbm, vmem),
        scratch_shapes=moved
        + [
            whole,
            pltpu.SemaphoreType.DMA((count,)),
            pltpu.VMEM((LANES, LANES), jnp.float32),
            pltpu.VMEM((LANES, LANES), jnp.float32),
            pltpu.VMEM((width // 2, 2 * LANES, 2 * LANES), jnp.bfloat16),
            pltpu.VMEM((batch * LANES, 2 * LANES), jnp.bfloat16),
            pltpu.VMEM((batch * LANES, 2 * LANES), jnp.bfloat16),
            pltpu.VMEM((batch, width, LANES, LANES), jnp.float32),
            pltpu.VMEM((batch, width, LANES, LANES), jnp.float32),
            pltpu.VMEM((16, 8, LANES), jnp.float32),
            pltpu.VMEM((8, LANES), jnp.float32),
        ],
        compiler_params=pltpu.CompilerParams(vmem_limit_bytes=SUM_ROOM if has_sum else SCAN_ROOM),
        cost_estimate=pl.CostEstimate(flops=2_000_000_000, bytes_accessed=30_000_000, transcendentals=0),
    )(*args)


def column_kernel(cost_ref, out_ref, sum_ref):
    length, width, _ = cost_ref.shape
    lane = lax.broadcasted_iota(jnp.int32, (width, DISP), 1)

    def step(state, index):
        cost = cost_ref[index].astype(jnp.float32)
        low = jnp.min(state, axis=1, keepdims=True)
        above = jnp.where(lane == DISP - 1, BIG, pltpu.roll(state, DISP - 1, 1))
        below = jnp.where(lane == 0, BIG, pltpu.roll(state, 1, 1))
        near = jnp.minimum(above, below) + P_SMALL
        return cost + jnp.minimum(jnp.minimum(state, near), low + P_LARGE) - low

    def first(index, states):
        down = step(states[0], index)
        up = step(states[1], length - 1 - index)
        sum_ref[index] = down
        sum_ref[length - 1 - index] = up
        return down, up

    def second(index, states):
        down = step(states[0], index)
        up = step(states[1], length - 1 - index)
        out_ref[index] = (sum_ref[index] + down).astype(jnp.bfloat16)
        out_ref[length - 1 - index] = (sum_ref[length - 1 - index] + up).astype(jnp.bfloat16)
        return down, up

    zero = jnp.zeros((width, DISP), jnp.float32)
    states = lax.fori_loop(0, length // 2, first, (zero, zero))
    lax.fori_loop(length // 2, length, second, states)


def lowest(state):
    level = list(state)
    while len(level) > 1:
        level = [jnp.minimum(level[i], level[i + 1]) for i in range(0, len(level), 2)]
    low = level[0]
    for shift in (4, 2, 1):
        low = jnp.minimum(low, pltpu.roll(low, shift, 0))
    return low


def column_tiles_kernel(cost_ref, out_ref, tile_ref, split_ref, spread_ref, path_ref, turn_ref, sum_ref):
    length, width, _ = cost_ref.shape
    both = 2 * width
    per = LANES // both
    tiles = length // per
    sublane = lax.broadcasted_iota(jnp.int32, (8, LANES), 0)
    lane_step = over(lax.broadcasted_iota(jnp.int32, (8, LANES), 1), both)
    k = lax.broadcasted_iota(jnp.int32, (LANES, per * LANES), 0)
    n = lax.broadcasted_iota(jnp.int32, (LANES, per * LANES), 1)
    pick = jnp.where(k == over(n, LANES) * both + within(n, both), 1.0, 0.0).astype(jnp.bfloat16)

    def places(tile):
        rows = []
        for step in range(per):
            rows += [tile * per + step, length - 1 - (tile * per + step)]
        return rows

    def prepare(index, carry):
        for slot in range(16):
            tile = index * 16 + slot
            block = jnp.concatenate([cost_ref[row] for row in places(tile)], axis=0)
            tile_ref[slot] = block.astype(jnp.float32).T
            for v in range(0, 16, 2):
                plane = jnp.concatenate(
                    [tile_ref[slot, pl.ds(v, 8, stride=16), :], tile_ref[slot, pl.ds(v + 1, 8, stride=16), :]], axis=0
                )
                split_ref[slot * LANES + v * 8 : slot * LANES + v * 8 + 16, :] = plane.astype(jnp.bfloat16)
        spread = jnp.dot(split_ref[...], pick, preferred_element_type=jnp.float32)
        for slot in range(16):
            for step in range(per):
                spread_ref[index * 16 + slot, step] = spread[
                    slot * LANES : slot * LANES + LANES, step * LANES : step * LANES + LANES
                ]
        return carry

    lax.fori_loop(0, tiles // 16, prepare, 0)

    def emit(tile, last):
        tile = jnp.maximum(tile, 0)
        for v in range(16):
            turn_ref[pl.ds(v, 8, stride=16), :] = path_ref[v]
        done = turn_ref[...].T
        for i, row in enumerate(places(tile)):
            piece = done[i * width : (i + 1) * width]
            if last:
                out_ref[row] = (sum_ref[row] + piece).astype(jnp.bfloat16)
            else:
                sum_ref[row] = piece

    def run(tile, state, last):
        emit(tile - 1, last)
        state = list(state)
        for step in range(per):
            low = lowest(state)
            bound = low + P_LARGE
            above = jnp.where(sublane == 7, BIG, pltpu.roll(state[0], 7, 0))
            below = jnp.where(sublane == 0, BIG, pltpu.roll(state[15], 1, 0))
            padded = [below] + state + [above]
            fresh = []
            for v in range(16):
                near = jnp.minimum(padded[v], padded[v + 2]) + P_SMALL
                best = jnp.minimum(jnp.minimum(state[v], near), bound)
                value = spread_ref[tile, step, v * 8 : v * 8 + 8, :] + (best - low)
                if step:
                    pltpu.store(path_ref.at[v], value, mask=lane_step == step)
                else:
                    path_ref[v] = value
                fresh.append(value)
            state = fresh
        return tuple(state)

    def loop(begin, end, state, last):
        return lax.fori_loop(begin, end, lambda tile, carry: run(tile, carry, last), state, unroll=16)

    state = (jnp.zeros((8, LANES), jnp.float32),) * 16
    state = loop(0, tiles // 2, state, False)
    emit(tiles // 2 - 1, False)
    state = loop(tiles // 2, tiles, state, True)
    emit(tiles - 1, True)


def column_scan(columns):
    length, width, _ = columns.shape
    vmem = pl.BlockSpec(memory_space=pltpu.VMEM)
    scratch = [pltpu.VMEM(columns.shape, jnp.float32)]
    kernel = column_kernel
    per = LANES // (2 * width)
    if width % 16 == 0 and LANES % (2 * width) == 0 and length % (32 * per) == 0:
        kernel = column_tiles_kernel
        scratch = [
            pltpu.VMEM((16, LANES, LANES), jnp.float32),
            pltpu.VMEM((16 * LANES, LANES), jnp.bfloat16),
            pltpu.VMEM((length // per, per, LANES, LANES), jnp.float32),
            pltpu.VMEM((16, 8, LANES), jnp.float32),
            pltpu.VMEM((LANES, LANES), jnp.float32),
        ] + scratch
    return pl.pallas_call(
        kernel,
        out_shape=jax.ShapeDtypeStruct(columns.shape, jnp.bfloat16),
        in_specs=[vmem],
        out_specs=vmem,
        scratch_shapes=scratch,
        compiler_params=pltpu.CompilerParams(vmem_limit_bytes=20 << 20),
        cost_estimate=pl.CostEstimate(flops=200_000_000, bytes_accessed=2_000_000, transcendentals=0),
    )(columns)


def add_kernel(across_ref, down_ref, out_ref):
    rows, cols, _ = across_ref.shape
    for row in range(rows):
        out_ref[row] = across_ref[row] + down_ref[:, row].reshape(cols, DISP).astype(jnp.float32)


def add_vertical(horizontal, vertical):
    rows, cols, _ = horizontal.shape
    if not packs(vertical.shape[2]):
        return horizontal + jnp.swapaxes(vertical, 0, 1).reshape(rows, cols, DISP).astype(jnp.float32)
    vmem = pl.BlockSpec(memory_space=pltpu.VMEM)
    return pl.pallas_call(
        add_kernel,
        out_shape=jax.ShapeDtypeStruct(horizontal.shape, jnp.float32),
        in_specs=[vmem, vmem],
        out_specs=vmem,
        compiler_params=pltpu.CompilerParams(vmem_limit_bytes=8 << 20),
        cost_estimate=pl.CostEstimate(flops=300_000, bytes_accessed=2_600_000, transcendentals=0),
    )(horizontal, vertical)


def normalize(image_pixels):
    return (image_pixels.astype(jnp.float32) / 1024.0 - 2.0).astype(jnp.bfloat16)


def weights_kernel(rows, base_ref, first_ref, wt_ref, w1_ref):
    wt_ref[...] = jnp.zeros_like(wt_ref)
    layers, taps = base_ref.shape[0], base_ref.shape[1]
    for layer in range(layers):
        for dy in range(taps):
            for dx in range(taps):
                block = base_ref[layer, dy, dx].astype(jnp.float32).T.astype(jnp.bfloat16)
                for out in range(wt_ref.shape[3] // CH):
                    top = (out + dy) * CH
                    wt_ref[layer, dx, top : top + CH, out * CH : (out + 1) * CH] = block
    shape = w1_ref.shape
    row = lax.broadcasted_iota(jnp.int32, shape, 0)
    tall = rows + 8
    column = over(lax.broadcasted_iota(jnp.int32, shape, 1), CH)
    value = jnp.zeros(shape, jnp.float32)
    for dy in range(taps):
        for dx in range(taps):
            line = first_ref[dy * taps + dx : dy * taps + dx + 1, :]
            value = jnp.where((row - dx * tall - column == dy) & (row >= dx * tall) & (row < (dx + 1) * tall), line, value)
    w1_ref[...] = value.astype(jnp.bfloat16)


def banded_weights(first_weight, conv_weights, rows):
    base = jnp.transpose(conv_weights, (0, 3, 4, 1, 2))
    lines = jnp.transpose(first_weight, (1, 2, 3, 0)).reshape(9, CH).astype(jnp.float32)
    lines = jnp.tile(lines, (1, rows + 6))
    vmem = pl.BlockSpec(memory_space=pltpu.VMEM)
    return pl.pallas_call(
        functools.partial(weights_kernel, rows),
        out_shape=(
            jax.ShapeDtypeStruct((base.shape[0], 3, 6 * CH, 4 * CH), jnp.bfloat16),
            jax.ShapeDtypeStruct((LANES, (rows + 6) * CH), jnp.bfloat16),
        ),
        in_specs=[vmem, vmem],
        out_specs=(vmem, vmem),
        compiler_params=pltpu.CompilerParams(vmem_limit_bytes=12 << 20),
        cost_estimate=pl.CostEstimate(flops=10_000_000, bytes_accessed=2_500_000, transcendentals=0),
    )(base, lines)


def neighbours(pair, weights, row_axis, strip_axis):
    groups, strips = lax.axis_size(row_axis), lax.axis_size(strip_axis)
    above = lax.ppermute(pair, row_axis, [(i, i + 1) for i in range(groups - 1)])
    below = lax.ppermute(pair, row_axis, [(i + 1, i) for i in range(groups - 1)])
    above, below, weights = lax.optimization_barrier((above, below, weights))
    own = jnp.concatenate([above, pair, below], axis=1)
    other = lax.ppermute(own, strip_axis, [(i, i ^ 1) for i in range(strips)])
    first = lax.axis_index(strip_axis) == 0
    return jnp.concatenate([jnp.where(first, own, other), jnp.where(first, other, own)], axis=2), weights


def stacked(image, start, length, flipped):
    part = lax.dynamic_slice_in_dim(image, start - 1, length + 2, 1)
    if flipped:
        part = lax.optimization_barrier(part[:, ::-1])
    shifts = [part[:, dx : dx + length] for dx in ((2, 1, 0) if flipped else (0, 1, 2))]
    joined = jnp.concatenate(shifts, axis=0)
    joined = jnp.pad(joined, ((0, LANES - joined.shape[0]), (0, 0)))
    return joined.T


def per_device(left_pixels, right_pixels, valid_mask, first_weight, conv_weights):
    rows, cols = left_pixels.shape
    groups, strips = lax.axis_size("rows"), lax.axis_size("strips")
    group, strip = lax.axis_index("rows"), lax.axis_index("strips")
    total_rows, total_cols = rows * groups, cols * strips

    wt, w1 = banded_weights(first_weight, conv_weights, rows)
    pair = jnp.stack([normalize(left_pixels), normalize(right_pixels)])
    band, (wt, w1) = neighbours(pair, (wt, w1), "rows", "strips")
    band = band[:, rows - 4 : 2 * rows + 4]
    left_length, right_length = plan(cols)[0], plan(cols + DISP)[0]
    margin = right_length + 8
    band = jnp.pad(band, ((0, 0), (0, 0), (margin, margin)))
    first_col = strip * cols
    left_stack = stacked(band[0], margin + first_col - 3 * EDGE, left_length, False)
    right_start = first_col + cols - 1 + 3 * EDGE - (right_length - 1)
    right_stack = stacked(band[1], margin + right_start, right_length, True)
    scale = -1.0 / math.sqrt(CH)
    mask = jnp.repeat((valid_mask.astype(jnp.float32) * scale).astype(jnp.bfloat16).T, CH, axis=1)
    place = jnp.stack([group * rows, first_col, strip]).astype(jnp.int32)

    per_group = cols // groups
    cost, *packed = cost_volume(
        left_stack, right_stack, mask, w1, wt, place, rows, cols, total_rows, total_cols, per_group
    )
    if packed:
        grouped = packed[0].reshape(groups, rows, per_group, DISP)
    else:
        centred = (cost - offsets(cost.reshape(-1, DISP)).reshape(cost.shape)).astype(jnp.bfloat16)
        grouped = jnp.swapaxes(centred.reshape(rows, groups, per_group, DISP), 0, 1)
    columns = lax.all_to_all(grouped, "rows", split_axis=0, concat_axis=0, tiled=True)
    columns = columns.reshape(total_rows, per_group, DISP)

    leading, end = row_scan(place, cost, None, None, False)
    received = lax.ppermute(end, "strips", [(i, i ^ 1) for i in range(strips)])
    columns, _ = lax.optimization_barrier((columns, end))
    column_sum, received = lax.optimization_barrier((column_scan(columns), received))
    vertical = lax.all_to_all(
        column_sum.reshape(groups, rows, per_group, DISP), "rows", split_axis=0, concat_axis=0, tiled=True
    )
    horizontal, _ = row_scan(place, cost, received, leading, True)
    return add_vertical(horizontal, vertical)


def solution(mesh):
    in_specs = (P("rows", "strips"), P("rows", "strips"), P("rows", "strips"), P(), P())
    out_specs = P("rows", "strips", None)
    return jax.shard_map(
        per_device, mesh=mesh, in_specs=in_specs, out_specs=out_specs, check_vma=False
    )
```
